32 devices in a mesh: dp: 16 (over z, y, core), tensor: 2 (over x).
Axes of the slice: x: 2, y: 2, z: 4, core: 2. Of those that a mesh axis runs over, the one named last changes fastest.
Arguments:
- inputs: bfloat16 [8192, 1024], P('dp'), may hold values from -6 to 6
- first_values: bfloat16 [8192, 1024], P('dp', 'tensor'), may hold values from -6 to 6
- w_query: bfloat16 [1024, 1024], P(None, 'tensor'), may hold values from -0.1875 to 0.1875
- w_key: bfloat16 [1024, 1024], P(None, 'tensor'), may hold values from -0.1875 to 0.1875
- w_value: bfloat16 [1024, 1024], P(None, 'tensor'), may hold values from -0.1875 to 0.1875
- w_out: bfloat16 [1024, 1024], P('tensor'), may hold values from -4 to 4
- w_gate: bfloat16 [1024, 2816], P(None, 'tensor'), may hold values from -0.1875 to 0.1875
- w_up: bfloat16 [1024, 2816], P(None, 'tensor'), may hold values from -0.1875 to 0.1875
- w_down: bfloat16 [2816, 1024], P('tensor'), may hold values from -0.109375 to 0.109375
- norm_attn: bfloat16 [1024], replicated, may hold values from 0.5 to 1.5
- norm_ffn: bfloat16 [1024], replicated, may hold values from 0.5 to 1.5
- cotangent: bfloat16 [8192, 1024], P('dp'), may hold values from -6 to 6
- parents: int32 [16], replicated, may hold values from -1 to 7, as said below
- depth_pos: int32 [16], replicated, may hold values from 0 to 2560, as said below
- assignment: int32 [16], replicated, may hold values from 0 to 15, as said below
Outputs:
- output: bfloat16 [8192, 1024], P('dp')
- grad_inputs: float32 [8192, 1024], P('dp')
- grad_first_values: float32 [8192, 1024], P('dp', 'tensor')
- grad_w_query: float32 [1024, 1024], P(None, 'tensor')
- grad_w_key: float32 [1024, 1024], P(None, 'tensor')
- grad_w_value: float32 [1024, 1024], P(None, 'tensor')
- grad_w_out: float32 [1024, 1024], P('tensor')
- grad_w_gate: float32 [1024, 2816], P(None, 'tensor')
- grad_w_up: float32 [1024, 2816], P(None, 'tensor')
- grad_w_down: float32 [2816, 1024], P('tensor')
- grad_norm_attn: float32 [1024], replicated
- grad_norm_ffn: float32 [1024], replicated
The draws below stay inside these ranges and needn't reach their ends.
Inputs may be any that keep to these rules, and one draw needn't show every extreme that they name: `parents`: the tree-ordered segments form 1 trees of 16: segment 16 k is a root, 16 k + j has parent 16 k + j - 1 for j = 1, 2, 3, segments 16 k + 4 to 16 k + 7 have parent 16 k + 3, and each of 16 k + 8 to 16 k + 15 has one of 16 k + 4 to 16 k + 7 as parent, each of those the parent of exactly two. A permutation: tree-ordered segment g lies in slot assignment[g], that is in rows assignment[g] * 512 to assignment[g] * 512 + 511. depth_pos[s] is 512 times the number of strict ancestors of the segment in slot s.
All inputs are finite; a program needn't handle non-finite values.
Results may differ from the reference program's by a relative error of at most 0.025.
Values may be sent and summed in bfloat16 or wider, within the bound.
No kernel may reach another device: no remote copies, remote signals or barrier semaphores. Data moves between devices by JAX's collectives and lax.ppermute only.
A program may use at most 256 MiB of HBM per device.

```python
import jax
import jax.numpy as jnp
import numpy as np
from jax import lax

D = 1024
HEAD_DIM = 64
FF = 2816
SEG = 512
NSEG = 16
TOKENS = 8192
N_TENSOR = 2


def tree_order(key):
    return jax.random.permutation(jax.random.fold_in(key, 23), NSEG).astype(jnp.int32)


def draw_parents(key, part):
    forest = NSEG // 16
    pair_keys = jax.random.split(jax.random.fold_in(key, 11), forest)
    pairing = jax.vmap(lambda single_key: jax.random.permutation(single_key, 8))(pair_keys).astype(jnp.int32)
    offset_rows = (jnp.arange(forest, dtype=jnp.int32) * 16)[:, None]
    upper_table = jnp.asarray(np.array([-1, 0, 1, 2, 3, 3, 3, 3], dtype=np.int32))[None, :]
    upper_parents = jnp.where(upper_table < 0, -1, upper_table + offset_rows)
    leaf_parents = 4 + pairing // 2 + offset_rows
    return jnp.concatenate([upper_parents, leaf_parents], axis=1).reshape(-1).astype(jnp.int32)


def draw_assignment(key, part):
    return tree_order(key)


def draw_depth_pos(key, part):
    order_slots = tree_order(key)
    segment_ids = jnp.argsort(order_slots).astype(jnp.int32)
    local_index = segment_ids % 16
    level_table = jnp.asarray(np.array([0, 1, 2, 3, 4, 4, 4, 4, 5, 5, 5, 5, 5, 5, 5, 5], dtype=np.int32))
    level_rows = jnp.sum(jnp.where(local_index[:, None] == jnp.arange(16, dtype=jnp.int32)[None, :], level_table[None, :], 0), axis=1)
    return (level_rows * SEG).astype(jnp.int32)


def block_levels(rng, dims, pieces, least, largest):
    factor_of = 1.0
    for axis_at, parts in pieces:
        heights = jax.random.uniform(jax.random.fold_in(jax.random.fold_in(rng, 6), axis_at), (parts,), jnp.float32, least / len(pieces), largest / len(pieces))
        factor_of = factor_of * jnp.repeat(jnp.exp(heights), dims[axis_at] // parts).reshape((-1,) + (1,) * (len(dims) - 1 - axis_at))
    return factor_of


def centred(rng, extent, deviation, reach, shards=(), held_as=jnp.bfloat16):
    result = deviation * jax.random.normal(rng, extent, jnp.float32)
    if shards:
        result = result * block_levels(rng, extent, shards, -0.22, 0.18)
    return jnp.clip(result, -reach, reach).astype(held_as)


def setup_inputs(seed: int = 0) -> dict:
    key_of = jax.random.split(jax.random.key(seed), 16)
    inputs = centred(key_of[0], (TOKENS, D), 1.0, 6.0, ((0, 16),))
    first_values = centred(key_of[1], (TOKENS, D), 1.0, 6.0, ((0, 16), (1, 2)))
    w_query = centred(key_of[2], (D, D), D ** -0.5, 0.1875, ((1, 2),))
    w_key = centred(key_of[3], (D, D), D ** -0.5, 0.1875, ((1, 2),))
    w_value = centred(key_of[4], (D, D), D ** -0.5, 0.1875, ((1, 2),))
    w_out = centred(key_of[5], (D, D), (D // (2 * SEG) + 1) ** -0.5, 4.0, ((0, 2),))
    w_gate = centred(key_of[6], (D, FF), D ** -0.5, 0.1875, ((1, 2),))
    w_up = centred(key_of[7], (D, FF), D ** -0.5, 0.1875, ((1, 2),))
    w_down = centred(key_of[8], (FF, D), FF ** -0.5, 0.109375, ((0, 2),))
    norm_attn = jnp.clip(1.0 + 0.1 * jax.random.normal(key_of[9], (D,), jnp.float32), 0.5, 1.5).astype(jnp.bfloat16)
    norm_ffn = jnp.clip(1.0 + 0.1 * jax.random.normal(key_of[10], (D,), jnp.float32), 0.5, 1.5).astype(jnp.bfloat16)
    cotangent = centred(key_of[11], (TOKENS, D), 1.0, 6.0, ((0, 16),))
    parents = draw_parents(jax.random.fold_in(key_of[15], 71), 0)
    depth_pos = draw_depth_pos(jax.random.fold_in(key_of[15], 71), 0)
    assignment = draw_assignment(jax.random.fold_in(key_of[15], 71), 0)
    return dict(inputs=inputs, first_values=first_values, w_query=w_query, w_key=w_key, w_value=w_value, w_out=w_out, w_gate=w_gate, w_up=w_up, w_down=w_down, norm_attn=norm_attn, norm_ffn=norm_ffn, cotangent=cotangent, parents=parents, depth_pos=depth_pos, assignment=assignment)


epsilon = 1e-06
rope_base = 10000.0
climb_steps = 5
masked_score = -1e+30
highest = lax.Precision.HIGHEST

@jax.custom_vjp
def low(v):
    return lax.optimization_barrier(v.astype(jnp.bfloat16)).astype(jnp.float32)

@jax.custom_vjp
def low_back(v):
    return v

def low_keep(v):
    return (low(v), None)

def low_pass(kept, grad):
    return (grad,)

def back_keep(v):
    return (v, None)

def back_low(kept, grad):
    return (low(grad),)
low.defvjp(low_keep, low_pass)
low_back.defvjp(back_keep, back_low)

def matmul(left, right):
    return jnp.dot(left, right, precision=highest, preferred_element_type=jnp.float32)

def parent_slots(parents, assignment):
    count = parents.shape[0]
    slot_ids = jnp.arange(count, dtype=jnp.int32)
    at_slot = assignment[None, :] == slot_ids[:, None]
    parent_seg = lax.optimization_barrier(jnp.sum(jnp.where(at_slot, parents[None, :], 0), axis=1)).astype(jnp.int32)
    parent_match = slot_ids[None, :] == parent_seg[:, None]
    above_slot = lax.optimization_barrier(jnp.sum(jnp.where(parent_match, assignment[None, :], 0), axis=1)).astype(jnp.int32)
    return jnp.where(parent_seg >= 0, above_slot, -1).astype(jnp.int32)

def climb(parent_slot, start_slots):
    slot_ids = jnp.arange(parent_slot.shape[0], dtype=jnp.int32)
    levels = [start_slots]
    current = start_slots
    for step_index in range(climb_steps):
        matched = current[:, None] == slot_ids[None, :]
        upward = lax.optimization_barrier(jnp.sum(jnp.where(matched, parent_slot[None, :], 0), axis=1)).astype(jnp.int32)
        current = jnp.where(current >= 0, upward, -1).astype(jnp.int32)
        levels.append(current)
    return jnp.stack(levels, axis=1)

def rms_norm(values, gain_vector):
    return values * lax.rsqrt(lax.optimization_barrier(jnp.mean(values * values, axis=-1, keepdims=True)) + epsilon) * gain_vector

def rotate(values, positions):
    head_dim = values.shape[-1]
    half_dim = head_dim // 2
    frequency = rope_base ** (-jnp.arange(half_dim, dtype=jnp.float32) * 2.0 / head_dim)
    angles = positions.astype(jnp.float32)[:, None] * frequency[None, :]
    cosine = jnp.cos(angles)[:, None, :]
    sine_table = jnp.sin(angles)[:, None, :]
    first_half = values[..., :half_dim]
    second_half = values[..., half_dim:]
    return jnp.concatenate([first_half * cosine - second_half * sine_table, second_half * cosine + first_half * sine_table], axis=-1)

def attend(queries, keys, values, paths):
    head_count = queries.shape[1]
    score_scale = queries.shape[-1] ** (-0.5)
    offsets = jnp.arange(SEG, dtype=jnp.int32)

    def one_segment(operand):
        query_block, path_row = operand
        key_parts = []
        value_parts = []
        valid_parts = []
        for level_index in range(climb_steps + 1):
            slot_index = path_row[level_index]
            row_begin = (jnp.maximum(slot_index, 0) * SEG).astype(jnp.int32)
            key_parts.append(lax.dynamic_slice_in_dim(keys, row_begin, SEG, 0))
            value_parts.append(lax.dynamic_slice_in_dim(values, row_begin, SEG, 0))
            if level_index == 0:
                valid_parts.append(offsets[None, :] <= offsets[:, None])
            else:
                valid_parts.append(jnp.broadcast_to(slot_index >= 0, (SEG, SEG)))
        near_keys = jnp.concatenate(key_parts, axis=0)
        near_values = jnp.concatenate(value_parts, axis=0)
        permit = jnp.concatenate(valid_parts, axis=1)
        scores = low_back(jnp.einsum('qhd,khd->hqk', query_block, near_keys, precision=highest) * score_scale)
        scores = jnp.where(permit[None], scores, masked_score)
        weights = low(jax.nn.softmax(scores, axis=-1))
        return jnp.einsum('hqk,khd->qhd', weights, near_values, precision=highest)
    shaped = queries.reshape(-1, SEG, head_count, queries.shape[-1])
    blocks = lax.map(jax.checkpoint(one_segment), (shaped, paths))
    return blocks.reshape(queries.shape)

def layer(inputs, first_values, w_query, w_key, w_value, w_out, w_gate, w_up, w_down, norm_attn, norm_ffn, positions, paths):
    tokens = inputs.shape[0]
    head_count = w_query.shape[1] // HEAD_DIM
    normed = low(rms_norm(inputs, norm_attn))
    query_proj = low_back(matmul(normed, w_query)).reshape(tokens, head_count, HEAD_DIM)
    key_proj = low_back(matmul(normed, w_key)).reshape(tokens, head_count, HEAD_DIM)
    value_proj = low_back(matmul(normed, w_value))
    queries = low(rotate(query_proj, positions))
    keys = low(rotate(key_proj, positions))
    mixed = low(0.5 * value_proj + 0.5 * first_values).reshape(tokens, head_count, HEAD_DIM)
    attended = attend(queries, keys, mixed, paths).reshape(tokens, D)
    attended = low(low_back(attended))
    group_cols = D // N_TENSOR
    branch_attn = jnp.zeros((tokens, D), jnp.float32)
    for group_index in range(N_TENSOR):
        lower_edge = group_index * group_cols
        branch_attn = branch_attn + low(matmul(attended[:, lower_edge:lower_edge + group_cols], w_out[lower_edge:lower_edge + group_cols]))
    hidden_state = inputs + low_back(branch_attn)
    normed_ffn = low(rms_norm(hidden_state, norm_ffn))
    gate_proj = low_back(matmul(normed_ffn, w_gate))
    up_proj = low_back(matmul(normed_ffn, w_up))
    activated = low(jax.nn.silu(gate_proj) * up_proj)
    group_units = FF // N_TENSOR
    feed = jnp.zeros((tokens, D), jnp.float32)
    for group_index in range(N_TENSOR):
        lower_edge = group_index * group_units
        feed = feed + low(matmul(activated[:, lower_edge:lower_edge + group_units], w_down[lower_edge:lower_edge + group_units]))
    return hidden_state + low_back(feed)

def reference(inputs, first_values, w_query, w_key, w_value, w_out, w_gate, w_up, w_down, norm_attn, norm_ffn, cotangent, parents, depth_pos, assignment):
    count = parents.shape[0]
    parent_slot = parent_slots(parents, assignment)
    paths = climb(parent_slot, jnp.arange(count, dtype=jnp.int32))
    positions = (jnp.repeat(depth_pos, SEG) + jnp.tile(jnp.arange(SEG, dtype=jnp.int32), count)).astype(jnp.int32)

    def forward(inputs_f, first_f, query_f, key_f, value_f, out_f, gate_f, up_f, down_f, attn_gain, ffn_gain):
        return layer(inputs_f, first_f, query_f, key_f, value_f, out_f, gate_f, up_f, down_f, attn_gain, ffn_gain, positions, paths)
    output, pullback = jax.vjp(forward, inputs.astype(jnp.float32), first_values.astype(jnp.float32), w_query.astype(jnp.float32), w_key.astype(jnp.float32), w_value.astype(jnp.float32), w_out.astype(jnp.float32), w_gate.astype(jnp.float32), w_up.astype(jnp.float32), w_down.astype(jnp.float32), norm_attn.astype(jnp.float32), norm_ffn.astype(jnp.float32))
    grads = pullback(cotangent.astype(jnp.float32))
    return (output.astype(jnp.bfloat16), grads[0], grads[1], grads[2], grads[3], grads[4], grads[5], grads[6], grads[7], grads[8], grads[9], grads[10])
```

```python
import jax
import jax.numpy as jnp
from jax import lax
from jax.experimental import pallas as pl
from jax.experimental.pallas import tpu as pltpu
from jax.sharding import PartitionSpec as P

HEAD_DIM = 64
SEG = 512


epsilon = 1e-06
rope_base = 10000.0
climb_steps = 5
masked_score = -1e30


def rms_scale(values):
    return lax.rsqrt(jnp.mean(values * values, axis=-1, keepdims=True) + epsilon)


def rotary_tables(positions, head_dim):
    half_dim = head_dim // 2
    frequency = rope_base ** (-jnp.arange(half_dim, dtype=jnp.float32) * 2.0 / head_dim)
    angles = positions.astype(jnp.float32)[:, None] * frequency[None, :]
    return (jnp.cos(angles)[:, None, :], jnp.sin(angles)[:, None, :])


def rotate(values, cosine, sine_table):
    half_dim = values.shape[-1] // 2
    first_half = values[..., :half_dim]
    second_half = values[..., half_dim:]
    return jnp.concatenate(
        [
            first_half * cosine - second_half * sine_table,
            second_half * cosine + first_half * sine_table,
        ],
        axis=-1,
    )


def rotate_back(gradient, cosine, sine_table):
    half_dim = gradient.shape[-1] // 2
    first_half = gradient[..., :half_dim]
    second_half = gradient[..., half_dim:]
    return jnp.concatenate(
        [
            first_half * cosine + second_half * sine_table,
            second_half * cosine - first_half * sine_table,
        ],
        axis=-1,
    )


def parent_slots(parents, assignment):
    count = parents.shape[0]
    slot_ids = jnp.arange(count, dtype=jnp.int32)
    at_slot = assignment[None, :] == slot_ids[:, None]
    parent_seg = jnp.sum(jnp.where(at_slot, parents[None, :], 0), axis=1)
    parent_match = slot_ids[None, :] == parent_seg[:, None]
    above_slot = jnp.sum(jnp.where(parent_match, assignment[None, :], 0), axis=1)
    return jnp.where(parent_seg >= 0, above_slot, -1)


def climb(parent_slot, start_slots):
    slot_ids = jnp.arange(parent_slot.shape[0], dtype=jnp.int32)
    levels = [start_slots]
    current = start_slots
    for step_index in range(climb_steps):
        matched = current[:, None] == slot_ids[None, :]
        upward = jnp.sum(jnp.where(matched, parent_slot[None, :], 0), axis=1)
        current = jnp.where(current >= 0, upward, -1)
        levels.append(current)
    return jnp.stack(levels, axis=1)


def norm_back(grad_normed, values, row_scale, gain_vector):
    scaled_grad = grad_normed * gain_vector
    grad_gain = jnp.sum(grad_normed * values * row_scale, axis=0)
    grad_values = row_scale * (
        scaled_grad
        - values * row_scale * row_scale * jnp.mean(scaled_grad * values, axis=-1, keepdims=True)
    )
    return (grad_values, grad_gain)


def path_rows(source, path_row):
    parts = []
    for level_index in range(climb_steps + 1):
        row_begin = (jnp.maximum(path_row[level_index], 0) * SEG).astype(jnp.int32)
        parts.append(lax.dynamic_slice_in_dim(source, row_begin, SEG, 0))
    return jnp.concatenate(parts, axis=0)


def path_permit(path_row, causal):
    parts = [causal]
    for level_index in range(1, climb_steps + 1):
        parts.append(jnp.broadcast_to(path_row[level_index] >= 0, (SEG, SEG)))
    return jnp.concatenate(parts, axis=1)


def body_general(
    inputs,
    first_values,
    w_query,
    w_key,
    w_value,
    w_out,
    w_gate,
    w_up,
    w_down,
    norm_attn,
    norm_ffn,
    cotangent,
    parents,
    depth_pos,
    assignment,
):
    row_count = inputs.shape[0]
    local_width = w_query.shape[1]
    head_count = local_width // HEAD_DIM
    score_scale = HEAD_DIM ** (-0.5)
    seg_count = row_count // SEG
    slot_total = parents.shape[0]
    slot_ids = jnp.arange(slot_total, dtype=jnp.int32)
    local_rows = jnp.arange(row_count, dtype=jnp.int32)
    own_slots = lax.axis_index("dp") * seg_count + jnp.arange(seg_count, dtype=jnp.int32)
    own_slot_rows = jnp.repeat(own_slots, SEG)
    depth_rows = jnp.sum(
        jnp.where(own_slot_rows[:, None] == slot_ids[None, :], depth_pos[None, :], 0), axis=1
    )
    positions = depth_rows + local_rows % SEG
    parent_slot = parent_slots(parents, assignment)
    own_paths = climb(parent_slot, own_slots)
    offsets = jnp.arange(SEG, dtype=jnp.int32)
    causal = offsets[None, :] <= offsets[:, None]
    cosine, sine_table = rotary_tables(positions, HEAD_DIM)
    inputs_wide = inputs.astype(jnp.float32)
    attn_scale = rms_scale(inputs_wide)
    gain_attn = norm_attn.astype(jnp.float32)
    normed = (inputs_wide * attn_scale * gain_attn).astype(jnp.bfloat16)
    query_proj = jnp.dot(normed, w_query, preferred_element_type=jnp.float32)
    key_proj = jnp.dot(normed, w_key, preferred_element_type=jnp.float32)
    value_proj = jnp.dot(normed, w_value, preferred_element_type=jnp.float32)
    query_rot = rotate(
        query_proj.reshape(row_count, head_count, HEAD_DIM), cosine, sine_table
    ).astype(jnp.bfloat16)
    key_rot = (
        rotate(key_proj.reshape(row_count, head_count, HEAD_DIM), cosine, sine_table)
        .astype(jnp.bfloat16)
        .reshape(row_count, local_width)
    )
    mixed = (0.5 * value_proj + 0.5 * first_values.astype(jnp.float32)).astype(jnp.bfloat16)
    key_all, value_all = (
        lax.all_gather(key_rot, "dp", axis=0, tiled=True),
        lax.all_gather(mixed, "dp", axis=0, tiled=True),
    )
    query_segs = query_rot.reshape(seg_count, SEG, head_count, HEAD_DIM)

    def segment_forward(operand):
        query_block, path_row = operand
        near_keys = path_rows(key_all, path_row).reshape(-1, head_count, HEAD_DIM)
        near_values = path_rows(value_all, path_row).reshape(-1, head_count, HEAD_DIM)
        permit = path_permit(path_row, causal)
        scores = (
            jnp.einsum("qhd,khd->hqk", query_block, near_keys, preferred_element_type=jnp.float32)
            * score_scale
        )
        scores = jnp.where(permit[None], scores, masked_score)
        row_max = jnp.max(scores, axis=-1)
        weights = jnp.where(permit[None], jnp.exp(scores - row_max[..., None]), 0.0)
        row_total = jnp.sum(weights, axis=-1)
        attn_probs = weights / row_total[..., None]
        block_out = jnp.einsum(
            "hqk,khd->qhd",
            attn_probs.astype(jnp.bfloat16),
            near_values,
            preferred_element_type=jnp.float32,
        )
        return (block_out, row_max + jnp.log(row_total))

    attn_parts, log_parts = lax.map(segment_forward, (query_segs, own_paths))
    attn_exact = attn_parts.reshape(row_count, head_count, HEAD_DIM)
    attended = attn_exact.reshape(row_count, local_width).astype(jnp.bfloat16)
    branch_attn = lax.psum(
        jnp.dot(attended, w_out, preferred_element_type=jnp.float32).astype(jnp.bfloat16), "tensor"
    ).astype(jnp.float32)
    hidden_state = inputs_wide + branch_attn
    ffn_scale = rms_scale(hidden_state)
    gain_ffn = norm_ffn.astype(jnp.float32)
    normed_ffn = (hidden_state * ffn_scale * gain_ffn).astype(jnp.bfloat16)
    gate_proj = jnp.dot(normed_ffn, w_gate, preferred_element_type=jnp.float32)
    up_proj = jnp.dot(normed_ffn, w_up, preferred_element_type=jnp.float32)
    silu_gate = jax.nn.silu(gate_proj)
    activated = (silu_gate * up_proj).astype(jnp.bfloat16)
    feed = lax.psum(
        jnp.dot(activated, w_down, preferred_element_type=jnp.float32).astype(jnp.bfloat16),
        "tensor",
    ).astype(jnp.float32)
    output = (hidden_state + feed).astype(jnp.bfloat16)
    grad_w_down = jnp.einsum("tf,td->fd", activated, cotangent, preferred_element_type=jnp.float32)
    grad_activated = jnp.einsum("td,fd->tf", cotangent, w_down, preferred_element_type=jnp.float32)
    sigmoid_gate = jax.nn.sigmoid(gate_proj)
    grad_gate = (
        grad_activated * up_proj * sigmoid_gate * (1.0 + gate_proj * (1.0 - sigmoid_gate))
    ).astype(jnp.bfloat16)
    grad_up = (grad_activated * silu_gate).astype(jnp.bfloat16)
    grad_w_gate = jnp.einsum("td,tf->df", normed_ffn, grad_gate, preferred_element_type=jnp.float32)
    grad_w_up = jnp.einsum("td,tf->df", normed_ffn, grad_up, preferred_element_type=jnp.float32)
    ffn_partial = jnp.einsum(
        "tf,df->td", grad_gate, w_gate, preferred_element_type=jnp.float32
    ) + jnp.einsum("tf,df->td", grad_up, w_up, preferred_element_type=jnp.float32)
    grad_normed_ffn = lax.psum(ffn_partial.astype(jnp.bfloat16), "tensor").astype(jnp.float32)
    grad_hidden_norm, grad_gain_ffn = norm_back(grad_normed_ffn, hidden_state, ffn_scale, gain_ffn)
    grad_hidden = cotangent.astype(jnp.float32) + grad_hidden_norm
    grad_branch = grad_hidden.astype(jnp.bfloat16)
    grad_w_out = jnp.einsum("tc,td->cd", attended, grad_branch, preferred_element_type=jnp.float32)
    grad_attended = jnp.einsum(
        "td,cd->tc", grad_branch, w_out, preferred_element_type=jnp.float32
    ).astype(jnp.bfloat16)
    grad_heads = grad_attended.reshape(row_count, head_count, HEAD_DIM)
    delta_rows = jnp.sum(grad_heads.astype(jnp.float32) * attn_exact, axis=-1)
    delta_parts = jnp.transpose(delta_rows.reshape(seg_count, SEG, head_count), (0, 2, 1))
    grad_segs = grad_heads.reshape(seg_count, SEG, head_count, HEAD_DIM)
    key_back, value_back = (key_all, value_all)

    def segment_back(query_block, grad_block, path_row, log_block, delta_block):
        near_keys = path_rows(key_back, path_row).reshape(-1, head_count, HEAD_DIM)
        near_values = path_rows(value_back, path_row).reshape(-1, head_count, HEAD_DIM)
        permit = path_permit(path_row, causal)
        scores = (
            jnp.einsum("qhd,khd->hqk", query_block, near_keys, preferred_element_type=jnp.float32)
            * score_scale
        )
        scores = jnp.where(permit[None], scores, masked_score)
        attn_probs = jnp.where(permit[None], jnp.exp(scores - log_block[..., None]), 0.0)
        grad_probs = jnp.einsum(
            "qhd,khd->hqk", grad_block, near_values, preferred_element_type=jnp.float32
        )
        grad_scores = (attn_probs * (grad_probs - delta_block[..., None])).astype(jnp.bfloat16)
        grad_part = (
            jnp.einsum("hqk,khd->qhd", grad_scores, near_keys, preferred_element_type=jnp.float32)
            * score_scale
        )
        return (attn_probs, grad_scores, grad_part)

    zero_rows = jnp.zeros((key_back.shape[0], local_width), jnp.float32)

    def scatter_step(fold_state, operand):
        key_acc, value_acc = fold_state
        query_block, grad_block, path_row, log_block, delta_block = operand
        attn_probs, grad_scores, grad_part = segment_back(
            query_block, grad_block, path_row, log_block, delta_block
        )
        key_term = (
            jnp.einsum("hqk,qhd->khd", grad_scores, query_block, preferred_element_type=jnp.float32)
            * score_scale
        ).reshape(climb_steps + 1, SEG, local_width)
        value_term = jnp.einsum(
            "hqk,qhd->khd",
            attn_probs.astype(jnp.bfloat16),
            grad_block,
            preferred_element_type=jnp.float32,
        ).reshape(climb_steps + 1, SEG, local_width)
        for level_index in range(climb_steps + 1):
            row_begin = (jnp.maximum(path_row[level_index], 0) * SEG).astype(jnp.int32)
            key_acc = lax.dynamic_update_slice_in_dim(
                key_acc,
                lax.dynamic_slice_in_dim(key_acc, row_begin, SEG, 0) + key_term[level_index],
                row_begin,
                0,
            )
            value_acc = lax.dynamic_update_slice_in_dim(
                value_acc,
                lax.dynamic_slice_in_dim(value_acc, row_begin, SEG, 0) + value_term[level_index],
                row_begin,
                0,
            )
        return ((key_acc, value_acc), grad_part)

    (key_terms, value_terms), grad_parts = lax.scan(
        scatter_step,
        (zero_rows, zero_rows),
        (query_segs, grad_segs, own_paths, log_parts, delta_parts),
    )
    grad_query_rot = grad_parts.reshape(row_count, head_count, HEAD_DIM)
    key_sums, value_sums = (
        lax.psum_scatter(
            key_terms.astype(jnp.bfloat16), "dp", scatter_dimension=0, tiled=True
        ).astype(jnp.float32),
        lax.psum_scatter(
            value_terms.astype(jnp.bfloat16), "dp", scatter_dimension=0, tiled=True
        ).astype(jnp.float32),
    )
    grad_key_rot = key_sums.reshape(row_count, head_count, HEAD_DIM)
    grad_first_values = 0.5 * value_sums
    grad_value = (0.5 * value_sums).astype(jnp.bfloat16)
    grad_key = (
        rotate_back(grad_key_rot, cosine, sine_table)
        .reshape(row_count, local_width)
        .astype(jnp.bfloat16)
    )
    grad_query = (
        rotate_back(grad_query_rot, cosine, sine_table)
        .reshape(row_count, local_width)
        .astype(jnp.bfloat16)
    )
    grad_w_query = jnp.einsum("td,tc->dc", normed, grad_query, preferred_element_type=jnp.float32)
    grad_w_key = jnp.einsum("td,tc->dc", normed, grad_key, preferred_element_type=jnp.float32)
    grad_w_value = jnp.einsum("td,tc->dc", normed, grad_value, preferred_element_type=jnp.float32)
    attn_partial = (
        jnp.einsum("tc,dc->td", grad_query, w_query, preferred_element_type=jnp.float32)
        + jnp.einsum("tc,dc->td", grad_key, w_key, preferred_element_type=jnp.float32)
        + jnp.einsum("tc,dc->td", grad_value, w_value, preferred_element_type=jnp.float32)
    )
    grad_normed = lax.psum(attn_partial.astype(jnp.bfloat16), "tensor").astype(jnp.float32)
    grad_input_norm, grad_gain_attn = norm_back(grad_normed, inputs_wide, attn_scale, gain_attn)
    grad_inputs = grad_hidden + grad_input_norm
    summed = (
        lax.psum(grad_w_query.astype(jnp.bfloat16), "dp").astype(jnp.float32),
        lax.psum(grad_w_key.astype(jnp.bfloat16), "dp").astype(jnp.float32),
        lax.psum(grad_w_value.astype(jnp.bfloat16), "dp").astype(jnp.float32),
        lax.psum(grad_w_out.astype(jnp.bfloat16), "dp").astype(jnp.float32),
        lax.psum(grad_w_gate.astype(jnp.bfloat16), "dp").astype(jnp.float32),
        lax.psum(grad_w_up.astype(jnp.bfloat16), "dp").astype(jnp.float32),
        lax.psum(grad_w_down.astype(jnp.bfloat16), "dp").astype(jnp.float32),
        lax.psum(grad_gain_attn.astype(jnp.bfloat16), "dp").astype(jnp.float32),
        lax.psum(grad_gain_ffn.astype(jnp.bfloat16), "dp").astype(jnp.float32),
    )
    return (
        output,
        grad_inputs,
        grad_first_values,
        summed[0],
        summed[1],
        summed[2],
        summed[3],
        summed[4],
        summed[5],
        summed[6],
        summed[7],
        summed[8],
    )


TREE = 16
TREE_DEPTHS = (0, 1, 2, 3, 4, 4, 4, 4, 5, 5, 5, 5, 5, 5, 5, 5)
LANES = 128
wide = jnp.float32
narrow = jnp.bfloat16
vmem_bytes = 60 * 1024 * 1024


def lane_ids(shape):
    return lax.broadcasted_iota(jnp.int32, shape, len(shape) - 1)


def swap_pairs(left, right):
    low = lane_ids(left.shape) < HEAD_DIM
    first = jnp.where(low, left, pltpu.roll(right, HEAD_DIM, 1))
    second = jnp.where(low, pltpu.roll(left, HEAD_DIM, 1), right)
    return first, second


def spin(values, cosine, signed_sine):
    half = HEAD_DIM // 2
    ahead = pltpu.roll(values, LANES - half, 1)
    behind = pltpu.roll(values, half, 1)
    other = jnp.where(lane_ids(values.shape) % HEAD_DIM < half, ahead, behind)
    return values * cosine + other * signed_sine


def dot_wide(left, right):
    return jnp.dot(left, right, preferred_element_type=wide)


def dot_rows(left, right):
    return lax.dot_general(left, right, (((1,), (1,)), ((), ())), preferred_element_type=wide)


def whole_spec():
    return pl.BlockSpec(memory_space=pltpu.VMEM)


def scalar_spec():
    return pl.BlockSpec(memory_space=pltpu.SMEM)


def project_kernel(
    x_ref, gain_ref, first_ref, cos_ref, sin_ref, wq_ref, wk_ref, wv_ref, send_ref, normed_ref
):
    rows = x_ref.shape[0]
    pairs = first_ref.shape[1] // LANES
    x = x_ref[...].astype(wide)
    normed = (x * rms_scale(x) * gain_ref[...].astype(wide)).astype(narrow)
    normed_ref[...] = normed
    query = dot_wide(normed, wq_ref[...]) * (HEAD_DIM ** (-0.5))
    key = dot_wide(normed, wk_ref[...])
    value = dot_wide(normed, wv_ref[...])
    mixed = 0.5 * value + 0.5 * first_ref[...].astype(wide)
    cosine = cos_ref[...]
    sine = sin_ref[...]
    for pair in range(pairs):
        cols = slice(pair * LANES, (pair + 1) * LANES)
        q = spin(query[:, cols], cosine, sine)
        k = spin(key[:, cols], cosine, sine)
        for at, tile in enumerate(swap_pairs(k, mixed[:, cols])):
            send_ref[2 * pair + at, 0, :rows, :] = tile.astype(narrow)
        for at, tile in enumerate(swap_pairs(q[: rows // 2], q[rows // 2 :])):
            send_ref[2 * pair + at, 0, rows:, :] = tile.astype(narrow)


def project(inputs, norm_attn, first_values, cosine, sine, w_query, w_key, w_value, groups):
    rows, width = inputs.shape
    local = w_query.shape[1]
    part = rows // groups
    heads = local // HEAD_DIM
    fixed = lambda step: (0, 0)
    moving = lambda step: (step, 0)
    return pl.pallas_call(
        project_kernel,
        grid=(groups,),
        in_specs=[
            pl.BlockSpec((part, width), moving),
            pl.BlockSpec((1, width), fixed),
            pl.BlockSpec((part, local), moving),
            pl.BlockSpec((part, LANES), moving),
            pl.BlockSpec((part, LANES), moving),
            pl.BlockSpec((width, local), fixed),
            pl.BlockSpec((width, local), fixed),
            pl.BlockSpec((width, local), fixed),
        ],
        out_specs=[
            pl.BlockSpec((heads, 1, part + part // 2, LANES), lambda step: (0, step, 0, 0)),
            pl.BlockSpec((part, width), moving),
        ],
        out_shape=[
            jax.ShapeDtypeStruct((heads, groups, part + part // 2, LANES), narrow),
            jax.ShapeDtypeStruct((rows, width), narrow),
        ],
        compiler_params=pltpu.CompilerParams(vmem_limit_bytes=vmem_bytes),
        name="project",
    )(inputs, norm_attn.reshape(1, width), first_values, cosine, sine, w_query, w_key, w_value)


def tree_walk(run, count):
    for base in range(0, count, TREE):
        at = 0
        while at < TREE:
            same = 1
            while at + same < TREE and TREE_DEPTHS[at + same] == TREE_DEPTHS[at]:
                same += 1
            depth = TREE_DEPTHS[at]
            if same == 1:
                run(base + at, depth)
            else:
                def step(i, carry, start=base + at, depth=depth):
                    run(start + i, depth)
                    return carry

                lax.fori_loop(0, same, step, 0)
            at += same


def path_of(parents_ref, assign_ref, segment, depth):
    slots = [assign_ref[segment]]
    current = segment
    for _ in range(depth):
        current = parents_ref[current]
        slots.append(assign_ref[current])
    return slots


def unpack_low(packed):
    values = packed.astype(wide)
    low = lane_ids(values.shape) < HEAD_DIM
    top = jnp.where(low, values, 0.0)
    bottom = jnp.where(low, pltpu.roll(values, HEAD_DIM, 1), 0.0)
    return jnp.concatenate([top, bottom], axis=0).astype(narrow)


def unpack_high(packed):
    values = packed.astype(wide)
    high = lane_ids(values.shape) >= HEAD_DIM
    top = jnp.where(high, pltpu.roll(values, HEAD_DIM, 1), 0.0)
    bottom = jnp.where(high, values, 0.0)
    return jnp.concatenate([top, bottom], axis=0).astype(narrow)


def pack_columns(transposed):
    half = transposed.shape[1] // 2
    stacked = jnp.concatenate([transposed[:, :half], transposed[:, half:]], axis=0)
    return jnp.transpose(stacked)


def gather_parts(part, recv_ref, other_ref, kv_ref, kvt_ref, lanes):
    rows = other_ref.shape[1]

    def fill(slot, carry):
        kv_ref[slot, pl.ds(pl.multiple_of(part * rows, rows), rows), :] = recv_ref[slot, :rows, :]
        kv_ref[slot, pl.ds(pl.multiple_of((1 - part) * rows, rows), rows), :] = other_ref[slot]
        flipped = jnp.transpose(kv_ref[slot].astype(wide))
        kvt_ref[slot] = flipped[lanes].astype(narrow)
        return carry

    lax.fori_loop(0, recv_ref.shape[0], fill, 0)


def visible(part, keys, rows):
    key_row = lax.broadcasted_iota(jnp.int32, (keys, rows), 0)
    query_row = lax.broadcasted_iota(jnp.int32, (keys, rows), 1) + part * rows
    return key_row <= query_row


def attend_kernel(
    parents_ref, assign_ref, part_ref, recv_ref, other_ref, send_ref, ot_ref, log_ref, kv_ref, vt_ref
):
    part = part_ref[0]
    rows = other_ref.shape[1]
    gather_parts(part, recv_ref, other_ref, kv_ref, vt_ref, slice(HEAD_DIM, LANES))

    def run(segment, depth):
        slots = path_of(parents_ref, assign_ref, segment, depth)
        own = slots[0]
        query = unpack_low(recv_ref[own, rows:, :])
        scores = []
        for level, slot in enumerate(slots):
            block = dot_rows(kv_ref[slot], query)
            if level == 0:
                block = jnp.where(visible(part, SEG, rows), block, masked_score)
            scores.append(block)
        peak = jnp.max(scores[0], axis=0, keepdims=True)
        for block in scores[1:]:
            peak = jnp.maximum(peak, jnp.max(block, axis=0, keepdims=True))
        total = jnp.zeros_like(peak)
        mixed = jnp.zeros((HEAD_DIM, rows), wide)
        for block, slot in zip(scores, slots, strict=True):
            weight = jnp.exp(block - peak)
            total = total + jnp.sum(weight, axis=0, keepdims=True)
            mixed = mixed + dot_wide(vt_ref[slot], weight.astype(narrow))
        mixed = mixed / total
        ot_ref[own] = mixed
        log_ref[own] = jnp.broadcast_to(peak + jnp.log(total), (8, rows))
        send_ref[own] = pack_columns(mixed).astype(narrow)

    tree_walk(run, recv_ref.shape[0])


def attend(parents, assignment, part, recv, other):
    count, rows, _ = other.shape
    return pl.pallas_call(
        attend_kernel,
        in_specs=[scalar_spec()] * 3 + [whole_spec()] * 2,
        out_specs=[whole_spec()] * 3,
        out_shape=[
            jax.ShapeDtypeStruct((count, rows // 2, LANES), narrow),
            jax.ShapeDtypeStruct((count, HEAD_DIM, rows), wide),
            jax.ShapeDtypeStruct((count, 8, rows), wide),
        ],
        scratch_shapes=[
            pltpu.VMEM((count, SEG, LANES), narrow),
            pltpu.VMEM((count, HEAD_DIM, SEG), narrow),
        ],
        compiler_params=pltpu.CompilerParams(vmem_limit_bytes=vmem_bytes),
        name="attend",
    )(parents, assignment, part, recv, other)


def attend_back_kernel(
    parents_ref,
    assign_ref,
    part_ref,
    recv_ref,
    other_ref,
    grad_ref,
    ot_ref,
    log_ref,
    dq_ref,
    mine_ref,
    theirs_ref,
    kv_ref,
    kt_ref,
    sum_ref,
):
    part = part_ref[0]
    rows = other_ref.shape[1]
    count = recv_ref.shape[0]
    gather_parts(part, recv_ref, other_ref, kv_ref, kt_ref, slice(0, HEAD_DIM))

    def clear(slot, carry):
        sum_ref[slot] = jnp.zeros((SEG, LANES), wide)
        return carry

    lax.fori_loop(0, count, clear, 0)

    def run(segment, depth):
        slots = path_of(parents_ref, assign_ref, segment, depth)
        own = slots[0]
        query = unpack_low(recv_ref[own, rows:, :])
        packed = grad_ref[own]
        grad = unpack_high(packed)
        flipped = jnp.transpose(packed.astype(wide))
        grad_t = jnp.concatenate([flipped[:HEAD_DIM], flipped[HEAD_DIM:]], axis=1)
        delta = jnp.sum(grad_t * ot_ref[own], axis=0, keepdims=True)
        log_row = log_ref[own][:1]
        grad_query = jnp.zeros((HEAD_DIM, rows), wide)
        for level, slot in enumerate(slots):
            pair = kv_ref[slot]
            probs = jnp.exp(dot_rows(pair, query) - log_row)
            if level == 0:
                probs = jnp.where(visible(part, SEG, rows), probs, 0.0)
            grad_probs = dot_rows(pair, grad)
            grad_scores = (probs * (grad_probs - delta)).astype(narrow)
            sum_ref[slot] += dot_wide(grad_scores, query) + dot_wide(probs.astype(narrow), grad)
            grad_query = grad_query + dot_wide(kt_ref[slot], grad_scores)
        dq_ref[own] = pack_columns(grad_query * (HEAD_DIM ** (-0.5))).astype(narrow)

    tree_walk(run, count)

    def finish(slot, carry):
        mine_ref[slot] = sum_ref[slot, pl.ds(pl.multiple_of(part * rows, rows), rows), :]
        theirs = sum_ref[slot, pl.ds(pl.multiple_of((1 - part) * rows, rows), rows), :]
        theirs_ref[slot] = theirs.astype(narrow)
        return carry

    lax.fori_loop(0, count, finish, 0)


def attend_back(parents, assignment, part, recv, other, grad, ot, logs):
    count, rows, _ = other.shape
    return pl.pallas_call(
        attend_back_kernel,
        in_specs=[scalar_spec()] * 3 + [whole_spec()] * 5,
        out_specs=[whole_spec()] * 3,
        out_shape=[
            jax.ShapeDtypeStruct((count, rows // 2, LANES), narrow),
            jax.ShapeDtypeStruct((count, rows, LANES), wide),
            jax.ShapeDtypeStruct((count, rows, LANES), narrow),
        ],
        scratch_shapes=[
            pltpu.VMEM((count, SEG, LANES), narrow),
            pltpu.VMEM((count, HEAD_DIM, SEG), narrow),
            pltpu.VMEM((count, SEG, LANES), wide),
        ],
        compiler_params=pltpu.CompilerParams(vmem_limit_bytes=vmem_bytes),
        name="attend_back",
    )(parents, assignment, part, recv, other, grad, ot, logs)


def heads_to_rows(recv_ref, groups):
    half = recv_ref.shape[1]
    heads = recv_ref.shape[0] // groups
    strips = []
    for pair in range(heads // 2):
        pieces = []
        for part in range(groups):
            left = recv_ref[2 * pair * groups + part].astype(wide)
            right = recv_ref[(2 * pair + 1) * groups + part].astype(wide)
            pieces += list(swap_pairs(left, right))
        strips.append(jnp.concatenate(pieces, axis=0))
    return jnp.concatenate(strips, axis=1).astype(narrow)


def merge_kernel(
    own_ref, other_ref, w_own_ref, w_other_ref, x_ref, gain_ref, attended_ref, hidden_ref, normed_ref
):
    groups = 2
    mine = heads_to_rows(own_ref, groups)
    attended_ref[...] = mine
    theirs = heads_to_rows(other_ref, groups)
    branch = dot_wide(mine, w_own_ref[...]).astype(narrow).astype(wide)
    branch = branch + dot_wide(theirs, w_other_ref[...]).astype(narrow).astype(wide)
    hidden = x_ref[...].astype(wide) + branch
    hidden_ref[...] = hidden
    normed_ref[...] = (hidden * rms_scale(hidden) * gain_ref[...].astype(wide)).astype(narrow)


def merge(own, other, w_own, w_other, inputs, norm_ffn):
    tokens, width = inputs.shape
    local = w_own.shape[0]
    return pl.pallas_call(
        merge_kernel,
        in_specs=[whole_spec()] * 6,
        out_specs=[whole_spec()] * 3,
        out_shape=[
            jax.ShapeDtypeStruct((tokens, local), narrow),
            jax.ShapeDtypeStruct((tokens, width), wide),
            jax.ShapeDtypeStruct((tokens, width), narrow),
        ],
        compiler_params=pltpu.CompilerParams(vmem_limit_bytes=vmem_bytes),
        name="merge",
    )(own, other, w_own, w_other, inputs, norm_ffn.reshape(1, width))


def branch_back_kernel(
    own_ref, other_ref, hidden_ref, cot_ref, gain_ref, w_ref, send_ref, hidden_grad_ref, branch_ref, gain_grad_ref
):
    groups = 2
    grad_normed = own_ref[...].astype(wide) + other_ref[...].astype(wide)
    hidden = hidden_ref[...]
    back, gain_grad = norm_back(grad_normed, hidden, rms_scale(hidden), gain_ref[...].astype(wide))
    gain_grad_ref[...] = gain_grad[None]
    grad_hidden = cot_ref[...].astype(wide) + back
    hidden_grad_ref[...] = grad_hidden
    grad_branch = grad_hidden.astype(narrow)
    branch_ref[...] = grad_branch
    attended_grad = dot_rows(grad_branch, w_ref[...])
    tokens, local = attended_grad.shape
    half = tokens // groups // 2
    for pair in range(local // LANES):
        for part in range(groups):
            cols = slice(pair * LANES, (pair + 1) * LANES)
            low = attended_grad[2 * part * half : (2 * part + 1) * half, cols]
            high = attended_grad[(2 * part + 1) * half : (2 * part + 2) * half, cols]
            for at, tile in enumerate(swap_pairs(low, high)):
                send_ref[2 * pair + at, part] = tile.astype(narrow)


def branch_back(own, other, hidden, cotangent, norm_ffn, w_out):
    tokens, width = hidden.shape
    local = w_out.shape[0]
    groups = 2
    return pl.pallas_call(
        branch_back_kernel,
        in_specs=[whole_spec()] * 6,
        out_specs=[whole_spec()] * 4,
        out_shape=[
            jax.ShapeDtypeStruct((local // HEAD_DIM, groups, tokens // groups // 2, LANES), narrow),
            jax.ShapeDtypeStruct((tokens, width), wide),
            jax.ShapeDtypeStruct((tokens, width), narrow),
            jax.ShapeDtypeStruct((1, width), wide),
        ],
        compiler_params=pltpu.CompilerParams(vmem_limit_bytes=vmem_bytes),
        name="branch_back",
    )(own, other, hidden, cotangent, norm_ffn.reshape(1, width), w_out)


def unproject_kernel(
    recv_ref, cos_ref, sin_ref, wq_ref, wk_ref, wv_ref, gq_ref, gk_ref, gv_ref, first_ref, part_ref
):
    groups = 2
    rows = recv_ref.shape[1] * 2 // 3
    half = rows // 2
    heads = recv_ref.shape[0] // groups
    for part in range(groups):
        span = slice(part * rows, (part + 1) * rows)
        cosine = cos_ref[span, :]
        sine = -sin_ref[span, :]
        for pair in range(heads // 2):
            cols = slice(pair * LANES, (pair + 1) * LANES)
            left = recv_ref[2 * pair * groups + part].astype(wide)
            right = recv_ref[(2 * pair + 1) * groups + part].astype(wide)
            key, value = swap_pairs(left[:rows], right[:rows])
            query = jnp.concatenate(swap_pairs(left[rows:], right[rows:]), axis=0)
            gq_ref[span, cols] = spin(query, cosine, sine).astype(narrow)
            gk_ref[span, cols] = spin(key, cosine, sine).astype(narrow)
            value = 0.5 * value
            first_ref[span, cols] = value
            gv_ref[span, cols] = value.astype(narrow)
    total = dot_rows(gq_ref[...], wq_ref[...])
    total = total + dot_rows(gk_ref[...], wk_ref[...])
    total = total + dot_rows(gv_ref[...], wv_ref[...])
    part_ref[...] = total.astype(narrow)


def unproject(recv, cosine, sine, w_query, w_key, w_value):
    width, local = w_query.shape
    tokens = cosine.shape[0]
    return pl.pallas_call(
        unproject_kernel,
        in_specs=[whole_spec()] * 6,
        out_specs=[whole_spec()] * 5,
        out_shape=[jax.ShapeDtypeStruct((tokens, local), narrow)] * 3
        + [
            jax.ShapeDtypeStruct((tokens, local), wide),
            jax.ShapeDtypeStruct((tokens, width), narrow),
        ],
        compiler_params=pltpu.CompilerParams(vmem_limit_bytes=vmem_bytes),
        name="unproject",
    )(recv, cosine, sine, w_query, w_key, w_value)


def swap_tensor(values):
    return lax.ppermute(values, "tensor", [(0, 1), (1, 0)])


def swap_bit(values, bit, count):
    return lax.ppermute(values, "dp", [(i, i ^ bit) for i in range(count)])


def add_narrow(left, right):
    return (left.astype(wide) + right.astype(wide)).astype(narrow)


def take_part(values, index, parts):
    size = values.shape[0] // parts
    return lax.dynamic_slice_in_dim(values, index * size, size, 0)


def reduce_bit(values, bit, place, count):
    mine = (place // bit) % 2
    arrived = swap_bit(take_part(values, 1 - mine, 2), bit, count)
    return add_narrow(take_part(values, mine, 2), arrived)


def gather_bit(values, bit, place, count):
    mine = (place // bit) % 2
    arrived = swap_bit(values, bit, count)
    row = jnp.concatenate([arrived, values, arrived], axis=0)
    size = values.shape[0]
    return lax.dynamic_slice_in_dim(row, (1 - mine) * size, 2 * size, 0)


def line_pairs(line, stride, count, up, keep):
    pairs = []
    for device in range(count):
        at = device // stride
        if up and at + 1 < line and keep(at):
            pairs.append((device, device + stride))
        if not up and at >= 1 and keep(line - 1 - at):
            pairs.append((device, device - stride))
    return pairs


def reduce_line(values, stride, place, count):
    line = count // stride
    at = place // stride
    up = down = None
    for step in range(1, line):
        share_up = take_part(values, jnp.clip(line - step + at, 0, line - 1), line)
        share_down = take_part(values, jnp.clip(step - line + at, 0, line - 1), line)
        if up is not None:
            share_up = add_narrow(share_up, up)
            share_down = add_narrow(share_down, down)
        keep = lambda index, step=step: index <= step - 1
        up = lax.ppermute(share_up, "dp", line_pairs(line, stride, count, True, keep))
        down = lax.ppermute(share_down, "dp", line_pairs(line, stride, count, False, keep))
    own = take_part(values, at, line).astype(wide)
    return (own + up.astype(wide) + down.astype(wide)).astype(narrow)


def gather_line(values, stride, place, count):
    line = count // stride
    at = place // stride
    below, above = [], []
    up = down = values
    for step in range(1, line):
        keep_up = lambda index, step=step: index >= step - 1
        up = lax.ppermute(up, "dp", line_pairs(line, stride, count, True, keep_up))
        down = lax.ppermute(down, "dp", line_pairs(line, stride, count, False, keep_up))
        below.append(up)
        above.append(down)
    row = jnp.concatenate(below[::-1] + [values] + above, axis=0)
    size = values.shape[0]
    return lax.dynamic_slice_in_dim(row, (line - 1 - at) * size, line * size, 0)


def sum_over_dp(values, place, count):
    values = reduce_bit(values, 1, place, count)
    values = reduce_bit(values, 2, place, count)
    values = reduce_line(values, 4, place, count)
    values = gather_line(values, 4, place, count)
    values = gather_bit(values, 2, place, count)
    return gather_bit(values, 1, place, count).astype(wide)


def sum_small(values, count):
    bit = 1
    while bit < count:
        values = values + swap_bit(values, bit, count)
        bit *= 2
    return values


def body_heads(
    inputs,
    first_values,
    w_query,
    w_key,
    w_value,
    w_out,
    w_gate,
    w_up,
    w_down,
    norm_attn,
    norm_ffn,
    cotangent,
    parents,
    depth_pos,
    assignment,
):
    count = parents.shape[0]
    tokens, width = inputs.shape
    local = w_query.shape[1]
    heads = local // HEAD_DIM
    groups = count // heads
    place = lax.axis_index("dp")
    part = (place % groups).astype(jnp.int32)
    part_array = part.reshape(1)

    w_out_other = swap_tensor(w_out)
    slot_ids = jnp.arange(count, dtype=jnp.int32)
    start = jnp.sum(jnp.where(slot_ids == place, depth_pos, 0))
    positions = (start + jnp.arange(tokens, dtype=jnp.int32)).astype(wide)
    half = HEAD_DIM // 2
    lanes = jnp.arange(LANES, dtype=jnp.int32)
    frequency = rope_base ** (-(lanes % half).astype(wide) * 2.0 / HEAD_DIM)
    angles = positions[:, None] * frequency[None, :]
    cosine = jnp.cos(angles)
    sine = jnp.sin(angles) * jnp.where(lanes % HEAD_DIM < half, -1.0, 1.0)[None, :]

    send, normed = project(
        inputs, norm_attn, first_values, cosine, sine, w_query, w_key, w_value, groups
    )
    rows = tokens // groups
    send = send.reshape(count, rows + rows // 2, LANES)
    recv = lax.all_to_all(send, "dp", split_axis=0, concat_axis=0, tiled=True)
    other = swap_bit(recv[:, :rows], 1, count)
    packed, ot, logs = attend(parents, assignment, part_array, recv, other)
    own_out = lax.all_to_all(packed, "dp", split_axis=0, concat_axis=0, tiled=True)
    other_out = swap_tensor(own_out)
    attended, hidden, normed_ffn = merge(own_out, other_out, w_out, w_out_other, inputs, norm_ffn)

    gate_proj = jnp.dot(normed_ffn, w_gate, preferred_element_type=wide)
    up_proj = jnp.dot(normed_ffn, w_up, preferred_element_type=wide)
    silu_gate = jax.nn.silu(gate_proj)
    activated = (silu_gate * up_proj).astype(narrow)
    grad_activated = jnp.einsum("td,fd->tf", cotangent, w_down, preferred_element_type=wide)
    sigmoid_gate = jax.nn.sigmoid(gate_proj)
    grad_gate = (
        grad_activated * up_proj * sigmoid_gate * (1.0 + gate_proj * (1.0 - sigmoid_gate))
    ).astype(narrow)
    grad_up = (grad_activated * silu_gate).astype(narrow)
    ffn_partial = (
        jnp.einsum("tf,df->td", grad_gate, w_gate, preferred_element_type=wide)
        + jnp.einsum("tf,df->td", grad_up, w_up, preferred_element_type=wide)
    ).astype(narrow)
    ffn_other = swap_tensor(ffn_partial)
    grad_w_gate = jnp.einsum("td,tf->df", normed_ffn, grad_gate, preferred_element_type=wide)
    grad_w_up = jnp.einsum("td,tf->df", normed_ffn, grad_up, preferred_element_type=wide)
    grad_w_down = jnp.einsum("tf,td->fd", activated, cotangent, preferred_element_type=wide)
    grad_w_gate, grad_w_up, grad_w_down = lax.psum(
        (grad_w_gate.astype(narrow), grad_w_up.astype(narrow), grad_w_down.astype(narrow)), "dp"
    )
    feed_partial = jnp.dot(activated, w_down, preferred_element_type=wide).astype(narrow)

    grad_send, grad_hidden, grad_branch, grad_gain_ffn = branch_back(
        ffn_partial, ffn_other, hidden, cotangent, norm_ffn, w_out
    )
    grad_recv = lax.all_to_all(
        grad_send.reshape(count, rows // 2, LANES), "dp", split_axis=0, concat_axis=0, tiled=True
    )
    feed_other = swap_tensor(feed_partial)
    feed = feed_partial.astype(wide) + feed_other.astype(wide)
    output = (hidden + feed).astype(narrow)
    grad_w_out = jnp.einsum("tc,td->cd", attended, grad_branch, preferred_element_type=wide)

    grad_q, mine, theirs = attend_back(
        parents, assignment, part_array, recv, other, grad_recv, ot, logs
    )
    arrived = swap_bit(theirs, 1, count)
    back_send = jnp.concatenate([(mine + arrived.astype(wide)).astype(narrow), grad_q], axis=1)
    back_recv = lax.all_to_all(back_send, "dp", split_axis=0, concat_axis=0, tiled=True)
    grad_query, grad_key, grad_value, grad_first, attn_partial = unproject(
        back_recv, cosine, sine, w_query, w_key, w_value
    )
    attn_other = swap_tensor(attn_partial)
    grad_w_query = jnp.einsum("td,tc->dc", normed, grad_query, preferred_element_type=wide)
    grad_w_key = jnp.einsum("td,tc->dc", normed, grad_key, preferred_element_type=wide)
    grad_w_value = jnp.einsum("td,tc->dc", normed, grad_value, preferred_element_type=wide)
    sums = [
        sum_over_dp(term.astype(narrow), place, count)
        for term in (grad_w_query, grad_w_key, grad_w_value, grad_w_out)
    ]
    inputs_wide = inputs.astype(wide)
    grad_normed = attn_partial.astype(wide) + attn_other.astype(wide)
    grad_input_norm, grad_gain_attn = norm_back(
        grad_normed, inputs_wide, rms_scale(inputs_wide), norm_attn.astype(wide)
    )
    grad_inputs = grad_hidden + grad_input_norm
    gains = sum_small(jnp.stack([grad_gain_attn, grad_gain_ffn[0]]), count)
    return (
        output,
        grad_inputs,
        grad_first,
        sums[0],
        sums[1],
        sums[2],
        sums[3],
        grad_w_gate.astype(wide),
        grad_w_up.astype(wide),
        grad_w_down.astype(wide),
        gains[0],
        gains[1],
    )


def pick_body(mesh):
    if mesh.shape["dp"] == 16 and mesh.shape["tensor"] == 2:
        return body_heads
    return body_general


def solution(mesh):
    placed = (
        P("dp", None),
        P("dp", "tensor"),
        P(None, "tensor"),
        P(None, "tensor"),
        P(None, "tensor"),
        P("tensor", None),
        P(None, "tensor"),
        P(None, "tensor"),
        P("tensor", None),
        P(),
        P(),
        P("dp", None),
        P(),
        P(),
        P(),
    )
    return jax.shard_map(
        pick_body(mesh),
        mesh=mesh,
        in_specs=placed,
        out_specs=(
            P("dp", None),
            P("dp", None),
            P("dp", "tensor"),
            P(None, "tensor"),
            P(None, "tensor"),
            P(None, "tensor"),
            P("tensor", None),
            P(None, "tensor"),
            P(None, "tensor"),
            P("tensor", None),
            P(),
            P(),
        ),
        check_vma=False,
    )
```

```python
import jax
import jax.numpy as jnp
from jax import lax
from jax.experimental import pallas as pl
from jax.experimental.pallas import tpu as pltpu
from jax.sharding import PartitionSpec as P

HEAD_DIM = 64
SEG = 512


epsilon = 1e-06
rope_base = 10000.0
climb_steps = 5
masked_score = -1e30


def rms_scale(values):
    return lax.rsqrt(jnp.mean(values * values, axis=-1, keepdims=True) + epsilon)


def rotary_tables(positions, head_dim):
    half_dim = head_dim // 2
    frequency = rope_base ** (-jnp.arange(half_dim, dtype=jnp.float32) * 2.0 / head_dim)
    angles = positions.astype(jnp.float32)[:, None] * frequency[None, :]
    return (jnp.cos(angles)[:, None, :], jnp.sin(angles)[:, None, :])


def rotate(values, cosine, sine_table):
    half_dim = values.shape[-1] // 2
    first_half = values[..., :half_dim]
    second_half = values[..., half_dim:]
    return jnp.concatenate(
        [
            first_half * cosine - second_half * sine_table,
            second_half * cosine + first_half * sine_table,
        ],
        axis=-1,
    )


def rotate_back(gradient, cosine, sine_table):
    half_dim = gradient.shape[-1] // 2
    first_half = gradient[..., :half_dim]
    second_half = gradient[..., half_dim:]
    return jnp.concatenate(
        [
            first_half * cosine + second_half * sine_table,
            second_half * cosine - first_half * sine_table,
        ],
        axis=-1,
    )


def parent_slots(parents, assignment):
    count = parents.shape[0]
    slot_ids = jnp.arange(count, dtype=jnp.int32)
    at_slot = assignment[None, :] == slot_ids[:, None]
    parent_seg = jnp.sum(jnp.where(at_slot, parents[None, :], 0), axis=1)
    parent_match = slot_ids[None, :] == parent_seg[:, None]
    above_slot = jnp.sum(jnp.where(parent_match, assignment[None, :], 0), axis=1)
    return jnp.where(parent_seg >= 0, above_slot, -1)


def climb(parent_slot, start_slots):
    slot_ids = jnp.arange(parent_slot.shape[0], dtype=jnp.int32)
    levels = [start_slots]
    current = start_slots
    for step_index in range(climb_steps):
        matched = current[:, None] == slot_ids[None, :]
        upward = jnp.sum(jnp.where(matched, parent_slot[None, :], 0), axis=1)
        current = jnp.where(current >= 0, upward, -1)
        levels.append(current)
    return jnp.stack(levels, axis=1)


def norm_back(grad_normed, values, row_scale, gain_vector):
    scaled_grad = grad_normed * gain_vector
    grad_gain = jnp.sum(grad_normed * values * row_scale, axis=0)
    grad_values = row_scale * (
        scaled_grad
        - values * row_scale * row_scale * jnp.mean(scaled_grad * values, axis=-1, keepdims=True)
    )
    return (grad_values, grad_gain)


def path_rows(source, path_row):
    parts = []
    for level_index in range(climb_steps + 1):
        row_begin = (jnp.maximum(path_row[level_index], 0) * SEG).astype(jnp.int32)
        parts.append(lax.dynamic_slice_in_dim(source, row_begin, SEG, 0))
    return jnp.concatenate(parts, axis=0)


def path_permit(path_row, causal):
    parts = [causal]
    for level_index in range(1, climb_steps + 1):
        parts.append(jnp.broadcast_to(path_row[level_index] >= 0, (SEG, SEG)))
    return jnp.concatenate(parts, axis=1)


def body_general(
    inputs,
    first_values,
    w_query,
    w_key,
    w_value,
    w_out,
    w_gate,
    w_up,
    w_down,
    norm_attn,
    norm_ffn,
    cotangent,
    parents,
    depth_pos,
    assignment,
):
    row_count = inputs.shape[0]
    local_width = w_query.shape[1]
    head_count = local_width // HEAD_DIM
    score_scale = HEAD_DIM ** (-0.5)
    seg_count = row_count // SEG
    slot_total = parents.shape[0]
    slot_ids = jnp.arange(slot_total, dtype=jnp.int32)
    local_rows = jnp.arange(row_count, dtype=jnp.int32)
    own_slots = lax.axis_index("dp") * seg_count + jnp.arange(seg_count, dtype=jnp.int32)
    own_slot_rows = jnp.repeat(own_slots, SEG)
    depth_rows = jnp.sum(
        jnp.where(own_slot_rows[:, None] == slot_ids[None, :], depth_pos[None, :], 0), axis=1
    )
    positions = depth_rows + local_rows % SEG
    parent_slot = parent_slots(parents, assignment)
    own_paths = climb(parent_slot, own_slots)
    offsets = jnp.arange(SEG, dtype=jnp.int32)
    causal = offsets[None, :] <= offsets[:, None]
    cosine, sine_table = rotary_tables(positions, HEAD_DIM)
    inputs_wide = inputs.astype(jnp.float32)
    attn_scale = rms_scale(inputs_wide)
    gain_attn = norm_attn.astype(jnp.float32)
    normed = (inputs_wide * attn_scale * gain_attn).astype(jnp.bfloat16)
    query_proj = jnp.dot(normed, w_query, preferred_element_type=jnp.float32)
    key_proj = jnp.dot(normed, w_key, preferred_element_type=jnp.float32)
    value_proj = jnp.dot(normed, w_value, preferred_element_type=jnp.float32)
    query_rot = rotate(
        query_proj.reshape(row_count, head_count, HEAD_DIM), cosine, sine_table
    ).astype(jnp.bfloat16)
    key_rot = (
        rotate(key_proj.reshape(row_count, head_count, HEAD_DIM), cosine, sine_table)
        .astype(jnp.bfloat16)
        .reshape(row_count, local_width)
    )
    mixed = (0.5 * value_proj + 0.5 * first_values.astype(jnp.float32)).astype(jnp.bfloat16)
    key_all, value_all = (
        lax.all_gather(key_rot, "dp", axis=0, tiled=True),
        lax.all_gather(mixed, "dp", axis=0, tiled=True),
    )
    query_segs = query_rot.reshape(seg_count, SEG, head_count, HEAD_DIM)

    def segment_forward(operand):
        query_block, path_row = operand
        near_keys = path_rows(key_all, path_row).reshape(-1, head_count, HEAD_DIM)
        near_values = path_rows(value_all, path_row).reshape(-1, head_count, HEAD_DIM)
        permit = path_permit(path_row, causal)
        scores = (
            jnp.einsum("qhd,khd->hqk", query_block, near_keys, preferred_element_type=jnp.float32)
            * score_scale
        )
        scores = jnp.where(permit[None], scores, masked_score)
        row_max = jnp.max(scores, axis=-1)
        weights = jnp.where(permit[None], jnp.exp(scores - row_max[..., None]), 0.0)
        row_total = jnp.sum(weights, axis=-1)
        attn_probs = weights / row_total[..., None]
        block_out = jnp.einsum(
            "hqk,khd->qhd",
            attn_probs.astype(jnp.bfloat16),
            near_values,
            preferred_element_type=jnp.float32,
        )
        return (block_out, row_max + jnp.log(row_total))

    attn_parts, log_parts = lax.map(segment_forward, (query_segs, own_paths))
    attn_exact = attn_parts.reshape(row_count, head_count, HEAD_DIM)
    attended = attn_exact.reshape(row_count, local_width).astype(jnp.bfloat16)
    branch_attn = lax.psum(
        jnp.dot(attended, w_out, preferred_element_type=jnp.float32).astype(jnp.bfloat16), "tensor"
    ).astype(jnp.float32)
    hidden_state = inputs_wide + branch_attn
    ffn_scale = rms_scale(hidden_state)
    gain_ffn = norm_ffn.astype(jnp.float32)
    normed_ffn = (hidden_state * ffn_scale * gain_ffn).astype(jnp.bfloat16)
    gate_proj = jnp.dot(normed_ffn, w_gate, preferred_element_type=jnp.float32)
    up_proj = jnp.dot(normed_ffn, w_up, preferred_element_type=jnp.float32)
    silu_gate = jax.nn.silu(gate_proj)
    activated = (silu_gate * up_proj).astype(jnp.bfloat16)
    feed = lax.psum(
        jnp.dot(activated, w_down, preferred_element_type=jnp.float32).astype(jnp.bfloat16),
        "tensor",
    ).astype(jnp.float32)
    output = (hidden_state + feed).astype(jnp.bfloat16)
    grad_w_down = jnp.einsum("tf,td->fd", activated, cotangent, preferred_element_type=jnp.float32)
    grad_activated = jnp.einsum("td,fd->tf", cotangent, w_down, preferred_element_type=jnp.float32)
    sigmoid_gate = jax.nn.sigmoid(gate_proj)
    grad_gate = (
        grad_activated * up_proj * sigmoid_gate * (1.0 + gate_proj * (1.0 - sigmoid_gate))
    ).astype(jnp.bfloat16)
    grad_up = (grad_activated * silu_gate).astype(jnp.bfloat16)
    grad_w_gate = jnp.einsum("td,tf->df", normed_ffn, grad_gate, preferred_element_type=jnp.float32)
    grad_w_up = jnp.einsum("td,tf->df", normed_ffn, grad_up, preferred_element_type=jnp.float32)
    ffn_partial = jnp.einsum(
        "tf,df->td", grad_gate, w_gate, preferred_element_type=jnp.float32
    ) + jnp.einsum("tf,df->td", grad_up, w_up, preferred_element_type=jnp.float32)
    grad_normed_ffn = lax.psum(ffn_partial.astype(jnp.bfloat16), "tensor").astype(jnp.float32)
    grad_hidden_norm, grad_gain_ffn = norm_back(grad_normed_ffn, hidden_state, ffn_scale, gain_ffn)
    grad_hidden = cotangent.astype(jnp.float32) + grad_hidden_norm
    grad_branch = grad_hidden.astype(jnp.bfloat16)
    grad_w_out = jnp.einsum("tc,td->cd", attended, grad_branch, preferred_element_type=jnp.float32)
    grad_attended = jnp.einsum(
        "td,cd->tc", grad_branch, w_out, preferred_element_type=jnp.float32
    ).astype(jnp.bfloat16)
    grad_heads = grad_attended.reshape(row_count, head_count, HEAD_DIM)
    delta_rows = jnp.sum(grad_heads.astype(jnp.float32) * attn_exact, axis=-1)
    delta_parts = jnp.transpose(delta_rows.reshape(seg_count, SEG, head_count), (0, 2, 1))
    grad_segs = grad_heads.reshape(seg_count, SEG, head_count, HEAD_DIM)
    key_back, value_back = (key_all, value_all)

    def segment_back(query_block, grad_block, path_row, log_block, delta_block):
        near_keys = path_rows(key_back, path_row).reshape(-1, head_count, HEAD_DIM)
        near_values = path_rows(value_back, path_row).reshape(-1, head_count, HEAD_DIM)
        permit = path_permit(path_row, causal)
        scores = (
            jnp.einsum("qhd,khd->hqk", query_block, near_keys, preferred_element_type=jnp.float32)
            * score_scale
        )
        scores = jnp.where(permit[None], scores, masked_score)
        attn_probs = jnp.where(permit[None], jnp.exp(scores - log_block[..., None]), 0.0)
        grad_probs = jnp.einsum(
            "qhd,khd->hqk", grad_block, near_values, preferred_element_type=jnp.float32
        )
        grad_scores = (attn_probs * (grad_probs - delta_block[..., None])).astype(jnp.bfloat16)
        grad_part = (
            jnp.einsum("hqk,khd->qhd", grad_scores, near_keys, preferred_element_type=jnp.float32)
            * score_scale
        )
        return (attn_probs, grad_scores, grad_part)

    zero_rows = jnp.zeros((key_back.shape[0], local_width), jnp.float32)

    def scatter_step(fold_state, operand):
        key_acc, value_acc = fold_state
        query_block, grad_block, path_row, log_block, delta_block = operand
        attn_probs, grad_scores, grad_part = segment_back(
            query_block, grad_block, path_row, log_block, delta_block
        )
        key_term = (
            jnp.einsum("hqk,qhd->khd", grad_scores, query_block, preferred_element_type=jnp.float32)
            * score_scale
        ).reshape(climb_steps + 1, SEG, local_width)
        value_term = jnp.einsum(
            "hqk,qhd->khd",
            attn_probs.astype(jnp.bfloat16),
            grad_block,
            preferred_element_type=jnp.float32,
        ).reshape(climb_steps + 1, SEG, local_width)
        for level_index in range(climb_steps + 1):
            row_begin = (jnp.maximum(path_row[level_index], 0) * SEG).astype(jnp.int32)
            key_acc = lax.dynamic_update_slice_in_dim(
                key_acc,
                lax.dynamic_slice_in_dim(key_acc, row_begin, SEG, 0) + key_term[level_index],
                row_begin,
                0,
            )
            value_acc = lax.dynamic_update_slice_in_dim(
                value_acc,
                lax.dynamic_slice_in_dim(value_acc, row_begin, SEG, 0) + value_term[level_index],
                row_begin,
                0,
            )
        return ((key_acc, value_acc), grad_part)

    (key_terms, value_terms), grad_parts = lax.scan(
        scatter_step,
        (zero_rows, zero_rows),
        (query_segs, grad_segs, own_paths, log_parts, delta_parts),
    )
    grad_query_rot = grad_parts.reshape(row_count, head_count, HEAD_DIM)
    key_sums, value_sums = (
        lax.psum_scatter(
            key_terms.astype(jnp.bfloat16), "dp", scatter_dimension=0, tiled=True
        ).astype(jnp.float32),
        lax.psum_scatter(
            value_terms.astype(jnp.bfloat16), "dp", scatter_dimension=0, tiled=True
        ).astype(jnp.float32),
    )
    grad_key_rot = key_sums.reshape(row_count, head_count, HEAD_DIM)
    grad_first_values = 0.5 * value_sums
    grad_value = (0.5 * value_sums).astype(jnp.bfloat16)
    grad_key = (
        rotate_back(grad_key_rot, cosine, sine_table)
        .reshape(row_count, local_width)
        .astype(jnp.bfloat16)
    )
    grad_query = (
        rotate_back(grad_query_rot, cosine, sine_table)
        .reshape(row_count, local_width)
        .astype(jnp.bfloat16)
    )
    grad_w_query = jnp.einsum("td,tc->dc", normed, grad_query, preferred_element_type=jnp.float32)
    grad_w_key = jnp.einsum("td,tc->dc", normed, grad_key, preferred_element_type=jnp.float32)
    grad_w_value = jnp.einsum("td,tc->dc", normed, grad_value, preferred_element_type=jnp.float32)
    attn_partial = (
        jnp.einsum("tc,dc->td", grad_query, w_query, preferred_element_type=jnp.float32)
        + jnp.einsum("tc,dc->td", grad_key, w_key, preferred_element_type=jnp.float32)
        + jnp.einsum("tc,dc->td", grad_value, w_value, preferred_element_type=jnp.float32)
    )
    grad_normed = lax.psum(attn_partial.astype(jnp.bfloat16), "tensor").astype(jnp.float32)
    grad_input_norm, grad_gain_attn = norm_back(grad_normed, inputs_wide, attn_scale, gain_attn)
    grad_inputs = grad_hidden + grad_input_norm
    summed = (
        lax.psum(grad_w_query.astype(jnp.bfloat16), "dp").astype(jnp.float32),
        lax.psum(grad_w_key.astype(jnp.bfloat16), "dp").astype(jnp.float32),
        lax.psum(grad_w_value.astype(jnp.bfloat16), "dp").astype(jnp.float32),
        lax.psum(grad_w_out.astype(jnp.bfloat16), "dp").astype(jnp.float32),
        lax.psum(grad_w_gate.astype(jnp.bfloat16), "dp").astype(jnp.float32),
        lax.psum(grad_w_up.astype(jnp.bfloat16), "dp").astype(jnp.float32),
        lax.psum(grad_w_down.astype(jnp.bfloat16), "dp").astype(jnp.float32),
        lax.psum(grad_gain_attn.astype(jnp.bfloat16), "dp").astype(jnp.float32),
        lax.psum(grad_gain_ffn.astype(jnp.bfloat16), "dp").astype(jnp.float32),
    )
    return (
        output,
        grad_inputs,
        grad_first_values,
        summed[0],
        summed[1],
        summed[2],
        summed[3],
        summed[4],
        summed[5],
        summed[6],
        summed[7],
        summed[8],
    )


TREE = 16
TREE_DEPTHS = (0, 1, 2, 3, 4, 4, 4, 4, 5, 5, 5, 5, 5, 5, 5, 5)
LANES = 128
wide = jnp.float32
narrow = jnp.bfloat16
vmem_bytes = 60 * 1024 * 1024


def busy(microseconds):
    return pl.CostEstimate(
        flops=int(microseconds * 1e9), bytes_accessed=int(microseconds * 2e6), transcendentals=0
    )


def lane_ids(shape):
    return lax.broadcasted_iota(jnp.int32, shape, len(shape) - 1)


def swap_pairs(left, right):
    low = lane_ids(left.shape) < HEAD_DIM
    first = jnp.where(low, left, pltpu.roll(right, HEAD_DIM, 1))
    second = jnp.where(low, pltpu.roll(left, HEAD_DIM, 1), right)
    return first, second


def spin(values, cosine, signed_sine):
    half = HEAD_DIM // 2
    ahead = pltpu.roll(values, LANES - half, 1)
    behind = pltpu.roll(values, half, 1)
    other = jnp.where(lane_ids(values.shape) % HEAD_DIM < half, ahead, behind)
    return values * cosine + other * signed_sine


def dot_wide(left, right):
    return jnp.dot(left, right, preferred_element_type=wide)


def dot_rows(left, right):
    return lax.dot_general(left, right, (((1,), (1,)), ((), ())), preferred_element_type=wide)


def whole_spec():
    return pl.BlockSpec(memory_space=pltpu.VMEM)


def scalar_spec():
    return pl.BlockSpec(memory_space=pltpu.SMEM)


def project_kernel(
    x_ref, gain_ref, first_ref, cos_ref, sin_ref, wq_ref, wk_ref, wv_ref, send_ref, normed_ref
):
    rows = x_ref.shape[0]
    pairs = first_ref.shape[1] // LANES
    x = x_ref[...].astype(wide)
    normed = (x * rms_scale(x) * gain_ref[...].astype(wide)).astype(narrow)
    normed_ref[...] = normed
    query = dot_wide(normed, wq_ref[...]) * (HEAD_DIM ** (-0.5))
    key = dot_wide(normed, wk_ref[...])
    value = dot_wide(normed, wv_ref[...])
    mixed = 0.5 * value + 0.5 * first_ref[...].astype(wide)
    cosine = cos_ref[...]
    sine = sin_ref[...]
    for pair in range(pairs):
        cols = slice(pair * LANES, (pair + 1) * LANES)
        q = spin(query[:, cols], cosine, sine)
        k = spin(key[:, cols], cosine, sine)
        for at, tile in enumerate(swap_pairs(k, mixed[:, cols])):
            send_ref[2 * pair + at, 0, :rows, :] = tile.astype(narrow)
        for at, tile in enumerate(swap_pairs(q[: rows // 2], q[rows // 2 :])):
            send_ref[2 * pair + at, 0, rows:, :] = tile.astype(narrow)


def project(inputs, norm_attn, first_values, cosine, sine, w_query, w_key, w_value, groups):
    rows, width = inputs.shape
    local = w_query.shape[1]
    part = rows // groups
    heads = local // HEAD_DIM
    fixed = lambda step: (0, 0)
    moving = lambda step: (step, 0)
    return pl.pallas_call(
        project_kernel,
        grid=(groups,),
        in_specs=[
            pl.BlockSpec((part, width), moving),
            pl.BlockSpec((1, width), fixed),
            pl.BlockSpec((part, local), moving),
            pl.BlockSpec((part, LANES), moving),
            pl.BlockSpec((part, LANES), moving),
            pl.BlockSpec((width, local), fixed),
            pl.BlockSpec((width, local), fixed),
            pl.BlockSpec((width, local), fixed),
        ],
        out_specs=[
            pl.BlockSpec((heads, 1, part + part // 2, LANES), lambda step: (0, step, 0, 0)),
            pl.BlockSpec((part, width), moving),
        ],
        out_shape=[
            jax.ShapeDtypeStruct((heads, groups, part + part // 2, LANES), narrow),
            jax.ShapeDtypeStruct((rows, width), narrow),
        ],
        compiler_params=pltpu.CompilerParams(vmem_limit_bytes=vmem_bytes),
        cost_estimate=busy(6),
        name="project",
    )(inputs, norm_attn.reshape(1, width), first_values, cosine, sine, w_query, w_key, w_value)


def tree_walk(run, count):
    for base in range(0, count, TREE):
        at = 0
        while at < TREE:
            same = 1
            while at + same < TREE and TREE_DEPTHS[at + same] == TREE_DEPTHS[at]:
                same += 1
            depth = TREE_DEPTHS[at]
            if same == 1:
                run(base + at, depth)
            else:
                def step(i, carry, start=base + at, depth=depth):
                    run(start + i, depth)
                    return carry

                lax.fori_loop(0, same, step, 0)
            at += same


def path_of(parents_ref, assign_ref, segment, depth):
    slots = [assign_ref[segment]]
    current = segment
    for _ in range(depth):
        current = parents_ref[current]
        slots.append(assign_ref[current])
    return slots


def unpack_low(packed):
    values = packed.astype(wide)
    low = lane_ids(values.shape) < HEAD_DIM
    top = jnp.where(low, values, 0.0)
    bottom = jnp.where(low, pltpu.roll(values, HEAD_DIM, 1), 0.0)
    return jnp.concatenate([top, bottom], axis=0).astype(narrow)


def unpack_high(packed):
    values = packed.astype(wide)
    high = lane_ids(values.shape) >= HEAD_DIM
    top = jnp.where(high, pltpu.roll(values, HEAD_DIM, 1), 0.0)
    bottom = jnp.where(high, values, 0.0)
    return jnp.concatenate([top, bottom], axis=0).astype(narrow)


def pack_columns(transposed):
    half = transposed.shape[1] // 2
    stacked = jnp.concatenate([transposed[:, :half], transposed[:, half:]], axis=0)
    return jnp.transpose(stacked)


def gather_parts(part, recv_ref, other_ref, kv_ref, kvt_ref, lanes):
    rows = other_ref.shape[1]

    def fill(slot, carry):
        kv_ref[slot, pl.ds(pl.multiple_of(part * rows, rows), rows), :] = recv_ref[slot, :rows, :]
        kv_ref[slot, pl.ds(pl.multiple_of((1 - part) * rows, rows), rows), :] = other_ref[slot]
        flipped = jnp.transpose(kv_ref[slot].astype(wide))
        kvt_ref[slot] = flipped[lanes].astype(narrow)
        return carry

    lax.fori_loop(0, recv_ref.shape[0], fill, 0)


def visible(part, keys, rows):
    key_row = lax.broadcasted_iota(jnp.int32, (keys, rows), 0)
    query_row = lax.broadcasted_iota(jnp.int32, (keys, rows), 1) + part * rows
    return key_row <= query_row


def attend_kernel(
    parents_ref, assign_ref, part_ref, recv_ref, other_ref, send_ref, ot_ref, log_ref, kv_ref, vt_ref
):
    part = part_ref[0]
    rows = other_ref.shape[1]
    gather_parts(part, recv_ref, other_ref, kv_ref, vt_ref, slice(HEAD_DIM, LANES))

    def run(segment, depth):
        slots = path_of(parents_ref, assign_ref, segment, depth)
        own = slots[0]
        query = unpack_low(recv_ref[own, rows:, :])
        scores = []
        for level, slot in enumerate(slots):
            block = dot_rows(kv_ref[slot], query)
            if level == 0:
                block = jnp.where(visible(part, SEG, rows), block, masked_score)
            scores.append(block)
        peak = jnp.max(scores[0], axis=0, keepdims=True)
        for block in scores[1:]:
            peak = jnp.maximum(peak, jnp.max(block, axis=0, keepdims=True))
        total = jnp.zeros_like(peak)
        mixed = jnp.zeros((HEAD_DIM, rows), wide)
        for block, slot in zip(scores, slots, strict=True):
            weight = jnp.exp(block - peak)
            total = total + jnp.sum(weight, axis=0, keepdims=True)
            mixed = mixed + dot_wide(vt_ref[slot], weight.astype(narrow))
        mixed = mixed / total
        ot_ref[own] = mixed
        log_ref[own] = jnp.broadcast_to(peak + jnp.log(total), (8, rows))
        send_ref[own] = pack_columns(mixed).astype(narrow)

    tree_walk(run, recv_ref.shape[0])


def attend(parents, assignment, part, recv, other):
    count, rows, _ = other.shape
    return pl.pallas_call(
        attend_kernel,
        in_specs=[scalar_spec()] * 3 + [whole_spec()] * 2,
        out_specs=[whole_spec()] * 3,
        out_shape=[
            jax.ShapeDtypeStruct((count, rows // 2, LANES), narrow),
            jax.ShapeDtypeStruct((count, HEAD_DIM, rows), wide),
            jax.ShapeDtypeStruct((count, 8, rows), wide),
        ],
        scratch_shapes=[
            pltpu.VMEM((count, SEG, LANES), narrow),
            pltpu.VMEM((count, HEAD_DIM, SEG), narrow),
        ],
        compiler_params=pltpu.CompilerParams(vmem_limit_bytes=vmem_bytes),
        cost_estimate=busy(30),
        name="attend",
    )(parents, assignment, part, recv, other)


def attend_back_kernel(
    parents_ref,
    assign_ref,
    part_ref,
    recv_ref,
    other_ref,
    grad_ref,
    ot_ref,
    log_ref,
    dq_ref,
    mine_ref,
    theirs_ref,
    kv_ref,
    kt_ref,
    sum_ref,
):
    part = part_ref[0]
    rows = other_ref.shape[1]
    count = recv_ref.shape[0]
    gather_parts(part, recv_ref, other_ref, kv_ref, kt_ref, slice(0, HEAD_DIM))

    def clear(slot, carry):
        sum_ref[slot] = jnp.zeros((SEG, LANES), wide)
        return carry

    lax.fori_loop(0, count, clear, 0)

    def run(segment, depth):
        slots = path_of(parents_ref, assign_ref, segment, depth)
        own = slots[0]
        query = unpack_low(recv_ref[own, rows:, :])
        packed = grad_ref[own]
        grad = unpack_high(packed)
        flipped = jnp.transpose(packed.astype(wide))
        grad_t = jnp.concatenate([flipped[:HEAD_DIM], flipped[HEAD_DIM:]], axis=1)
        delta = jnp.sum(grad_t * ot_ref[own], axis=0, keepdims=True)
        log_row = log_ref[own][:1]
        grad_query = jnp.zeros((HEAD_DIM, rows), wide)
        for level, slot in enumerate(slots):
            pair = kv_ref[slot]
            probs = jnp.exp(dot_rows(pair, query) - log_row)
            if level == 0:
                probs = jnp.where(visible(part, SEG, rows), probs, 0.0)
            grad_probs = dot_rows(pair, grad)
            grad_scores = (probs * (grad_probs - delta)).astype(narrow)
            sum_ref[slot] += dot_wide(grad_scores, query) + dot_wide(probs.astype(narrow), grad)
            grad_query = grad_query + dot_wide(kt_ref[slot], grad_scores)
        dq_ref[own] = pack_columns(grad_query * (HEAD_DIM ** (-0.5))).astype(narrow)

    tree_walk(run, count)

    def finish(slot, carry):
        mine_ref[slot] = sum_ref[slot, pl.ds(pl.multiple_of(part * rows, rows), rows), :]
        theirs = sum_ref[slot, pl.ds(pl.multiple_of((1 - part) * rows, rows), rows), :]
        theirs_ref[slot] = theirs.astype(narrow)
        return carry

    lax.fori_loop(0, count, finish, 0)


def attend_back(parents, assignment, part, recv, other, grad, ot, logs):
    count, rows, _ = other.shape
    return pl.pallas_call(
        attend_back_kernel,
        in_specs=[scalar_spec()] * 3 + [whole_spec()] * 5,
        out_specs=[whole_spec()] * 3,
        out_shape=[
            jax.ShapeDtypeStruct((count, rows // 2, LANES), narrow),
            jax.ShapeDtypeStruct((count, rows, LANES), wide),
            jax.ShapeDtypeStruct((count, rows, LANES), narrow),
        ],
        scratch_shapes=[
            pltpu.VMEM((count, SEG, LANES), narrow),
            pltpu.VMEM((count, HEAD_DIM, SEG), narrow),
            pltpu.VMEM((count, SEG, LANES), wide),
        ],
        compiler_params=pltpu.CompilerParams(vmem_limit_bytes=vmem_bytes),
        cost_estimate=busy(37),
        name="attend_back",
    )(parents, assignment, part, recv, other, grad, ot, logs)


def heads_to_rows(recv_ref, groups):
    half = recv_ref.shape[1]
    heads = recv_ref.shape[0] // groups
    strips = []
    for pair in range(heads // 2):
        pieces = []
        for part in range(groups):
            left = recv_ref[2 * pair * groups + part].astype(wide)
            right = recv_ref[(2 * pair + 1) * groups + part].astype(wide)
            pieces += list(swap_pairs(left, right))
        strips.append(jnp.concatenate(pieces, axis=0))
    return jnp.concatenate(strips, axis=1).astype(narrow)


def merge_kernel(
    own_ref, other_ref, w_own_ref, w_other_ref, x_ref, gain_ref, attended_ref, hidden_ref, normed_ref
):
    groups = 2
    mine = heads_to_rows(own_ref, groups)
    attended_ref[...] = mine
    theirs = heads_to_rows(other_ref, groups)
    branch = dot_wide(mine, w_own_ref[...]).astype(narrow).astype(wide)
    branch = branch + dot_wide(theirs, w_other_ref[...]).astype(narrow).astype(wide)
    hidden = x_ref[...].astype(wide) + branch
    hidden_ref[...] = hidden
    normed_ref[...] = (hidden * rms_scale(hidden) * gain_ref[...].astype(wide)).astype(narrow)


def merge(own, other, w_own, w_other, inputs, norm_ffn):
    tokens, width = inputs.shape
    local = w_own.shape[0]
    return pl.pallas_call(
        merge_kernel,
        in_specs=[whole_spec()] * 6,
        out_specs=[whole_spec()] * 3,
        out_shape=[
            jax.ShapeDtypeStruct((tokens, local), narrow),
            jax.ShapeDtypeStruct((tokens, width), wide),
            jax.ShapeDtypeStruct((tokens, width), narrow),
        ],
        compiler_params=pltpu.CompilerParams(vmem_limit_bytes=vmem_bytes),
        cost_estimate=busy(6),
        name="merge",
    )(own, other, w_own, w_other, inputs, norm_ffn.reshape(1, width))


def branch_back_kernel(
    own_ref, other_ref, hidden_ref, cot_ref, gain_ref, w_ref, send_ref, hidden_grad_ref, branch_ref, gain_grad_ref
):
    groups = 2
    grad_normed = own_ref[...].astype(wide) + other_ref[...].astype(wide)
    hidden = hidden_ref[...]
    back, gain_grad = norm_back(grad_normed, hidden, rms_scale(hidden), gain_ref[...].astype(wide))
    gain_grad_ref[...] = gain_grad[None]
    grad_hidden = cot_ref[...].astype(wide) + back
    hidden_grad_ref[...] = grad_hidden
    grad_branch = grad_hidden.astype(narrow)
    branch_ref[...] = grad_branch
    attended_grad = dot_rows(grad_branch, w_ref[...])
    tokens, local = attended_grad.shape
    half = tokens // groups // 2
    for pair in range(local // LANES):
        for part in range(groups):
            cols = slice(pair * LANES, (pair + 1) * LANES)
            low = attended_grad[2 * part * half : (2 * part + 1) * half, cols]
            high = attended_grad[(2 * part + 1) * half : (2 * part + 2) * half, cols]
            for at, tile in enumerate(swap_pairs(low, high)):
                send_ref[2 * pair + at, part] = tile.astype(narrow)


def branch_back(own, other, hidden, cotangent, norm_ffn, w_out):
    tokens, width = hidden.shape
    local = w_out.shape[0]
    groups = 2
    return pl.pallas_call(
        branch_back_kernel,
        in_specs=[whole_spec()] * 6,
        out_specs=[whole_spec()] * 4,
        out_shape=[
            jax.ShapeDtypeStruct((local // HEAD_DIM, groups, tokens // groups // 2, LANES), narrow),
            jax.ShapeDtypeStruct((tokens, width), wide),
            jax.ShapeDtypeStruct((tokens, width), narrow),
            jax.ShapeDtypeStruct((1, width), wide),
        ],
        compiler_params=pltpu.CompilerParams(vmem_limit_bytes=vmem_bytes),
        cost_estimate=busy(6),
        name="branch_back",
    )(own, other, hidden, cotangent, norm_ffn.reshape(1, width), w_out)


def fold_kernel(
    mine_ref, arrived_ref, dq_ref, cos_ref, sin_ref, slot_cos_ref, slot_sin_ref, send_ref, feats_ref
):
    count, rows, _ = mine_ref.shape
    half = rows // 2
    low = lane_ids((rows, LANES)) < HEAD_DIM

    def step(slot, carry):
        turn_cos = slot_cos_ref[slot][:1]
        turn_sin = slot_sin_ref[slot][:1]
        cosine = cos_ref[...] * turn_cos - sin_ref[...] * turn_sin
        sine = -(sin_ref[...] * turn_cos + cos_ref[...] * turn_sin)
        pair = mine_ref[slot] + arrived_ref[slot].astype(wide)
        key = spin(pair, cosine, sine)
        send_ref[slot, :rows, :] = jnp.where(low, key, pair).astype(narrow)
        feats_ref[slot, :, :LANES] = jnp.where(low, key, 0.5 * pair.astype(narrow).astype(wide)).astype(narrow)
        packed = dq_ref[slot].astype(wide)
        query = jnp.concatenate([packed, pltpu.roll(packed, HEAD_DIM, 1)], axis=0)
        query = jnp.where(low, spin(query, cosine, sine), 0.0)
        feats_ref[slot, :, LANES:] = query.astype(narrow)
        top = query[:half]
        bottom = pltpu.roll(query[half:], HEAD_DIM, 1)
        send_ref[slot, rows:, :] = jnp.where(low[:half], top, bottom).astype(narrow)
        return carry

    lax.fori_loop(0, count, step, 0)


def fold(mine, arrived, grad_q, cosine, sine, slot_cos, slot_sin):
    count, rows, _ = mine.shape
    return pl.pallas_call(
        fold_kernel,
        in_specs=[whole_spec()] * 7,
        out_specs=[whole_spec()] * 2,
        out_shape=[
            jax.ShapeDtypeStruct((count, rows + rows // 2, LANES), narrow),
            jax.ShapeDtypeStruct((count, rows, 2 * LANES), narrow),
        ],
        compiler_params=pltpu.CompilerParams(vmem_limit_bytes=vmem_bytes),
        cost_estimate=busy(9),
        name="fold",
    )(mine, arrived, grad_q, cosine, sine, slot_cos, slot_sin)


def unproject_kernel(recv_ref, wq_ref, wk_ref, wv_ref, first_ref, part_ref):
    groups = 2
    rows = recv_ref.shape[1] * 2 // 3
    heads = recv_ref.shape[0] // groups
    for part in range(groups):
        span = slice(part * rows, (part + 1) * rows)
        keys, values, queries = [], [], []
        for pair in range(heads // 2):
            cols = slice(pair * LANES, (pair + 1) * LANES)
            left = recv_ref[2 * pair * groups + part].astype(wide)
            right = recv_ref[(2 * pair + 1) * groups + part].astype(wide)
            key, value = swap_pairs(left[:rows], right[:rows])
            query = jnp.concatenate(swap_pairs(left[rows:], right[rows:]), axis=0)
            value = 0.5 * value
            first_ref[span, cols] = value
            keys.append(key.astype(narrow))
            values.append(value.astype(narrow))
            queries.append(query.astype(narrow))
        total = dot_rows(jnp.concatenate(queries, axis=1), wq_ref[...])
        total = total + dot_rows(jnp.concatenate(keys, axis=1), wk_ref[...])
        total = total + dot_rows(jnp.concatenate(values, axis=1), wv_ref[...])
        part_ref[span, :] = total.astype(narrow)


def unproject(recv, w_query, w_key, w_value):
    width, local = w_query.shape
    tokens = recv.shape[1] * 4 // 3
    return pl.pallas_call(
        unproject_kernel,
        in_specs=[whole_spec()] * 4,
        out_specs=[whole_spec()] * 2,
        out_shape=[
            jax.ShapeDtypeStruct((tokens, local), wide),
            jax.ShapeDtypeStruct((tokens, width), narrow),
        ],
        compiler_params=pltpu.CompilerParams(vmem_limit_bytes=vmem_bytes),
        cost_estimate=busy(6),
        name="unproject",
    )(recv, w_query, w_key, w_value)


def finish_kernel(part_ref, own_ref, other_ref, query_ref, key_ref, value_ref, out_ref):
    chips, size, width = own_ref.shape
    part = part_ref[0]
    head_rows = 3 * HEAD_DIM // 2
    out_rows = size - head_rows

    def emit(first, second):
        for chip in range(chips):
            at = chip * out_rows
            out_ref[at : at + out_rows, :] = first[chip, head_rows:, :].astype(wide)
            at += chips * out_rows
            out_ref[at : at + out_rows, :] = second[chip, head_rows:, :].astype(wide)

        def column(block, carry):
            cols = pl.ds(pl.multiple_of(block * LANES, LANES), LANES)
            for pair in range(chips // 2):
                pieces = [
                    jnp.concatenate(
                        [first[chip, :head_rows, cols], second[chip, :head_rows, cols]], axis=0
                    ).astype(wide)
                    for chip in (2 * pair, 2 * pair + 1)
                ]
                for at, target in enumerate((key_ref, value_ref, query_ref)):
                    span = slice(at * HEAD_DIM, (at + 1) * HEAD_DIM)
                    both = jnp.concatenate([piece[span] for piece in pieces], axis=0)
                    target[cols, pair * LANES : (pair + 1) * LANES] = jnp.transpose(both)
            return carry

        lax.fori_loop(0, width // LANES, column, 0)

    @pl.when(part == 0)
    def _():
        emit(own_ref, other_ref)

    @pl.when(part == 1)
    def _():
        emit(other_ref, own_ref)


def finish(part, own, other, local):
    width = own.shape[2]
    return pl.pallas_call(
        finish_kernel,
        in_specs=[scalar_spec()] + [whole_spec()] * 2,
        out_specs=[whole_spec()] * 4,
        out_shape=[jax.ShapeDtypeStruct((width, local), wide)] * 3
        + [jax.ShapeDtypeStruct((local, width), wide)],
        compiler_params=pltpu.CompilerParams(vmem_limit_bytes=vmem_bytes),
        cost_estimate=busy(6),
        name="finish",
    )(part, own, other)


def swap_tensor(values):
    return lax.ppermute(values, "tensor", [(0, 1), (1, 0)])


def swap_bit(values, bit, count):
    return lax.ppermute(values, "dp", [(i, i ^ bit) for i in range(count)])


def add_narrow(left, right):
    return (left.astype(wide) + right.astype(wide)).astype(narrow)


def take_part(values, index, parts):
    size = values.shape[0] // parts
    return lax.dynamic_slice_in_dim(values, index * size, size, 0)


def reduce_bit(values, bit, place, count):
    mine = (place // bit) % 2
    arrived = swap_bit(take_part(values, 1 - mine, 2), bit, count)
    return add_narrow(take_part(values, mine, 2), arrived)


def side_groups(count):
    return [[chip * 2 + core for chip in range(count // 2)] for core in range(2)]


def to_chips(values, count):
    return lax.all_to_all(
        values, "dp", split_axis=0, concat_axis=0, tiled=True, axis_index_groups=side_groups(count)
    )


def spread(values, count):
    chips = count // 2
    return to_chips(jnp.broadcast_to(values[None], (chips,) + values.shape), count)


def spread_rows(values, before, place, count):
    lines = [[z * 4 + rest for z in range(count // 4)] for rest in range(4)]
    length = count // 4
    along = lax.all_to_all(
        jnp.broadcast_to(values[None], (length,) + values.shape),
        "dp",
        split_axis=0,
        concat_axis=0,
        tiled=True,
        axis_index_groups=lines,
    )
    along = after(along, before)
    arrived = swap_bit(along, 2, count)
    high = (place // 2) % 2 == 1
    pair = jnp.stack([jnp.where(high, arrived, along), jnp.where(high, along, arrived)], axis=1)
    return pair.reshape((2 * length,) + values.shape)


def gather_core(values, axis, place, count):
    mine = place % 2
    arrived = swap_bit(values, 1, count)
    row = jnp.concatenate([arrived, values, arrived], axis=axis)
    size = values.shape[axis]
    return lax.dynamic_slice_in_dim(row, (1 - mine) * size, 2 * size, axis)


def sum_over_dp(values, place, count):
    chips = count // 2
    values = reduce_bit(values, 1, place, count)
    shares = to_chips(values.reshape((chips, values.shape[0] // chips) + values.shape[1:]), count)
    total = jnp.sum(shares.astype(wide), axis=0).astype(narrow)
    whole = spread(total, count)
    whole = whole.reshape((-1,) + whole.shape[2:])
    return gather_core(whole, 0, place, count)


def reduce_z(values, place, count):
    at = place // 4
    total = take_part(values, at, 4).astype(wide)
    for step in (1, 2, 3):
        share = take_part(values, at ^ step, 4)
        total = total + swap_bit(share, 4 * step, count).astype(wide)
    return total.astype(narrow)


def gather_z(values, place, count):
    at = place // 4
    shares = [values] + [swap_bit(values, 4 * step, count) for step in (1, 2, 3)]
    row = jnp.concatenate(shares, axis=0)
    return jnp.concatenate([take_part(row, at ^ target, 4) for target in range(4)], axis=0)


def gather_bit(values, bit, place, count):
    mine = (place // bit) % 2
    arrived = swap_bit(values, bit, count)
    row = jnp.concatenate([arrived, values, arrived], axis=0)
    size = values.shape[0]
    return lax.dynamic_slice_in_dim(row, (1 - mine) * size, 2 * size, 0)


def after(value, *others):
    return lax.optimization_barrier((value,) + others)[0]


def sum_small(values, count):
    bit = 1
    while bit < count:
        values = values + swap_bit(values, bit, count)
        bit *= 2
    return values


def body_heads(
    inputs,
    first_values,
    w_query,
    w_key,
    w_value,
    w_out,
    w_gate,
    w_up,
    w_down,
    norm_attn,
    norm_ffn,
    cotangent,
    parents,
    depth_pos,
    assignment,
):
    count = parents.shape[0]
    tokens, width = inputs.shape
    local = w_query.shape[1]
    heads = local // HEAD_DIM
    groups = count // heads
    place = lax.axis_index("dp")
    part = (place % groups).astype(jnp.int32)
    part_array = part.reshape(1)

    rows = tokens // groups
    half = HEAD_DIM // 2
    w_out_other = swap_tensor(w_out)
    slot_ids = jnp.arange(count, dtype=jnp.int32)
    start = jnp.sum(jnp.where(slot_ids == place, depth_pos, 0))
    lanes = jnp.arange(LANES, dtype=jnp.int32)
    frequency = rope_base ** (-(lanes % half).astype(wide) * 2.0 / HEAD_DIM)
    sign = jnp.where(lanes % HEAD_DIM < half, -1.0, 1.0)[None, :]
    positions = (start + jnp.arange(tokens, dtype=jnp.int32)).astype(wide)
    angles = positions[:, None] * frequency[None, :]
    cosine = jnp.cos(angles)
    sine = jnp.sin(angles) * sign
    part_positions = (part * rows + jnp.arange(rows, dtype=jnp.int32)).astype(wide)
    part_angles = part_positions[:, None] * frequency[None, :]
    part_cos = jnp.cos(part_angles)
    part_sin = jnp.sin(part_angles) * sign
    slot_angles = depth_pos.astype(wide)[:, None] * frequency[None, :]
    slot_shape = (count, 8, LANES)
    slot_cos = jnp.broadcast_to(jnp.cos(slot_angles)[:, None, :], slot_shape)
    slot_sin = jnp.broadcast_to((jnp.sin(slot_angles) * sign)[:, None, :], slot_shape)

    send, normed = project(
        inputs, norm_attn, first_values, cosine, sine, w_query, w_key, w_value, groups
    )
    send = send.reshape(count, rows + rows // 2, LANES)
    recv = lax.all_to_all(send, "dp", split_axis=0, concat_axis=0, tiled=True)
    normed_theirs = swap_bit(take_part(normed, 1 - part, groups), 1, count)
    normed_mine = take_part(normed, part, groups)
    normed_row = jnp.concatenate([normed_theirs, normed_mine, normed_theirs], axis=0)
    normed_chip = lax.dynamic_slice_in_dim(normed_row, (1 - part) * rows, groups * rows, 0)
    side = lax.axis_index("tensor")
    quarter = rows // 2
    normed_quarter = lax.dynamic_index_in_dim(
        normed_chip.reshape(groups, 2, quarter, width), side, 1, keepdims=False
    ).reshape(groups * quarter, width)
    recv, normed_quarter = lax.optimization_barrier((recv, normed_quarter))
    normed_own = lax.all_gather(
        normed_quarter, "dp", axis=0, tiled=True, axis_index_groups=side_groups(count)
    )

    other = swap_bit(recv[:, :rows], 1, count)
    packed, ot, logs = attend(parents, assignment, part_array, recv, other)
    own_out = lax.all_to_all(packed, "dp", split_axis=0, concat_axis=0, tiled=True)
    other_out = swap_tensor(own_out)
    attended, hidden, normed_ffn = merge(own_out, other_out, w_out, w_out_other, inputs, norm_ffn)

    gate_proj = jnp.dot(normed_ffn, w_gate, preferred_element_type=wide)
    up_proj = jnp.dot(normed_ffn, w_up, preferred_element_type=wide)
    silu_gate = jax.nn.silu(gate_proj)
    activated = (silu_gate * up_proj).astype(narrow)
    grad_activated = jnp.einsum("td,fd->tf", cotangent, w_down, preferred_element_type=wide)
    sigmoid_gate = jax.nn.sigmoid(gate_proj)
    grad_gate = (
        grad_activated * up_proj * sigmoid_gate * (1.0 + gate_proj * (1.0 - sigmoid_gate))
    ).astype(narrow)
    grad_up = (grad_activated * silu_gate).astype(narrow)
    ffn_partial = (
        jnp.einsum("tf,df->td", grad_gate, w_gate, preferred_element_type=wide)
        + jnp.einsum("tf,df->td", grad_up, w_up, preferred_element_type=wide)
    ).astype(narrow)
    ffn_other = swap_tensor(ffn_partial)
    ffn_grads = tuple(
        jnp.einsum(form, left, right, preferred_element_type=wide).astype(narrow)
        for form, left, right in (
            ("td,tf->df", normed_ffn, grad_gate),
            ("td,tf->df", normed_ffn, grad_up),
            ("tf,td->fd", activated, cotangent),
        )
    )
    feed_partial = jnp.dot(activated, w_down, preferred_element_type=wide).astype(narrow)

    normed_own, *ffn_grads = lax.optimization_barrier((normed_own,) + ffn_grads)
    ffn_sums = lax.psum(tuple(ffn_grads), "dp")
    ffn_other = after(ffn_other, *ffn_grads)

    def way_back(ffn_other, normed_own):
        grad_send, grad_hidden, grad_branch, grad_gain_ffn = branch_back(
            ffn_partial, ffn_other, hidden, cotangent, norm_ffn, w_out
        )
        grad_recv = lax.all_to_all(
            grad_send.reshape(count, rows // 2, LANES), "dp", split_axis=0, concat_axis=0, tiled=True
        )
        grad_w_out = jnp.einsum("tc,td->cd", attended, grad_branch, preferred_element_type=wide)
        out_half = reduce_bit(grad_w_out.astype(narrow), 1, place, count)
        grad_recv, out_half = lax.optimization_barrier((grad_recv, out_half))
        chips = count // 2
        out_shares = to_chips(out_half.reshape(chips, local // count, width), count)
        out_share = jnp.sum(out_shares.astype(wide), axis=0).astype(narrow)
        normed_other = swap_tensor(normed_own)
        feed_other = swap_tensor(after(feed_partial, normed_other))

        grad_q, mine, theirs = attend_back(
            parents, assignment, part_array, recv, other, grad_recv, ot, logs
        )
        arrived = swap_bit(theirs, 1, count)
        back_send, feats = fold(
            mine, arrived, grad_q, part_cos, part_sin, slot_cos, slot_sin
        )
        back_recv = lax.all_to_all(back_send, "dp", split_axis=0, concat_axis=0, tiled=True)
        feats = feats.reshape(count, 2, quarter, 2 * LANES)
        head_grads = sum(
            jnp.einsum(
                "tc,td->cd",
                lax.dynamic_index_in_dim(feats, at, 1, keepdims=False).reshape(-1, 2 * LANES),
                normed_part,
                preferred_element_type=wide,
            )
            for at, normed_part in ((side, normed_own), (1 - side, normed_other))
        )
        head_grads = head_grads[: 3 * HEAD_DIM].astype(narrow)
        head_share = reduce_bit(head_grads, 1, place, count)
        share = jnp.concatenate([head_share, out_share], axis=0)
        back_recv, feed_other = lax.optimization_barrier((back_recv, feed_other))
        grad_first, attn_partial = unproject(back_recv, w_query, w_key, w_value)
        attn_other = swap_tensor(attn_partial)
        spread_all = spread_rows(after(share, attn_partial), attn_other, place, count)
        spread_other = swap_bit(spread_all, 1, count)

        output = (hidden + (feed_partial.astype(wide) + feed_other.astype(wide))).astype(narrow)
        inputs_wide = inputs.astype(wide)
        grad_normed = attn_partial.astype(wide) + attn_other.astype(wide)
        grad_input_norm, grad_gain_attn = norm_back(
            grad_normed, inputs_wide, rms_scale(inputs_wide), norm_attn.astype(wide)
        )
        grad_inputs = grad_hidden + grad_input_norm
        gains = sum_small(jnp.stack([grad_gain_attn, grad_gain_ffn[0]]), count)
        head_grads = finish(part_array, spread_all, spread_other, local)
        return (output, grad_inputs, grad_first, gains) + tuple(head_grads)

    def no_tree(*operands):
        shapes = jax.eval_shape(way_back, *operands)
        return tuple(jnp.zeros(leaf.shape, leaf.dtype) for leaf in shapes)

    output, grad_inputs, grad_first, gains, *head_grads = lax.cond(
        parents[0] < 0, way_back, no_tree, ffn_other, normed_own
    )
    head_query, head_key, head_value, sum_w_out = head_grads
    ffn_sums = [after(term, gains) for term in ffn_sums]
    return (
        output,
        grad_inputs,
        grad_first,
        head_query,
        head_key,
        head_value,
        sum_w_out,
        ffn_sums[0].astype(wide),
        ffn_sums[1].astype(wide),
        ffn_sums[2].astype(wide),
        gains[0],
        gains[1],
    )


def pick_body(mesh):
    if mesh.shape["dp"] == 16 and mesh.shape["tensor"] == 2:
        return body_heads
    return body_general


def solution(mesh):
    placed = (
        P("dp", None),
        P("dp", "tensor"),
        P(None, "tensor"),
        P(None, "tensor"),
        P(None, "tensor"),
        P("tensor", None),
        P(None, "tensor"),
        P(None, "tensor"),
        P("tensor", None),
        P(),
        P(),
        P("dp", None),
        P(),
        P(),
        P(),
    )
    return jax.shard_map(
        pick_body(mesh),
        mesh=mesh,
        in_specs=placed,
        out_specs=(
            P("dp", None),
            P("dp", None),
            P("dp", "tensor"),
            P(None, "tensor"),
            P(None, "tensor"),
            P(None, "tensor"),
            P("tensor", None),
            P(None, "tensor"),
            P(None, "tensor"),
            P("tensor", None),
            P(),
            P(),
        ),
        check_vma=False,
    )
```

```python
import jax
import jax.numpy as jnp
from jax import lax
from jax.experimental import pallas as pl
from jax.experimental.pallas import tpu as pltpu
from jax.sharding import PartitionSpec as P

HEAD_DIM = 64
SEG = 512


epsilon = 1e-06
rope_base = 10000.0
climb_steps = 5
masked_score = -1e30


def rms_scale(values):
    return lax.rsqrt(jnp.mean(values * values, axis=-1, keepdims=True) + epsilon)


def rotary_tables(positions, head_dim):
    half_dim = head_dim // 2
    frequency = rope_base ** (-jnp.arange(half_dim, dtype=jnp.float32) * 2.0 / head_dim)
    angles = positions.astype(jnp.float32)[:, None] * frequency[None, :]
    return (jnp.cos(angles)[:, None, :], jnp.sin(angles)[:, None, :])


def rotate(values, cosine, sine_table):
    half_dim = values.shape[-1] // 2
    first_half = values[..., :half_dim]
    second_half = values[..., half_dim:]
    return jnp.concatenate(
        [
            first_half * cosine - second_half * sine_table,
            second_half * cosine + first_half * sine_table,
        ],
        axis=-1,
    )


def rotate_back(gradient, cosine, sine_table):
    half_dim = gradient.shape[-1] // 2
    first_half = gradient[..., :half_dim]
    second_half = gradient[..., half_dim:]
    return jnp.concatenate(
        [
            first_half * cosine + second_half * sine_table,
            second_half * cosine - first_half * sine_table,
        ],
        axis=-1,
    )


def parent_slots(parents, assignment):
    count = parents.shape[0]
    slot_ids = jnp.arange(count, dtype=jnp.int32)
    at_slot = assignment[None, :] == slot_ids[:, None]
    parent_seg = jnp.sum(jnp.where(at_slot, parents[None, :], 0), axis=1)
    parent_match = slot_ids[None, :] == parent_seg[:, None]
    above_slot = jnp.sum(jnp.where(parent_match, assignment[None, :], 0), axis=1)
    return jnp.where(parent_seg >= 0, above_slot, -1)


def climb(parent_slot, start_slots):
    slot_ids = jnp.arange(parent_slot.shape[0], dtype=jnp.int32)
    levels = [start_slots]
    current = start_slots
    for step_index in range(climb_steps):
        matched = current[:, None] == slot_ids[None, :]
        upward = jnp.sum(jnp.where(matched, parent_slot[None, :], 0), axis=1)
        current = jnp.where(current >= 0, upward, -1)
        levels.append(current)
    return jnp.stack(levels, axis=1)


def norm_back(grad_normed, values, row_scale, gain_vector):
    scaled_grad = grad_normed * gain_vector
    grad_gain = jnp.sum(grad_normed * values * row_scale, axis=0)
    grad_values = row_scale * (
        scaled_grad
        - values * row_scale * row_scale * jnp.mean(scaled_grad * values, axis=-1, keepdims=True)
    )
    return (grad_values, grad_gain)


def path_rows(source, path_row):
    parts = []
    for level_index in range(climb_steps + 1):
        row_begin = (jnp.maximum(path_row[level_index], 0) * SEG).astype(jnp.int32)
        parts.append(lax.dynamic_slice_in_dim(source, row_begin, SEG, 0))
    return jnp.concatenate(parts, axis=0)


def path_permit(path_row, causal):
    parts = [causal]
    for level_index in range(1, climb_steps + 1):
        parts.append(jnp.broadcast_to(path_row[level_index] >= 0, (SEG, SEG)))
    return jnp.concatenate(parts, axis=1)


def body_general(
    inputs,
    first_values,
    w_query,
    w_key,
    w_value,
    w_out,
    w_gate,
    w_up,
    w_down,
    norm_attn,
    norm_ffn,
    cotangent,
    parents,
    depth_pos,
    assignment,
):
    row_count = inputs.shape[0]
    local_width = w_query.shape[1]
    head_count = local_width // HEAD_DIM
    score_scale = HEAD_DIM ** (-0.5)
    seg_count = row_count // SEG
    slot_total = parents.shape[0]
    slot_ids = jnp.arange(slot_total, dtype=jnp.int32)
    local_rows = jnp.arange(row_count, dtype=jnp.int32)
    own_slots = lax.axis_index("dp") * seg_count + jnp.arange(seg_count, dtype=jnp.int32)
    own_slot_rows = jnp.repeat(own_slots, SEG)
    depth_rows = jnp.sum(
        jnp.where(own_slot_rows[:, None] == slot_ids[None, :], depth_pos[None, :], 0), axis=1
    )
    positions = depth_rows + local_rows % SEG
    parent_slot = parent_slots(parents, assignment)
    own_paths = climb(parent_slot, own_slots)
    offsets = jnp.arange(SEG, dtype=jnp.int32)
    causal = offsets[None, :] <= offsets[:, None]
    cosine, sine_table = rotary_tables(positions, HEAD_DIM)
    inputs_wide = inputs.astype(jnp.float32)
    attn_scale = rms_scale(inputs_wide)
    gain_attn = norm_attn.astype(jnp.float32)
    normed = (inputs_wide * attn_scale * gain_attn).astype(jnp.bfloat16)
    query_proj = jnp.dot(normed, w_query, preferred_element_type=jnp.float32)
    key_proj = jnp.dot(normed, w_key, preferred_element_type=jnp.float32)
    value_proj = jnp.dot(normed, w_value, preferred_element_type=jnp.float32)
    query_rot = rotate(
        query_proj.reshape(row_count, head_count, HEAD_DIM), cosine, sine_table
    ).astype(jnp.bfloat16)
    key_rot = (
        rotate(key_proj.reshape(row_count, head_count, HEAD_DIM), cosine, sine_table)
        .astype(jnp.bfloat16)
        .reshape(row_count, local_width)
    )
    mixed = (0.5 * value_proj + 0.5 * first_values.astype(jnp.float32)).astype(jnp.bfloat16)
    key_all, value_all = (
        lax.all_gather(key_rot, "dp", axis=0, tiled=True),
        lax.all_gather(mixed, "dp", axis=0, tiled=True),
    )
    query_segs = query_rot.reshape(seg_count, SEG, head_count, HEAD_DIM)

    def segment_forward(operand):
        query_block, path_row = operand
        near_keys = path_rows(key_all, path_row).reshape(-1, head_count, HEAD_DIM)
        near_values = path_rows(value_all, path_row).reshape(-1, head_count, HEAD_DIM)
        permit = path_permit(path_row, causal)
        scores = (
            jnp.einsum("qhd,khd->hqk", query_block, near_keys, preferred_element_type=jnp.float32)
            * score_scale
        )
        scores = jnp.where(permit[None], scores, masked_score)
        row_max = jnp.max(scores, axis=-1)
        weights = jnp.where(permit[None], jnp.exp(scores - row_max[..., None]), 0.0)
        row_total = jnp.sum(weights, axis=-1)
        attn_probs = weights / row_total[..., None]
        block_out = jnp.einsum(
            "hqk,khd->qhd",
            attn_probs.astype(jnp.bfloat16),
            near_values,
            preferred_element_type=jnp.float32,
        )
        return (block_out, row_max + jnp.log(row_total))

    attn_parts, log_parts = lax.map(segment_forward, (query_segs, own_paths))
    attn_exact = attn_parts.reshape(row_count, head_count, HEAD_DIM)
    attended = attn_exact.reshape(row_count, local_width).astype(jnp.bfloat16)
    branch_attn = lax.psum(
        jnp.dot(attended, w_out, preferred_element_type=jnp.float32).astype(jnp.bfloat16), "tensor"
    ).astype(jnp.float32)
    hidden_state = inputs_wide + branch_attn
    ffn_scale = rms_scale(hidden_state)
    gain_ffn = norm_ffn.astype(jnp.float32)
    normed_ffn = (hidden_state * ffn_scale * gain_ffn).astype(jnp.bfloat16)
    gate_proj = jnp.dot(normed_ffn, w_gate, preferred_element_type=jnp.float32)
    up_proj = jnp.dot(normed_ffn, w_up, preferred_element_type=jnp.float32)
    silu_gate = jax.nn.silu(gate_proj)
    activated = (silu_gate * up_proj).astype(jnp.bfloat16)
    feed = lax.psum(
        jnp.dot(activated, w_down, preferred_element_type=jnp.float32).astype(jnp.bfloat16),
        "tensor",
    ).astype(jnp.float32)
    output = (hidden_state + feed).astype(jnp.bfloat16)
    grad_w_down = jnp.einsum("tf,td->fd", activated, cotangent, preferred_element_type=jnp.float32)
    grad_activated = jnp.einsum("td,fd->tf", cotangent, w_down, preferred_element_type=jnp.float32)
    sigmoid_gate = jax.nn.sigmoid(gate_proj)
    grad_gate = (
        grad_activated * up_proj * sigmoid_gate * (1.0 + gate_proj * (1.0 - sigmoid_gate))
    ).astype(jnp.bfloat16)
    grad_up = (grad_activated * silu_gate).astype(jnp.bfloat16)
    grad_w_gate = jnp.einsum("td,tf->df", normed_ffn, grad_gate, preferred_element_type=jnp.float32)
    grad_w_up = jnp.einsum("td,tf->df", normed_ffn, grad_up, preferred_element_type=jnp.float32)
    ffn_partial = jnp.einsum(
        "tf,df->td", grad_gate, w_gate, preferred_element_type=jnp.float32
    ) + jnp.einsum("tf,df->td", grad_up, w_up, preferred_element_type=jnp.float32)
    grad_normed_ffn = lax.psum(ffn_partial.astype(jnp.bfloat16), "tensor").astype(jnp.float32)
    grad_hidden_norm, grad_gain_ffn = norm_back(grad_normed_ffn, hidden_state, ffn_scale, gain_ffn)
    grad_hidden = cotangent.astype(jnp.float32) + grad_hidden_norm
    grad_branch = grad_hidden.astype(jnp.bfloat16)
    grad_w_out = jnp.einsum("tc,td->cd", attended, grad_branch, preferred_element_type=jnp.float32)
    grad_attended = jnp.einsum(
        "td,cd->tc", grad_branch, w_out, preferred_element_type=jnp.float32
    ).astype(jnp.bfloat16)
    grad_heads = grad_attended.reshape(row_count, head_count, HEAD_DIM)
    delta_rows = jnp.sum(grad_heads.astype(jnp.float32) * attn_exact, axis=-1)
    delta_parts = jnp.transpose(delta_rows.reshape(seg_count, SEG, head_count), (0, 2, 1))
    grad_segs = grad_heads.reshape(seg_count, SEG, head_count, HEAD_DIM)
    key_back, value_back = (key_all, value_all)

    def segment_back(query_block, grad_block, path_row, log_block, delta_block):
        near_keys = path_rows(key_back, path_row).reshape(-1, head_count, HEAD_DIM)
        near_values = path_rows(value_back, path_row).reshape(-1, head_count, HEAD_DIM)
        permit = path_permit(path_row, causal)
        scores = (
            jnp.einsum("qhd,khd->hqk", query_block, near_keys, preferred_element_type=jnp.float32)
            * score_scale
        )
        scores = jnp.where(permit[None], scores, masked_score)
        attn_probs = jnp.where(permit[None], jnp.exp(scores - log_block[..., None]), 0.0)
        grad_probs = jnp.einsum(
            "qhd,khd->hqk", grad_block, near_values, preferred_element_type=jnp.float32
        )
        grad_scores = (attn_probs * (grad_probs - delta_block[..., None])).astype(jnp.bfloat16)
        grad_part = (
            jnp.einsum("hqk,khd->qhd", grad_scores, near_keys, preferred_element_type=jnp.float32)
            * score_scale
        )
        return (attn_probs, grad_scores, grad_part)

    zero_rows = jnp.zeros((key_back.shape[0], local_width), jnp.float32)

    def scatter_step(fold_state, operand):
        key_acc, value_acc = fold_state
        query_block, grad_block, path_row, log_block, delta_block = operand
        attn_probs, grad_scores, grad_part = segment_back(
            query_block, grad_block, path_row, log_block, delta_block
        )
        key_term = (
            jnp.einsum("hqk,qhd->khd", grad_scores, query_block, preferred_element_type=jnp.float32)
            * score_scale
        ).reshape(climb_steps + 1, SEG, local_width)
        value_term = jnp.einsum(
            "hqk,qhd->khd",
            attn_probs.astype(jnp.bfloat16),
            grad_block,
            preferred_element_type=jnp.float32,
        ).reshape(climb_steps + 1, SEG, local_width)
        for level_index in range(climb_steps + 1):
            row_begin = (jnp.maximum(path_row[level_index], 0) * SEG).astype(jnp.int32)
            key_acc = lax.dynamic_update_slice_in_dim(
                key_acc,
                lax.dynamic_slice_in_dim(key_acc, row_begin, SEG, 0) + key_term[level_index],
                row_begin,
                0,
            )
            value_acc = lax.dynamic_update_slice_in_dim(
                value_acc,
                lax.dynamic_slice_in_dim(value_acc, row_begin, SEG, 0) + value_term[level_index],
                row_begin,
                0,
            )
        return ((key_acc, value_acc), grad_part)

    (key_terms, value_terms), grad_parts = lax.scan(
        scatter_step,
        (zero_rows, zero_rows),
        (query_segs, grad_segs, own_paths, log_parts, delta_parts),
    )
    grad_query_rot = grad_parts.reshape(row_count, head_count, HEAD_DIM)
    key_sums, value_sums = (
        lax.psum_scatter(
            key_terms.astype(jnp.bfloat16), "dp", scatter_dimension=0, tiled=True
        ).astype(jnp.float32),
        lax.psum_scatter(
            value_terms.astype(jnp.bfloat16), "dp", scatter_dimension=0, tiled=True
        ).astype(jnp.float32),
    )
    grad_key_rot = key_sums.reshape(row_count, head_count, HEAD_DIM)
    grad_first_values = 0.5 * value_sums
    grad_value = (0.5 * value_sums).astype(jnp.bfloat16)
    grad_key = (
        rotate_back(grad_key_rot, cosine, sine_table)
        .reshape(row_count, local_width)
        .astype(jnp.bfloat16)
    )
    grad_query = (
        rotate_back(grad_query_rot, cosine, sine_table)
        .reshape(row_count, local_width)
        .astype(jnp.bfloat16)
    )
    grad_w_query = jnp.einsum("td,tc->dc", normed, grad_query, preferred_element_type=jnp.float32)
    grad_w_key = jnp.einsum("td,tc->dc", normed, grad_key, preferred_element_type=jnp.float32)
    grad_w_value = jnp.einsum("td,tc->dc", normed, grad_value, preferred_element_type=jnp.float32)
    attn_partial = (
        jnp.einsum("tc,dc->td", grad_query, w_query, preferred_element_type=jnp.float32)
        + jnp.einsum("tc,dc->td", grad_key, w_key, preferred_element_type=jnp.float32)
        + jnp.einsum("tc,dc->td", grad_value, w_value, preferred_element_type=jnp.float32)
    )
    grad_normed = lax.psum(attn_partial.astype(jnp.bfloat16), "tensor").astype(jnp.float32)
    grad_input_norm, grad_gain_attn = norm_back(grad_normed, inputs_wide, attn_scale, gain_attn)
    grad_inputs = grad_hidden + grad_input_norm
    summed = (
        lax.psum(grad_w_query.astype(jnp.bfloat16), "dp").astype(jnp.float32),
        lax.psum(grad_w_key.astype(jnp.bfloat16), "dp").astype(jnp.float32),
        lax.psum(grad_w_value.astype(jnp.bfloat16), "dp").astype(jnp.float32),
        lax.psum(grad_w_out.astype(jnp.bfloat16), "dp").astype(jnp.float32),
        lax.psum(grad_w_gate.astype(jnp.bfloat16), "dp").astype(jnp.float32),
        lax.psum(grad_w_up.astype(jnp.bfloat16), "dp").astype(jnp.float32),
        lax.psum(grad_w_down.astype(jnp.bfloat16), "dp").astype(jnp.float32),
        lax.psum(grad_gain_attn.astype(jnp.bfloat16), "dp").astype(jnp.float32),
        lax.psum(grad_gain_ffn.astype(jnp.bfloat16), "dp").astype(jnp.float32),
    )
    return (
        output,
        grad_inputs,
        grad_first_values,
        summed[0],
        summed[1],
        summed[2],
        summed[3],
        summed[4],
        summed[5],
        summed[6],
        summed[7],
        summed[8],
    )


TREE = 16
TREE_DEPTHS = (0, 1, 2, 3, 4, 4, 4, 4, 5, 5, 5, 5, 5, 5, 5, 5)
LANES = 128
wide = jnp.float32
narrow = jnp.bfloat16
vmem_bytes = 60 * 1024 * 1024
safe_excess = 40.0


def busy(microseconds):
    return pl.CostEstimate(
        flops=int(microseconds * 1e9), bytes_accessed=int(microseconds * 2e6), transcendentals=0
    )


def lane_ids(shape):
    return lax.broadcasted_iota(jnp.int32, shape, len(shape) - 1)


def swap_pairs(left, right):
    low = lane_ids(left.shape) < HEAD_DIM
    first = jnp.where(low, left, pltpu.roll(right, HEAD_DIM, 1))
    second = jnp.where(low, pltpu.roll(left, HEAD_DIM, 1), right)
    return first, second


def spin(values, cosine, signed_sine):
    half = HEAD_DIM // 2
    ahead = pltpu.roll(values, LANES - half, 1)
    behind = pltpu.roll(values, half, 1)
    other = jnp.where(lane_ids(values.shape) % HEAD_DIM < half, ahead, behind)
    return values * cosine + other * signed_sine


def dot_wide(left, right):
    return jnp.dot(left, right, preferred_element_type=wide)


def dot_rows(left, right):
    return lax.dot_general(left, right, (((1,), (1,)), ((), ())), preferred_element_type=wide)


def whole_spec():
    return pl.BlockSpec(memory_space=pltpu.VMEM)


def scalar_spec():
    return pl.BlockSpec(memory_space=pltpu.SMEM)


def project_kernel(
    x_ref, gain_ref, first_ref, cos_ref, sin_ref, wq_ref, wk_ref, wv_ref, send_ref, normed_ref
):
    rows = x_ref.shape[0]
    pairs = first_ref.shape[1] // LANES
    x = x_ref[...].astype(wide)
    normed = (x * rms_scale(x) * gain_ref[...].astype(wide)).astype(narrow)
    normed_ref[...] = normed
    query = dot_wide(normed, wq_ref[...]) * (HEAD_DIM ** (-0.5))
    key = dot_wide(normed, wk_ref[...])
    value = dot_wide(normed, wv_ref[...])
    mixed = 0.5 * value + 0.5 * first_ref[...].astype(wide)
    cosine = cos_ref[...]
    sine = sin_ref[...]
    for pair in range(pairs):
        cols = slice(pair * LANES, (pair + 1) * LANES)
        q = spin(query[:, cols], cosine, sine)
        k = spin(key[:, cols], cosine, sine)
        for at, tile in enumerate(swap_pairs(k, mixed[:, cols])):
            send_ref[2 * pair + at, 0, :rows, :] = tile.astype(narrow)
        for at, tile in enumerate(swap_pairs(q[: rows // 2], q[rows // 2 :])):
            send_ref[2 * pair + at, 0, rows:, :] = tile.astype(narrow)


def project(inputs, norm_attn, first_values, cosine, sine, w_query, w_key, w_value, groups):
    rows, width = inputs.shape
    local = w_query.shape[1]
    part = rows // groups
    heads = local // HEAD_DIM
    fixed = lambda step: (0, 0)
    moving = lambda step: (step, 0)
    return pl.pallas_call(
        project_kernel,
        grid=(groups,),
        in_specs=[
            pl.BlockSpec((part, width), moving),
            pl.BlockSpec((1, width), fixed),
            pl.BlockSpec((part, local), moving),
            pl.BlockSpec((part, LANES), moving),
            pl.BlockSpec((part, LANES), moving),
            pl.BlockSpec((width, local), fixed),
            pl.BlockSpec((width, local), fixed),
            pl.BlockSpec((width, local), fixed),
        ],
        out_specs=[
            pl.BlockSpec((heads, 1, part + part // 2, LANES), lambda step: (0, step, 0, 0)),
            pl.BlockSpec((part, width), moving),
        ],
        out_shape=[
            jax.ShapeDtypeStruct((heads, groups, part + part // 2, LANES), narrow),
            jax.ShapeDtypeStruct((rows, width), narrow),
        ],
        compiler_params=pltpu.CompilerParams(vmem_limit_bytes=vmem_bytes),
        cost_estimate=busy(6),
        name="project",
    )(inputs, norm_attn.reshape(1, width), first_values, cosine, sine, w_query, w_key, w_value)


def tree_walk(run, count, unroll):
    for base in range(0, count, TREE):
        at = 0
        while at < TREE:
            same = 1
            while at + same < TREE and TREE_DEPTHS[at + same] == TREE_DEPTHS[at]:
                same += 1
            depth = TREE_DEPTHS[at]
            if same == 1:
                run(base + at, depth)
            else:
                def step(i, carry, start=base + at, depth=depth):
                    run(start + i, depth)
                    return carry

                lax.fori_loop(0, same, step, 0, unroll=unroll)
            at += same


def path_of(parents_ref, assign_ref, segment, depth):
    slots = [assign_ref[segment]]
    current = segment
    for _ in range(depth):
        current = parents_ref[current]
        slots.append(assign_ref[current])
    return slots


def unpack_low(packed):
    values = packed.astype(wide)
    low = lane_ids(values.shape) < HEAD_DIM
    top = jnp.where(low, values, 0.0)
    bottom = jnp.where(low, pltpu.roll(values, HEAD_DIM, 1), 0.0)
    return jnp.concatenate([top, bottom], axis=0).astype(narrow)


def unpack_high(packed):
    values = packed.astype(wide)
    high = lane_ids(values.shape) >= HEAD_DIM
    top = jnp.where(high, pltpu.roll(values, HEAD_DIM, 1), 0.0)
    bottom = jnp.where(high, values, 0.0)
    return jnp.concatenate([top, bottom], axis=0).astype(narrow)


def pack_columns(transposed):
    half = transposed.shape[1] // 2
    stacked = jnp.concatenate([transposed[:, :half], transposed[:, half:]], axis=0)
    return jnp.transpose(stacked)


def gather_parts(part, recv_ref, other_ref, kv_ref, kvt_ref, lanes):
    rows = other_ref.shape[1]

    def fill(slot, carry):
        kv_ref[slot, pl.ds(pl.multiple_of(part * rows, rows), rows), :] = recv_ref[slot, :rows, :]
        kv_ref[slot, pl.ds(pl.multiple_of((1 - part) * rows, rows), rows), :] = other_ref[slot]
        flipped = jnp.transpose(kv_ref[slot].astype(wide))
        kvt_ref[slot] = flipped[lanes].astype(narrow)
        return carry

    lax.fori_loop(0, recv_ref.shape[0], fill, 0)


def visible(part, keys, rows):
    key_row = lax.broadcasted_iota(jnp.int32, (keys, rows), 0)
    query_row = lax.broadcasted_iota(jnp.int32, (keys, rows), 1) + part * rows
    return key_row <= query_row


def fold_rows(values, combine):
    blocks = values.reshape(values.shape[0] // 8, 8, values.shape[1])
    return combine(blocks, axis=0)


def attend_kernel(
    parents_ref,
    assign_ref,
    part_ref,
    recv_ref,
    other_ref,
    send_ref,
    ot_ref,
    log_ref,
    kv_ref,
    vt_ref,
    excess_ref,
):
    part = part_ref[0]
    rows = other_ref.shape[1]
    count = recv_ref.shape[0]
    gather_parts(part, recv_ref, other_ref, kv_ref, vt_ref, slice(HEAD_DIM, LANES))
    excess_ref[...] = jnp.zeros_like(excess_ref)

    def own_scores(own, query):
        block = dot_rows(kv_ref[own], query)
        return jnp.where(visible(part, SEG, rows), block, masked_score)

    def store(own, peak, total, mixed):
        mixed = mixed / total
        ot_ref[own] = mixed
        log_ref[own] = jnp.broadcast_to(peak + jnp.log(total), (8, rows))
        send_ref[own] = pack_columns(mixed).astype(narrow)

    def run(segment, depth):
        slots = path_of(parents_ref, assign_ref, segment, depth)
        own = slots[0]
        query = unpack_low(recv_ref[own, rows:, :])
        block = own_scores(own, query)
        peak = jnp.max(block, axis=0, keepdims=True)
        weight = jnp.exp(block - peak)
        total = fold_rows(weight, jnp.sum)
        mixed = dot_wide(vt_ref[own], weight.astype(narrow))
        crest = jnp.broadcast_to(peak, (8, rows))
        for slot in slots[1:]:
            block = dot_rows(kv_ref[slot], query)
            crest = jnp.maximum(crest, fold_rows(block, jnp.max))
            weight = jnp.exp(block - peak)
            total = total + fold_rows(weight, jnp.sum)
            mixed = mixed + dot_wide(vt_ref[slot], weight.astype(narrow))
        excess_ref[...] = jnp.maximum(excess_ref[...], crest - peak)
        store(own, peak, jnp.sum(total, axis=0, keepdims=True), mixed)

    tree_walk(run, count, 2)

    @pl.when(jnp.max(excess_ref[...]) > safe_excess)
    def _():
        def again(segment, carry):
            own = assign_ref[segment]
            query = unpack_low(recv_ref[own, rows:, :])

            def climb_up(state):
                current, peak, total, mixed = state
                current = parents_ref[current]
                slot = assign_ref[current]
                block = dot_rows(kv_ref[slot], query)
                crest = jnp.maximum(peak, jnp.max(block, axis=0, keepdims=True))
                fade = jnp.exp(peak - crest)
                weight = jnp.exp(block - crest)
                total = total * fade + jnp.sum(weight, axis=0, keepdims=True)
                mixed = mixed * fade + dot_wide(vt_ref[slot], weight.astype(narrow))
                return current, crest, total, mixed

            block = own_scores(own, query)
            peak = jnp.max(block, axis=0, keepdims=True)
            weight = jnp.exp(block - peak)
            total = jnp.sum(weight, axis=0, keepdims=True)
            mixed = dot_wide(vt_ref[own], weight.astype(narrow))
            _, peak, total, mixed = lax.while_loop(
                lambda state: parents_ref[state[0]] >= 0, climb_up, (segment, peak, total, mixed)
            )
            store(own, peak, total, mixed)
            return carry

        lax.fori_loop(0, count, again, 0)


def attend(parents, assignment, part, recv, other):
    count, rows, _ = other.shape
    return pl.pallas_call(
        attend_kernel,
        in_specs=[scalar_spec()] * 3 + [whole_spec()] * 2,
        out_specs=[whole_spec()] * 3,
        out_shape=[
            jax.ShapeDtypeStruct((count, rows // 2, LANES), narrow),
            jax.ShapeDtypeStruct((count, HEAD_DIM, rows), wide),
            jax.ShapeDtypeStruct((count, 8, rows), wide),
        ],
        scratch_shapes=[
            pltpu.VMEM((count, SEG, LANES), narrow),
            pltpu.VMEM((count, HEAD_DIM, SEG), narrow),
            pltpu.VMEM((8, rows), wide),
        ],
        compiler_params=pltpu.CompilerParams(vmem_limit_bytes=vmem_bytes),
        cost_estimate=busy(22),
        name="attend",
    )(parents, assignment, part, recv, other)


def attend_back_kernel(
    parents_ref,
    assign_ref,
    part_ref,
    recv_ref,
    other_ref,
    grad_ref,
    ot_ref,
    log_ref,
    dq_ref,
    mine_ref,
    theirs_ref,
    kv_ref,
    kt_ref,
    sum_ref,
):
    part = part_ref[0]
    rows = other_ref.shape[1]
    count = recv_ref.shape[0]
    gather_parts(part, recv_ref, other_ref, kv_ref, kt_ref, slice(0, HEAD_DIM))

    def clear(slot, carry):
        sum_ref[slot] = jnp.zeros((SEG, LANES), wide)
        return carry

    lax.fori_loop(0, count, clear, 0)

    def run(segment, depth):
        slots = path_of(parents_ref, assign_ref, segment, depth)
        own = slots[0]
        query = unpack_low(recv_ref[own, rows:, :])
        packed = grad_ref[own]
        grad = unpack_high(packed)
        flipped = jnp.transpose(packed.astype(wide))
        grad_t = jnp.concatenate([flipped[:HEAD_DIM], flipped[HEAD_DIM:]], axis=1)
        delta = jnp.sum(grad_t * ot_ref[own], axis=0, keepdims=True)
        log_row = log_ref[own][:1]
        grad_query = jnp.zeros((HEAD_DIM, rows), wide)
        for level, slot in enumerate(slots):
            pair = kv_ref[slot]
            probs = jnp.exp(dot_rows(pair, query) - log_row)
            if level == 0:
                probs = jnp.where(visible(part, SEG, rows), probs, 0.0)
            grad_probs = dot_rows(pair, grad)
            grad_scores = (probs * (grad_probs - delta)).astype(narrow)
            sum_ref[slot] += dot_wide(grad_scores, query) + dot_wide(probs.astype(narrow), grad)
            grad_query = grad_query + dot_wide(kt_ref[slot], grad_scores)
        dq_ref[own] = pack_columns(grad_query * (HEAD_DIM ** (-0.5))).astype(narrow)

    tree_walk(run, count, 1)

    def finish(slot, carry):
        mine_ref[slot] = sum_ref[slot, pl.ds(pl.multiple_of(part * rows, rows), rows), :]
        theirs = sum_ref[slot, pl.ds(pl.multiple_of((1 - part) * rows, rows), rows), :]
        theirs_ref[slot] = theirs.astype(narrow)
        return carry

    lax.fori_loop(0, count, finish, 0)


def attend_back(parents, assignment, part, recv, other, grad, ot, logs):
    count, rows, _ = other.shape
    return pl.pallas_call(
        attend_back_kernel,
        in_specs=[scalar_spec()] * 3 + [whole_spec()] * 5,
        out_specs=[whole_spec()] * 3,
        out_shape=[
            jax.ShapeDtypeStruct((count, rows // 2, LANES), narrow),
            jax.ShapeDtypeStruct((count, rows, LANES), wide),
            jax.ShapeDtypeStruct((count, rows, LANES), narrow),
        ],
        scratch_shapes=[
            pltpu.VMEM((count, SEG, LANES), narrow),
            pltpu.VMEM((count, HEAD_DIM, SEG), narrow),
            pltpu.VMEM((count, SEG, LANES), wide),
        ],
        compiler_params=pltpu.CompilerParams(vmem_limit_bytes=vmem_bytes),
        cost_estimate=busy(37),
        name="attend_back",
    )(parents, assignment, part, recv, other, grad, ot, logs)


def heads_to_rows(recv_ref, groups):
    half = recv_ref.shape[1]
    heads = recv_ref.shape[0] // groups
    strips = []
    for pair in range(heads // 2):
        pieces = []
        for part in range(groups):
            left = recv_ref[2 * pair * groups + part].astype(wide)
            right = recv_ref[(2 * pair + 1) * groups + part].astype(wide)
            pieces += list(swap_pairs(left, right))
        strips.append(jnp.concatenate(pieces, axis=0))
    return jnp.concatenate(strips, axis=1).astype(narrow)


def merge_kernel(
    own_ref, other_ref, w_own_ref, w_other_ref, x_ref, gain_ref, attended_ref, hidden_ref, normed_ref
):
    groups = 2
    mine = heads_to_rows(own_ref, groups)
    attended_ref[...] = mine
    theirs = heads_to_rows(other_ref, groups)
    branch = dot_wide(mine, w_own_ref[...]).astype(narrow).astype(wide)
    branch = branch + dot_wide(theirs, w_other_ref[...]).astype(narrow).astype(wide)
    hidden = x_ref[...].astype(wide) + branch
    hidden_ref[...] = hidden
    normed_ref[...] = (hidden * rms_scale(hidden) * gain_ref[...].astype(wide)).astype(narrow)


def merge(own, other, w_own, w_other, inputs, norm_ffn):
    tokens, width = inputs.shape
    local = w_own.shape[0]
    return pl.pallas_call(
        merge_kernel,
        in_specs=[whole_spec()] * 6,
        out_specs=[whole_spec()] * 3,
        out_shape=[
            jax.ShapeDtypeStruct((tokens, local), narrow),
            jax.ShapeDtypeStruct((tokens, width), wide),
            jax.ShapeDtypeStruct((tokens, width), narrow),
        ],
        compiler_params=pltpu.CompilerParams(vmem_limit_bytes=vmem_bytes),
        cost_estimate=busy(6),
        name="merge",
    )(own, other, w_own, w_other, inputs, norm_ffn.reshape(1, width))


def branch_back_kernel(
    own_ref,
    early_ref,
    late_ref,
    hidden_ref,
    cot_ref,
    gain_ref,
    w_ref,
    send_ref,
    hidden_grad_ref,
    branch_ref,
    gain_grad_ref,
):
    groups = 2
    other = jnp.concatenate([early_ref[...], late_ref[...]], axis=0)
    grad_normed = own_ref[...].astype(wide) + other.astype(wide)
    hidden = hidden_ref[...]
    back, gain_grad = norm_back(grad_normed, hidden, rms_scale(hidden), gain_ref[...].astype(wide))
    gain_grad_ref[...] = gain_grad[None]
    grad_hidden = cot_ref[...].astype(wide) + back
    hidden_grad_ref[...] = grad_hidden
    grad_branch = grad_hidden.astype(narrow)
    branch_ref[...] = grad_branch
    attended_grad = dot_rows(grad_branch, w_ref[...])
    tokens, local = attended_grad.shape
    half = tokens // groups // 2
    for pair in range(local // LANES):
        for part in range(groups):
            cols = slice(pair * LANES, (pair + 1) * LANES)
            low = attended_grad[2 * part * half : (2 * part + 1) * half, cols]
            high = attended_grad[(2 * part + 1) * half : (2 * part + 2) * half, cols]
            for at, tile in enumerate(swap_pairs(low, high)):
                send_ref[2 * pair + at, part] = tile.astype(narrow)


def branch_back(own, early, late, hidden, cotangent, norm_ffn, w_out):
    tokens, width = hidden.shape
    local = w_out.shape[0]
    groups = 2
    return pl.pallas_call(
        branch_back_kernel,
        in_specs=[whole_spec()] * 7,
        out_specs=[whole_spec()] * 4,
        out_shape=[
            jax.ShapeDtypeStruct((local // HEAD_DIM, groups, tokens // groups // 2, LANES), narrow),
            jax.ShapeDtypeStruct((tokens, width), wide),
            jax.ShapeDtypeStruct((tokens, width), narrow),
            jax.ShapeDtypeStruct((1, width), wide),
        ],
        compiler_params=pltpu.CompilerParams(vmem_limit_bytes=vmem_bytes),
        cost_estimate=busy(6),
        name="branch_back",
    )(own, early, late, hidden, cotangent, norm_ffn.reshape(1, width), w_out)


def fold_kernel(
    mine_ref, arrived_ref, dq_ref, cos_ref, sin_ref, slot_cos_ref, slot_sin_ref, send_ref, feats_ref
):
    count, rows, _ = mine_ref.shape
    half = rows // 2
    low = lane_ids((rows, LANES)) < HEAD_DIM

    def step(slot, carry):
        turn_cos = slot_cos_ref[slot][:1]
        turn_sin = slot_sin_ref[slot][:1]
        cosine = cos_ref[...] * turn_cos - sin_ref[...] * turn_sin
        sine = -(sin_ref[...] * turn_cos + cos_ref[...] * turn_sin)
        pair = mine_ref[slot] + arrived_ref[slot].astype(wide)
        key = spin(pair, cosine, sine)
        send_ref[slot, :rows, :] = jnp.where(low, key, pair).astype(narrow)
        feats_ref[slot, :, :LANES] = jnp.where(low, key, 0.5 * pair.astype(narrow).astype(wide)).astype(narrow)
        packed = dq_ref[slot].astype(wide)
        query = jnp.concatenate([packed, pltpu.roll(packed, HEAD_DIM, 1)], axis=0)
        query = jnp.where(low, spin(query, cosine, sine), 0.0)
        feats_ref[slot, :, LANES:] = query.astype(narrow)
        top = query[:half]
        bottom = pltpu.roll(query[half:], HEAD_DIM, 1)
        send_ref[slot, rows:, :] = jnp.where(low[:half], top, bottom).astype(narrow)
        return carry

    lax.fori_loop(0, count, step, 0, unroll=4)


def fold(mine, arrived, grad_q, cosine, sine, slot_cos, slot_sin):
    count, rows, _ = mine.shape
    return pl.pallas_call(
        fold_kernel,
        in_specs=[whole_spec()] * 7,
        out_specs=[whole_spec()] * 2,
        out_shape=[
            jax.ShapeDtypeStruct((count, rows + rows // 2, LANES), narrow),
            jax.ShapeDtypeStruct((count, rows, 2 * LANES), narrow),
        ],
        compiler_params=pltpu.CompilerParams(vmem_limit_bytes=vmem_bytes),
        cost_estimate=busy(9),
        name="fold",
    )(mine, arrived, grad_q, cosine, sine, slot_cos, slot_sin)


def unproject_kernel(recv_ref, wq_ref, wk_ref, wv_ref, first_ref, part_ref):
    groups = 2
    rows = recv_ref.shape[1] * 2 // 3
    heads = recv_ref.shape[0] // groups
    for part in range(groups):
        span = slice(part * rows, (part + 1) * rows)
        keys, values, queries = [], [], []
        for pair in range(heads // 2):
            cols = slice(pair * LANES, (pair + 1) * LANES)
            left = recv_ref[2 * pair * groups + part].astype(wide)
            right = recv_ref[(2 * pair + 1) * groups + part].astype(wide)
            key, value = swap_pairs(left[:rows], right[:rows])
            query = jnp.concatenate(swap_pairs(left[rows:], right[rows:]), axis=0)
            value = 0.5 * value
            first_ref[span, cols] = value
            keys.append(key.astype(narrow))
            values.append(value.astype(narrow))
            queries.append(query.astype(narrow))
        total = dot_rows(jnp.concatenate(queries, axis=1), wq_ref[...])
        total = total + dot_rows(jnp.concatenate(keys, axis=1), wk_ref[...])
        total = total + dot_rows(jnp.concatenate(values, axis=1), wv_ref[...])
        part_ref[span, :] = total.astype(narrow)


def unproject(recv, w_query, w_key, w_value):
    width, local = w_query.shape
    tokens = recv.shape[1] * 4 // 3
    return pl.pallas_call(
        unproject_kernel,
        in_specs=[whole_spec()] * 4,
        out_specs=[whole_spec()] * 2,
        out_shape=[
            jax.ShapeDtypeStruct((tokens, local), wide),
            jax.ShapeDtypeStruct((tokens, width), narrow),
        ],
        compiler_params=pltpu.CompilerParams(vmem_limit_bytes=vmem_bytes),
        cost_estimate=busy(60),
        name="unproject",
    )(recv, w_query, w_key, w_value)


def finish_kernel(part_ref, own_ref, other_ref, query_ref, key_ref, value_ref, out_ref):
    chips, size, width = own_ref.shape
    part = part_ref[0]
    head_rows = 3 * HEAD_DIM // 2
    out_rows = size - head_rows

    def emit(first, second):
        for chip in range(chips):
            at = chip * out_rows
            out_ref[at : at + out_rows, :] = first[chip, head_rows:, :].astype(wide)
            at += chips * out_rows
            out_ref[at : at + out_rows, :] = second[chip, head_rows:, :].astype(wide)

        def column(block, carry):
            cols = pl.ds(pl.multiple_of(block * LANES, LANES), LANES)
            for pair in range(chips // 2):
                pieces = [
                    jnp.concatenate(
                        [first[chip, :head_rows, cols], second[chip, :head_rows, cols]], axis=0
                    ).astype(wide)
                    for chip in (2 * pair, 2 * pair + 1)
                ]
                for at, target in enumerate((key_ref, value_ref, query_ref)):
                    span = slice(at * HEAD_DIM, (at + 1) * HEAD_DIM)
                    both = jnp.concatenate([piece[span] for piece in pieces], axis=0)
                    target[cols, pair * LANES : (pair + 1) * LANES] = jnp.transpose(both)
            return carry

        lax.fori_loop(0, width // LANES, column, 0)

    @pl.when(part == 0)
    def _():
        emit(own_ref, other_ref)

    @pl.when(part == 1)
    def _():
        emit(other_ref, own_ref)


def finish(part, own, other, local):
    width = own.shape[2]
    return pl.pallas_call(
        finish_kernel,
        in_specs=[scalar_spec()] + [whole_spec()] * 2,
        out_specs=[whole_spec()] * 4,
        out_shape=[jax.ShapeDtypeStruct((width, local), wide)] * 3
        + [jax.ShapeDtypeStruct((local, width), wide)],
        compiler_params=pltpu.CompilerParams(vmem_limit_bytes=vmem_bytes),
        cost_estimate=busy(6),
        name="finish",
    )(part, own, other)


def swap_tensor(values):
    return lax.ppermute(values, "tensor", [(0, 1), (1, 0)])


def swap_bit(values, bit, count):
    return lax.ppermute(values, "dp", [(i, i ^ bit) for i in range(count)])


def add_narrow(left, right):
    return (left.astype(wide) + right.astype(wide)).astype(narrow)


def take_part(values, index, parts):
    size = values.shape[0] // parts
    return lax.dynamic_slice_in_dim(values, index * size, size, 0)


def reduce_bit(values, bit, place, count):
    mine = (place // bit) % 2
    arrived = swap_bit(take_part(values, 1 - mine, 2), bit, count)
    return add_narrow(take_part(values, mine, 2), arrived)


def side_groups(count):
    return [[chip * 2 + core for chip in range(count // 2)] for core in range(2)]


def to_chips(values, count):
    return lax.all_to_all(
        values, "dp", split_axis=0, concat_axis=0, tiled=True, axis_index_groups=side_groups(count)
    )


def spread(values, count):
    chips = count // 2
    return to_chips(jnp.broadcast_to(values[None], (chips,) + values.shape), count)


def spread_line(copies, count):
    length = count // 4
    return lax.all_to_all(
        copies,
        "dp",
        split_axis=0,
        concat_axis=0,
        tiled=True,
        axis_index_groups=[[z * 4 + rest for z in range(length)] for rest in range(4)],
    )


def spread_pair(along, place, count):
    arrived = swap_bit(along, 2, count)
    high = (place // 2) % 2 == 1
    pair = jnp.stack([jnp.where(high, arrived, along), jnp.where(high, along, arrived)], axis=1)
    return pair.reshape((2 * along.shape[0],) + along.shape[1:])


def gather_core(values, axis, place, count):
    mine = place % 2
    arrived = swap_bit(values, 1, count)
    row = jnp.concatenate([arrived, values, arrived], axis=axis)
    size = values.shape[axis]
    return lax.dynamic_slice_in_dim(row, (1 - mine) * size, 2 * size, axis)


def sum_over_dp(values, place, count):
    chips = count // 2
    values = reduce_bit(values, 1, place, count)
    shares = to_chips(values.reshape((chips, values.shape[0] // chips) + values.shape[1:]), count)
    total = jnp.sum(shares.astype(wide), axis=0).astype(narrow)
    whole = spread(total, count)
    whole = whole.reshape((-1,) + whole.shape[2:])
    return gather_core(whole, 0, place, count)


def reduce_z(values, place, count):
    at = place // 4
    total = take_part(values, at, 4).astype(wide)
    for step in (1, 2, 3):
        share = take_part(values, at ^ step, 4)
        total = total + swap_bit(share, 4 * step, count).astype(wide)
    return total.astype(narrow)


def gather_z(values, place, count):
    at = place // 4
    shares = [values] + [swap_bit(values, 4 * step, count) for step in (1, 2, 3)]
    row = jnp.concatenate(shares, axis=0)
    return jnp.concatenate([take_part(row, at ^ target, 4) for target in range(4)], axis=0)


def gather_bit(values, bit, place, count):
    mine = (place // bit) % 2
    arrived = swap_bit(values, bit, count)
    row = jnp.concatenate([arrived, values, arrived], axis=0)
    size = values.shape[0]
    return lax.dynamic_slice_in_dim(row, (1 - mine) * size, 2 * size, 0)


def after(value, *others):
    return lax.optimization_barrier((value,) + others)[0]


def sum_small(values, count):
    bit = 1
    while bit < count:
        values = values + swap_bit(values, bit, count)
        bit *= 2
    return values


def body_heads(
    inputs,
    first_values,
    w_query,
    w_key,
    w_value,
    w_out,
    w_gate,
    w_up,
    w_down,
    norm_attn,
    norm_ffn,
    cotangent,
    parents,
    depth_pos,
    assignment,
):
    count = parents.shape[0]
    tokens, width = inputs.shape
    local = w_query.shape[1]
    heads = local // HEAD_DIM
    groups = count // heads
    place = lax.axis_index("dp")
    part = (place % groups).astype(jnp.int32)
    part_array = part.reshape(1)

    rows = tokens // groups
    half = HEAD_DIM // 2
    w_out_other = swap_tensor(w_out)
    slot_ids = jnp.arange(count, dtype=jnp.int32)
    start = jnp.sum(jnp.where(slot_ids == place, depth_pos, 0))
    lanes = jnp.arange(LANES, dtype=jnp.int32)
    frequency = rope_base ** (-(lanes % half).astype(wide) * 2.0 / HEAD_DIM)
    sign = jnp.where(lanes % HEAD_DIM < half, -1.0, 1.0)[None, :]
    positions = (start + jnp.arange(tokens, dtype=jnp.int32)).astype(wide)
    angles = positions[:, None] * frequency[None, :]
    cosine = jnp.cos(angles)
    sine = jnp.sin(angles) * sign
    part_positions = (part * rows + jnp.arange(rows, dtype=jnp.int32)).astype(wide)
    part_angles = part_positions[:, None] * frequency[None, :]
    part_cos = jnp.cos(part_angles)
    part_sin = jnp.sin(part_angles) * sign
    slot_angles = depth_pos.astype(wide)[:, None] * frequency[None, :]
    slot_shape = (count, 8, LANES)
    slot_cos = jnp.broadcast_to(jnp.cos(slot_angles)[:, None, :], slot_shape)
    slot_sin = jnp.broadcast_to((jnp.sin(slot_angles) * sign)[:, None, :], slot_shape)

    send, normed = project(
        inputs, norm_attn, first_values, cosine, sine, w_query, w_key, w_value, groups
    )
    send = send.reshape(count, rows + rows // 2, LANES)
    recv = lax.all_to_all(send, "dp", split_axis=0, concat_axis=0, tiled=True)
    normed_theirs = swap_bit(take_part(normed, 1 - part, groups), 1, count)
    normed_mine = take_part(normed, part, groups)
    normed_row = jnp.concatenate([normed_theirs, normed_mine, normed_theirs], axis=0)
    normed_chip = lax.dynamic_slice_in_dim(normed_row, (1 - part) * rows, groups * rows, 0)
    side = lax.axis_index("tensor")
    quarter = rows // 2
    normed_quarter = lax.dynamic_index_in_dim(
        normed_chip.reshape(groups, 2, quarter, width), side, 1, keepdims=False
    ).reshape(groups * quarter, width)
    recv, normed_quarter = lax.optimization_barrier((recv, normed_quarter))
    normed_own = lax.all_gather(
        normed_quarter, "dp", axis=0, tiled=True, axis_index_groups=side_groups(count)
    )

    other = swap_bit(recv[:, :rows], 1, count)
    packed, ot, logs = attend(parents, assignment, part_array, recv, other)
    own_out = lax.all_to_all(packed, "dp", split_axis=0, concat_axis=0, tiled=True)
    other_out = swap_tensor(own_out)
    attended, hidden, normed_ffn = merge(own_out, other_out, w_out, w_out_other, inputs, norm_ffn)

    gate_proj = jnp.dot(normed_ffn, w_gate, preferred_element_type=wide)
    up_proj = jnp.dot(normed_ffn, w_up, preferred_element_type=wide)
    silu_gate = jax.nn.silu(gate_proj)
    activated = (silu_gate * up_proj).astype(narrow)
    grad_activated = jnp.einsum("td,fd->tf", cotangent, w_down, preferred_element_type=wide)
    sigmoid_gate = jax.nn.sigmoid(gate_proj)
    grad_gate = (
        grad_activated * up_proj * sigmoid_gate * (1.0 + gate_proj * (1.0 - sigmoid_gate))
    ).astype(narrow)
    grad_up = (grad_activated * silu_gate).astype(narrow)
    ffn_partial = (
        jnp.einsum("tf,df->td", grad_gate, w_gate, preferred_element_type=wide)
        + jnp.einsum("tf,df->td", grad_up, w_up, preferred_element_type=wide)
    ).astype(narrow)
    ffn_early = swap_tensor(ffn_partial[: tokens // 2])
    ffn_grads = tuple(
        jnp.einsum(form, left, right, preferred_element_type=wide).astype(narrow)
        for form, left, right in (
            ("td,tf->df", normed_ffn, grad_gate),
            ("td,tf->df", normed_ffn, grad_up),
            ("tf,td->fd", activated, cotangent),
        )
    )
    feed_partial = jnp.dot(activated, w_down, preferred_element_type=wide).astype(narrow)

    normed_own, *ffn_grads = lax.optimization_barrier((normed_own,) + ffn_grads)
    ffn_sums = lax.psum(tuple(ffn_grads), "dp")
    ffn_early = after(ffn_early, *ffn_grads)

    def way_back(ffn_early, normed_own):
        ffn_late = swap_tensor(ffn_partial[tokens // 2 :])
        grad_send, grad_hidden, grad_branch, grad_gain_ffn = branch_back(
            ffn_partial, ffn_early, ffn_late, hidden, cotangent, norm_ffn, w_out
        )
        grad_recv = lax.all_to_all(
            grad_send.reshape(count, rows // 2, LANES), "dp", split_axis=0, concat_axis=0, tiled=True
        )
        grad_w_out = jnp.einsum("tc,td->cd", attended, grad_branch, preferred_element_type=wide)
        out_half = reduce_bit(grad_w_out.astype(narrow), 1, place, count)
        grad_recv, out_half = lax.optimization_barrier((grad_recv, out_half))
        chips = count // 2
        out_shares = to_chips(out_half.reshape(chips, local // count, width), count)
        normed_other = swap_tensor(normed_own)
        feed_other = swap_tensor(after(feed_partial, normed_other))

        grad_q, mine, theirs = attend_back(
            parents, assignment, part_array, recv, other, grad_recv, ot, logs
        )
        grad_q, mine, theirs, out_shares = lax.optimization_barrier(
            (grad_q, mine, theirs, out_shares)
        )
        arrived = swap_bit(theirs, 1, count)
        back_send, feats = fold(
            mine, arrived, grad_q, part_cos, part_sin, slot_cos, slot_sin
        )
        back_recv = lax.all_to_all(back_send, "dp", split_axis=0, concat_axis=0, tiled=True)
        feats = feats.reshape(count, 2, quarter, 2 * LANES)
        head_grads = sum(
            jnp.einsum(
                "tc,td->cd",
                lax.dynamic_index_in_dim(feats, at, 1, keepdims=False).reshape(-1, 2 * LANES),
                normed_part,
                preferred_element_type=wide,
            )
            for at, normed_part in ((side, normed_own), (1 - side, normed_other))
        )
        head_grads = head_grads[: 3 * HEAD_DIM].astype(narrow)
        head_share = reduce_bit(head_grads, 1, place, count)
        out_share = jnp.sum(out_shares.astype(wide), axis=0).astype(narrow)
        share = jnp.concatenate([head_share, out_share], axis=0)
        copies = jnp.broadcast_to(share[None], (count // 4,) + share.shape)
        back_recv, feed_other, copies = lax.optimization_barrier((back_recv, feed_other, copies))
        grad_first, attn_partial = unproject(back_recv, w_query, w_key, w_value)
        attn_other = swap_tensor(attn_partial)
        along = spread_line(copies, count)
        spread_all = spread_pair(after(along, attn_partial), place, count)
        output = (hidden + (feed_partial.astype(wide) + feed_other.astype(wide))).astype(narrow)
        return (
            output,
            grad_hidden,
            grad_gain_ffn,
            grad_first,
            attn_partial,
            attn_other,
            spread_all,
        )

    def no_tree(*operands):
        shapes = jax.eval_shape(way_back, *operands)
        return tuple(jnp.zeros(leaf.shape, leaf.dtype) for leaf in shapes)

    output, grad_hidden, grad_gain_ffn, grad_first, attn_partial, attn_other, spread_all = lax.cond(
        parents[0] < 0, way_back, no_tree, ffn_early, normed_own
    )
    spread_other = swap_bit(spread_all, 1, count)
    inputs_wide = inputs.astype(wide)
    grad_normed = attn_partial.astype(wide) + attn_other.astype(wide)
    grad_input_norm, grad_gain_attn = norm_back(
        grad_normed, inputs_wide, rms_scale(inputs_wide), norm_attn.astype(wide)
    )
    grad_inputs = grad_hidden + grad_input_norm
    gains = jnp.stack([grad_gain_attn, grad_gain_ffn[0]])
    head_query, head_key, head_value, sum_w_out = finish(part_array, spread_all, spread_other, local)
    gains = after(gains + swap_bit(gains, 1, count), sum_w_out)
    sums = []
    for at, term in enumerate(ffn_sums):
        sums.append(after(term, grad_inputs, sum_w_out).astype(wide))
        gains = after(gains + swap_bit(gains, 2 << at, count), sums[-1])
    return (
        output,
        grad_inputs,
        grad_first,
        head_query,
        head_key,
        head_value,
        sum_w_out,
        sums[0],
        sums[1],
        sums[2],
        gains[0],
        gains[1],
    )


def pick_body(mesh):
    if mesh.shape["dp"] == 16 and mesh.shape["tensor"] == 2:
        return body_heads
    return body_general


def solution(mesh):
    placed = (
        P("dp", None),
        P("dp", "tensor"),
        P(None, "tensor"),
        P(None, "tensor"),
        P(None, "tensor"),
        P("tensor", None),
        P(None, "tensor"),
        P(None, "tensor"),
        P("tensor", None),
        P(),
        P(),
        P("dp", None),
        P(),
        P(),
        P(),
    )
    return jax.shard_map(
        pick_body(mesh),
        mesh=mesh,
        in_specs=placed,
        out_specs=(
            P("dp", None),
            P("dp", None),
            P("dp", "tensor"),
            P(None, "tensor"),
            P(None, "tensor"),
            P(None, "tensor"),
            P("tensor", None),
            P(None, "tensor"),
            P(None, "tensor"),
            P("tensor", None),
            P(),
            P(),
        ),
        check_vma=False,
    )
```

```python
import jax
import jax.numpy as jnp
import numpy as np
from jax import lax
from jax.experimental import pallas as pl
from jax.experimental.pallas import tpu as pltpu
from jax.sharding import PartitionSpec as P

HEAD_DIM = 64
SEG = 512


epsilon = 1e-06
rope_base = 10000.0
climb_steps = 5
masked_score = -1e30


def rms_scale(values):
    return lax.rsqrt(jnp.mean(values * values, axis=-1, keepdims=True) + epsilon)


def rotary_tables(positions, head_dim):
    half_dim = head_dim // 2
    frequency = rope_base ** (-jnp.arange(half_dim, dtype=jnp.float32) * 2.0 / head_dim)
    angles = positions.astype(jnp.float32)[:, None] * frequency[None, :]
    return (jnp.cos(angles)[:, None, :], jnp.sin(angles)[:, None, :])


def rotate(values, cosine, sine_table):
    half_dim = values.shape[-1] // 2
    first_half = values[..., :half_dim]
    second_half = values[..., half_dim:]
    return jnp.concatenate(
        [
            first_half * cosine - second_half * sine_table,
            second_half * cosine + first_half * sine_table,
        ],
        axis=-1,
    )


def rotate_back(gradient, cosine, sine_table):
    half_dim = gradient.shape[-1] // 2
    first_half = gradient[..., :half_dim]
    second_half = gradient[..., half_dim:]
    return jnp.concatenate(
        [
            first_half * cosine + second_half * sine_table,
            second_half * cosine - first_half * sine_table,
        ],
        axis=-1,
    )


def parent_slots(parents, assignment):
    count = parents.shape[0]
    slot_ids = jnp.arange(count, dtype=jnp.int32)
    at_slot = assignment[None, :] == slot_ids[:, None]
    parent_seg = jnp.sum(jnp.where(at_slot, parents[None, :], 0), axis=1)
    parent_match = slot_ids[None, :] == parent_seg[:, None]
    above_slot = jnp.sum(jnp.where(parent_match, assignment[None, :], 0), axis=1)
    return jnp.where(parent_seg >= 0, above_slot, -1)


def climb(parent_slot, start_slots):
    slot_ids = jnp.arange(parent_slot.shape[0], dtype=jnp.int32)
    levels = [start_slots]
    current = start_slots
    for step_index in range(climb_steps):
        matched = current[:, None] == slot_ids[None, :]
        upward = jnp.sum(jnp.where(matched, parent_slot[None, :], 0), axis=1)
        current = jnp.where(current >= 0, upward, -1)
        levels.append(current)
    return jnp.stack(levels, axis=1)


def norm_back(grad_normed, values, row_scale, gain_vector):
    scaled_grad = grad_normed * gain_vector
    grad_gain = jnp.sum(grad_normed * values * row_scale, axis=0)
    grad_values = row_scale * (
        scaled_grad
        - values * row_scale * row_scale * jnp.mean(scaled_grad * values, axis=-1, keepdims=True)
    )
    return (grad_values, grad_gain)


def path_rows(source, path_row):
    parts = []
    for level_index in range(climb_steps + 1):
        row_begin = (jnp.maximum(path_row[level_index], 0) * SEG).astype(jnp.int32)
        parts.append(lax.dynamic_slice_in_dim(source, row_begin, SEG, 0))
    return jnp.concatenate(parts, axis=0)


def path_permit(path_row, causal):
    parts = [causal]
    for level_index in range(1, climb_steps + 1):
        parts.append(jnp.broadcast_to(path_row[level_index] >= 0, (SEG, SEG)))
    return jnp.concatenate(parts, axis=1)


def body_general(
    inputs,
    first_values,
    w_query,
    w_key,
    w_value,
    w_out,
    w_gate,
    w_up,
    w_down,
    norm_attn,
    norm_ffn,
    cotangent,
    parents,
    depth_pos,
    assignment,
):
    row_count = inputs.shape[0]
    local_width = w_query.shape[1]
    head_count = local_width // HEAD_DIM
    score_scale = HEAD_DIM ** (-0.5)
    seg_count = row_count // SEG
    slot_total = parents.shape[0]
    slot_ids = jnp.arange(slot_total, dtype=jnp.int32)
    local_rows = jnp.arange(row_count, dtype=jnp.int32)
    own_slots = lax.axis_index("dp") * seg_count + jnp.arange(seg_count, dtype=jnp.int32)
    own_slot_rows = jnp.repeat(own_slots, SEG)
    depth_rows = jnp.sum(
        jnp.where(own_slot_rows[:, None] == slot_ids[None, :], depth_pos[None, :], 0), axis=1
    )
    positions = depth_rows + local_rows % SEG
    parent_slot = parent_slots(parents, assignment)
    own_paths = climb(parent_slot, own_slots)
    offsets = jnp.arange(SEG, dtype=jnp.int32)
    causal = offsets[None, :] <= offsets[:, None]
    cosine, sine_table = rotary_tables(positions, HEAD_DIM)
    inputs_wide = inputs.astype(jnp.float32)
    attn_scale = rms_scale(inputs_wide)
    gain_attn = norm_attn.astype(jnp.float32)
    normed = (inputs_wide * attn_scale * gain_attn).astype(jnp.bfloat16)
    query_proj = jnp.dot(normed, w_query, preferred_element_type=jnp.float32)
    key_proj = jnp.dot(normed, w_key, preferred_element_type=jnp.float32)
    value_proj = jnp.dot(normed, w_value, preferred_element_type=jnp.float32)
    query_rot = rotate(
        query_proj.reshape(row_count, head_count, HEAD_DIM), cosine, sine_table
    ).astype(jnp.bfloat16)
    key_rot = (
        rotate(key_proj.reshape(row_count, head_count, HEAD_DIM), cosine, sine_table)
        .astype(jnp.bfloat16)
        .reshape(row_count, local_width)
    )
    mixed = (0.5 * value_proj + 0.5 * first_values.astype(jnp.float32)).astype(jnp.bfloat16)
    key_all, value_all = (
        lax.all_gather(key_rot, "dp", axis=0, tiled=True),
        lax.all_gather(mixed, "dp", axis=0, tiled=True),
    )
    query_segs = query_rot.reshape(seg_count, SEG, head_count, HEAD_DIM)

    def segment_forward(operand):
        query_block, path_row = operand
        near_keys = path_rows(key_all, path_row).reshape(-1, head_count, HEAD_DIM)
        near_values = path_rows(value_all, path_row).reshape(-1, head_count, HEAD_DIM)
        permit = path_permit(path_row, causal)
        scores = (
            jnp.einsum("qhd,khd->hqk", query_block, near_keys, preferred_element_type=jnp.float32)
            * score_scale
        )
        scores = jnp.where(permit[None], scores, masked_score)
        row_max = jnp.max(scores, axis=-1)
        weights = jnp.where(permit[None], jnp.exp(scores - row_max[..., None]), 0.0)
        row_total = jnp.sum(weights, axis=-1)
        attn_probs = weights / row_total[..., None]
        block_out = jnp.einsum(
            "hqk,khd->qhd",
            attn_probs.astype(jnp.bfloat16),
            near_values,
            preferred_element_type=jnp.float32,
        )
        return (block_out, row_max + jnp.log(row_total))

    attn_parts, log_parts = lax.map(segment_forward, (query_segs, own_paths))
    attn_exact = attn_parts.reshape(row_count, head_count, HEAD_DIM)
    attended = attn_exact.reshape(row_count, local_width).astype(jnp.bfloat16)
    branch_attn = lax.psum(
        jnp.dot(attended, w_out, preferred_element_type=jnp.float32).astype(jnp.bfloat16), "tensor"
    ).astype(jnp.float32)
    hidden_state = inputs_wide + branch_attn
    ffn_scale = rms_scale(hidden_state)
    gain_ffn = norm_ffn.astype(jnp.float32)
    normed_ffn = (hidden_state * ffn_scale * gain_ffn).astype(jnp.bfloat16)
    gate_proj = jnp.dot(normed_ffn, w_gate, preferred_element_type=jnp.float32)
    up_proj = jnp.dot(normed_ffn, w_up, preferred_element_type=jnp.float32)
    silu_gate = jax.nn.silu(gate_proj)
    activated = (silu_gate * up_proj).astype(jnp.bfloat16)
    feed = lax.psum(
        jnp.dot(activated, w_down, preferred_element_type=jnp.float32).astype(jnp.bfloat16),
        "tensor",
    ).astype(jnp.float32)
    output = (hidden_state + feed).astype(jnp.bfloat16)
    grad_w_down = jnp.einsum("tf,td->fd", activated, cotangent, preferred_element_type=jnp.float32)
    grad_activated = jnp.einsum("td,fd->tf", cotangent, w_down, preferred_element_type=jnp.float32)
    sigmoid_gate = jax.nn.sigmoid(gate_proj)
    grad_gate = (
        grad_activated * up_proj * sigmoid_gate * (1.0 + gate_proj * (1.0 - sigmoid_gate))
    ).astype(jnp.bfloat16)
    grad_up = (grad_activated * silu_gate).astype(jnp.bfloat16)
    grad_w_gate = jnp.einsum("td,tf->df", normed_ffn, grad_gate, preferred_element_type=jnp.float32)
    grad_w_up = jnp.einsum("td,tf->df", normed_ffn, grad_up, preferred_element_type=jnp.float32)
    ffn_partial = jnp.einsum(
        "tf,df->td", grad_gate, w_gate, preferred_element_type=jnp.float32
    ) + jnp.einsum("tf,df->td", grad_up, w_up, preferred_element_type=jnp.float32)
    grad_normed_ffn = lax.psum(ffn_partial.astype(jnp.bfloat16), "tensor").astype(jnp.float32)
    grad_hidden_norm, grad_gain_ffn = norm_back(grad_normed_ffn, hidden_state, ffn_scale, gain_ffn)
    grad_hidden = cotangent.astype(jnp.float32) + grad_hidden_norm
    grad_branch = grad_hidden.astype(jnp.bfloat16)
    grad_w_out = jnp.einsum("tc,td->cd", attended, grad_branch, preferred_element_type=jnp.float32)
    grad_attended = jnp.einsum(
        "td,cd->tc", grad_branch, w_out, preferred_element_type=jnp.float32
    ).astype(jnp.bfloat16)
    grad_heads = grad_attended.reshape(row_count, head_count, HEAD_DIM)
    delta_rows = jnp.sum(grad_heads.astype(jnp.float32) * attn_exact, axis=-1)
    delta_parts = jnp.transpose(delta_rows.reshape(seg_count, SEG, head_count), (0, 2, 1))
    grad_segs = grad_heads.reshape(seg_count, SEG, head_count, HEAD_DIM)
    key_back, value_back = (key_all, value_all)

    def segment_back(query_block, grad_block, path_row, log_block, delta_block):
        near_keys = path_rows(key_back, path_row).reshape(-1, head_count, HEAD_DIM)
        near_values = path_rows(value_back, path_row).reshape(-1, head_count, HEAD_DIM)
        permit = path_permit(path_row, causal)
        scores = (
            jnp.einsum("qhd,khd->hqk", query_block, near_keys, preferred_element_type=jnp.float32)
            * score_scale
        )
        scores = jnp.where(permit[None], scores, masked_score)
        attn_probs = jnp.where(permit[None], jnp.exp(scores - log_block[..., None]), 0.0)
        grad_probs = jnp.einsum(
            "qhd,khd->hqk", grad_block, near_values, preferred_element_type=jnp.float32
        )
        grad_scores = (attn_probs * (grad_probs - delta_block[..., None])).astype(jnp.bfloat16)
        grad_part = (
            jnp.einsum("hqk,khd->qhd", grad_scores, near_keys, preferred_element_type=jnp.float32)
            * score_scale
        )
        return (attn_probs, grad_scores, grad_part)

    zero_rows = jnp.zeros((key_back.shape[0], local_width), jnp.float32)

    def scatter_step(fold_state, operand):
        key_acc, value_acc = fold_state
        query_block, grad_block, path_row, log_block, delta_block = operand
        attn_probs, grad_scores, grad_part = segment_back(
            query_block, grad_block, path_row, log_block, delta_block
        )
        key_term = (
            jnp.einsum("hqk,qhd->khd", grad_scores, query_block, preferred_element_type=jnp.float32)
            * score_scale
        ).reshape(climb_steps + 1, SEG, local_width)
        value_term = jnp.einsum(
            "hqk,qhd->khd",
            attn_probs.astype(jnp.bfloat16),
            grad_block,
            preferred_element_type=jnp.float32,
        ).reshape(climb_steps + 1, SEG, local_width)
        for level_index in range(climb_steps + 1):
            row_begin = (jnp.maximum(path_row[level_index], 0) * SEG).astype(jnp.int32)
            key_acc = lax.dynamic_update_slice_in_dim(
                key_acc,
                lax.dynamic_slice_in_dim(key_acc, row_begin, SEG, 0) + key_term[level_index],
                row_begin,
                0,
            )
            value_acc = lax.dynamic_update_slice_in_dim(
                value_acc,
                lax.dynamic_slice_in_dim(value_acc, row_begin, SEG, 0) + value_term[level_index],
                row_begin,
                0,
            )
        return ((key_acc, value_acc), grad_part)

    (key_terms, value_terms), grad_parts = lax.scan(
        scatter_step,
        (zero_rows, zero_rows),
        (query_segs, grad_segs, own_paths, log_parts, delta_parts),
    )
    grad_query_rot = grad_parts.reshape(row_count, head_count, HEAD_DIM)
    key_sums, value_sums = (
        lax.psum_scatter(
            key_terms.astype(jnp.bfloat16), "dp", scatter_dimension=0, tiled=True
        ).astype(jnp.float32),
        lax.psum_scatter(
            value_terms.astype(jnp.bfloat16), "dp", scatter_dimension=0, tiled=True
        ).astype(jnp.float32),
    )
    grad_key_rot = key_sums.reshape(row_count, head_count, HEAD_DIM)
    grad_first_values = 0.5 * value_sums
    grad_value = (0.5 * value_sums).astype(jnp.bfloat16)
    grad_key = (
        rotate_back(grad_key_rot, cosine, sine_table)
        .reshape(row_count, local_width)
        .astype(jnp.bfloat16)
    )
    grad_query = (
        rotate_back(grad_query_rot, cosine, sine_table)
        .reshape(row_count, local_width)
        .astype(jnp.bfloat16)
    )
    grad_w_query = jnp.einsum("td,tc->dc", normed, grad_query, preferred_element_type=jnp.float32)
    grad_w_key = jnp.einsum("td,tc->dc", normed, grad_key, preferred_element_type=jnp.float32)
    grad_w_value = jnp.einsum("td,tc->dc", normed, grad_value, preferred_element_type=jnp.float32)
    attn_partial = (
        jnp.einsum("tc,dc->td", grad_query, w_query, preferred_element_type=jnp.float32)
        + jnp.einsum("tc,dc->td", grad_key, w_key, preferred_element_type=jnp.float32)
        + jnp.einsum("tc,dc->td", grad_value, w_value, preferred_element_type=jnp.float32)
    )
    grad_normed = lax.psum(attn_partial.astype(jnp.bfloat16), "tensor").astype(jnp.float32)
    grad_input_norm, grad_gain_attn = norm_back(grad_normed, inputs_wide, attn_scale, gain_attn)
    grad_inputs = grad_hidden + grad_input_norm
    summed = (
        lax.psum(grad_w_query.astype(jnp.bfloat16), "dp").astype(jnp.float32),
        lax.psum(grad_w_key.astype(jnp.bfloat16), "dp").astype(jnp.float32),
        lax.psum(grad_w_value.astype(jnp.bfloat16), "dp").astype(jnp.float32),
        lax.psum(grad_w_out.astype(jnp.bfloat16), "dp").astype(jnp.float32),
        lax.psum(grad_w_gate.astype(jnp.bfloat16), "dp").astype(jnp.float32),
        lax.psum(grad_w_up.astype(jnp.bfloat16), "dp").astype(jnp.float32),
        lax.psum(grad_w_down.astype(jnp.bfloat16), "dp").astype(jnp.float32),
        lax.psum(grad_gain_attn.astype(jnp.bfloat16), "dp").astype(jnp.float32),
        lax.psum(grad_gain_ffn.astype(jnp.bfloat16), "dp").astype(jnp.float32),
    )
    return (
        output,
        grad_inputs,
        grad_first_values,
        summed[0],
        summed[1],
        summed[2],
        summed[3],
        summed[4],
        summed[5],
        summed[6],
        summed[7],
        summed[8],
    )


TREE = 16
TREE_DEPTHS = (0, 1, 2, 3, 4, 4, 4, 4, 5, 5, 5, 5, 5, 5, 5, 5)
LANES = 128
wide = jnp.float32
narrow = jnp.bfloat16
vmem_bytes = 60 * 1024 * 1024
safe_excess = 40.0


def busy(microseconds):
    return pl.CostEstimate(
        flops=int(microseconds * 1e9), bytes_accessed=int(microseconds * 2e6), transcendentals=0
    )


def lane_ids(shape):
    return lax.broadcasted_iota(jnp.int32, shape, len(shape) - 1)


def swap_pairs(left, right):
    low = lane_ids(left.shape) < HEAD_DIM
    first = jnp.where(low, left, pltpu.roll(right, HEAD_DIM, 1))
    second = jnp.where(low, pltpu.roll(left, HEAD_DIM, 1), right)
    return first, second


def spin(values, cosine, signed_sine):
    half = HEAD_DIM // 2
    ahead = pltpu.roll(values, LANES - half, 1)
    behind = pltpu.roll(values, half, 1)
    other = jnp.where(lane_ids(values.shape) % HEAD_DIM < half, ahead, behind)
    return values * cosine + other * signed_sine


def turn_constants():
    half = HEAD_DIM // 2
    lanes = np.arange(LANES)
    frequency = rope_base ** (-(lanes % half).astype(np.float64) * 2.0 / HEAD_DIM)
    sign = np.where(lanes % HEAD_DIM < half, -1.0, 1.0)
    levels = -(-(climb_steps + 1) // 8) * 8
    at = np.concatenate([np.arange(16), 16 * np.arange(SEG // 16), SEG * np.arange(levels)])
    angles = at[:, None].astype(np.float64) * frequency[None, :]
    return np.stack([np.cos(angles), np.sin(angles) * sign[None, :]]).astype(np.float32)


def turn(one, other):
    return one[0] * other[0] - one[1] * other[1], one[1] * other[0] + one[0] * other[1]


def turn_rows(turn_ref, first, rows):
    fine = turn_ref[0, :16, :], turn_ref[1, :16, :]
    parts = []
    for block in range(rows // 16):
        at = 16 + first // 16 + block
        coarse = turn_ref[0, pl.ds(at, 1), :], turn_ref[1, pl.ds(at, 1), :]
        parts.append(turn(fine, coarse))
    return tuple(jnp.concatenate(pieces, axis=0) for pieces in zip(*parts, strict=True))


def turn_depth(turn_ref, depth_pos):
    at = 16 + SEG // 16 + depth_pos // SEG
    return turn_ref[0, pl.ds(at, 1), :], turn_ref[1, pl.ds(at, 1), :]


def dot_wide(left, right):
    return jnp.dot(left, right, preferred_element_type=wide)


def dot_rows(left, right):
    return lax.dot_general(left, right, (((1,), (1,)), ((), ())), preferred_element_type=wide)


def whole_spec():
    return pl.BlockSpec(memory_space=pltpu.VMEM)


def scalar_spec():
    return pl.BlockSpec(memory_space=pltpu.SMEM)


def project_kernel(
    place_ref,
    depth_ref,
    x_ref,
    gain_ref,
    first_ref,
    turn_ref,
    wq_ref,
    wk_ref,
    wv_ref,
    send_ref,
    normed_ref,
):
    rows = x_ref.shape[0]
    pairs = first_ref.shape[1] // LANES
    x = x_ref[...].astype(wide)
    normed = (x * rms_scale(x) * gain_ref[...].astype(wide)[None]).astype(narrow)
    normed_ref[...] = normed
    query = dot_wide(normed, wq_ref[...]) * (HEAD_DIM ** (-0.5))
    key = dot_wide(normed, wk_ref[...])
    value = dot_wide(normed, wv_ref[...])
    mixed = 0.5 * value + 0.5 * first_ref[...].astype(wide)
    local = turn_rows(turn_ref, pl.program_id(0) * rows, rows)
    cosine, sine = turn(local, turn_depth(turn_ref, depth_ref[place_ref[0]]))
    for pair in range(pairs):
        cols = slice(pair * LANES, (pair + 1) * LANES)
        q = spin(query[:, cols], cosine, sine)
        k = spin(key[:, cols], cosine, sine)
        for at, tile in enumerate(swap_pairs(k, mixed[:, cols])):
            send_ref[2 * pair + at, 0, :rows, :] = tile.astype(narrow)
        for at, tile in enumerate(swap_pairs(q[: rows // 2], q[rows // 2 :])):
            send_ref[2 * pair + at, 0, rows:, :] = tile.astype(narrow)


def project(place, depth_pos, inputs, norm_attn, first_values, turns, w_query, w_key, w_value, groups):
    rows, width = inputs.shape
    local = w_query.shape[1]
    part = rows // groups
    heads = local // HEAD_DIM
    fixed = lambda step: (0, 0)
    moving = lambda step: (step, 0)
    return pl.pallas_call(
        project_kernel,
        grid=(groups,),
        in_specs=[
            scalar_spec(),
            scalar_spec(),
            pl.BlockSpec((part, width), moving),
            pl.BlockSpec((width,), lambda step: (0,)),
            pl.BlockSpec((part, local), moving),
            pl.BlockSpec(turns.shape, lambda step: (0, 0, 0)),
            pl.BlockSpec((width, local), fixed),
            pl.BlockSpec((width, local), fixed),
            pl.BlockSpec((width, local), fixed),
        ],
        out_specs=[
            pl.BlockSpec((heads, 1, part + part // 2, LANES), lambda step: (0, step, 0, 0)),
            pl.BlockSpec((part, width), moving),
        ],
        out_shape=[
            jax.ShapeDtypeStruct((heads, groups, part + part // 2, LANES), narrow),
            jax.ShapeDtypeStruct((rows, width), narrow),
        ],
        compiler_params=pltpu.CompilerParams(vmem_limit_bytes=vmem_bytes),
        cost_estimate=busy(6),
        name="project",
    )(place, depth_pos, inputs, norm_attn, first_values, turns, w_query, w_key, w_value)


def tree_walk(run, count, unroll):
    for base in range(0, count, TREE):
        at = 0
        while at < TREE:
            same = 1
            while at + same < TREE and TREE_DEPTHS[at + same] == TREE_DEPTHS[at]:
                same += 1
            depth = TREE_DEPTHS[at]
            if same == 1:
                run(base + at, depth)
            else:
                def step(i, carry, start=base + at, depth=depth):
                    run(start + i, depth)
                    return carry

                lax.fori_loop(0, same, step, 0, unroll=unroll)
            at += same


def path_of(parents_ref, assign_ref, segment, depth):
    slots = [assign_ref[segment]]
    current = segment
    for _ in range(depth):
        current = parents_ref[current]
        slots.append(assign_ref[current])
    return slots


def unpack_low(packed):
    values = packed.astype(wide)
    low = lane_ids(values.shape) < HEAD_DIM
    top = jnp.where(low, values, 0.0)
    bottom = jnp.where(low, pltpu.roll(values, HEAD_DIM, 1), 0.0)
    return jnp.concatenate([top, bottom], axis=0).astype(narrow)


def unpack_high(packed):
    values = packed.astype(wide)
    high = lane_ids(values.shape) >= HEAD_DIM
    top = jnp.where(high, pltpu.roll(values, HEAD_DIM, 1), 0.0)
    bottom = jnp.where(high, values, 0.0)
    return jnp.concatenate([top, bottom], axis=0).astype(narrow)


def pack_columns(transposed):
    half = transposed.shape[1] // 2
    stacked = jnp.concatenate([transposed[:, :half], transposed[:, half:]], axis=0)
    return jnp.transpose(stacked)


def gather_parts(part, recv_ref, other_ref, kv_ref, kvt_ref, lanes):
    rows = other_ref.shape[1] * 2 // 3

    def fill(slot, carry):
        kv_ref[slot, pl.ds(pl.multiple_of(part * rows, rows), rows), :] = recv_ref[slot, :rows, :]
        kv_ref[slot, pl.ds(pl.multiple_of((1 - part) * rows, rows), rows), :] = other_ref[slot, :rows, :]
        flipped = jnp.transpose(kv_ref[slot].astype(wide))
        kvt_ref[slot] = flipped[lanes].astype(narrow)
        return carry

    lax.fori_loop(0, recv_ref.shape[0], fill, 0)


def visible(part, keys, rows):
    key_row = lax.broadcasted_iota(jnp.int32, (keys, rows), 0)
    query_row = lax.broadcasted_iota(jnp.int32, (keys, rows), 1) + part * rows
    return key_row <= query_row


def fold_rows(values, combine):
    blocks = values.reshape(values.shape[0] // 8, 8, values.shape[1])
    return combine(blocks, axis=0)


def attend_kernel(
    parents_ref,
    assign_ref,
    part_ref,
    recv_ref,
    other_ref,
    send_ref,
    ot_ref,
    log_ref,
    kv_ref,
    vt_ref,
    excess_ref,
):
    part = part_ref[0]
    rows = other_ref.shape[1] * 2 // 3
    count = recv_ref.shape[0]
    gather_parts(part, recv_ref, other_ref, kv_ref, vt_ref, slice(HEAD_DIM, LANES))
    excess_ref[...] = jnp.zeros_like(excess_ref)

    def own_scores(own, query):
        block = dot_rows(kv_ref[own], query)
        return jnp.where(visible(part, SEG, rows), block, masked_score)

    def store(own, peak, total, mixed):
        mixed = mixed / total
        ot_ref[own] = mixed
        log_ref[own] = jnp.broadcast_to(peak + jnp.log(total), (8, rows))
        send_ref[own] = pack_columns(mixed).astype(narrow)

    def run(segment, depth):
        slots = path_of(parents_ref, assign_ref, segment, depth)
        own = slots[0]
        query = unpack_low(recv_ref[own, rows:, :])
        block = own_scores(own, query)
        peak = jnp.max(block, axis=0, keepdims=True)
        weight = jnp.exp(block - peak)
        total = fold_rows(weight, jnp.sum)
        mixed = dot_wide(vt_ref[own], weight.astype(narrow))
        crest = jnp.broadcast_to(peak, (8, rows))
        for slot in slots[1:]:
            block = dot_rows(kv_ref[slot], query)
            crest = jnp.maximum(crest, fold_rows(block, jnp.max))
            weight = jnp.exp(block - peak)
            total = total + fold_rows(weight, jnp.sum)
            mixed = mixed + dot_wide(vt_ref[slot], weight.astype(narrow))
        excess_ref[...] = jnp.maximum(excess_ref[...], crest - peak)
        store(own, peak, jnp.sum(total, axis=0, keepdims=True), mixed)

    tree_walk(run, count, 2)

    @pl.when(jnp.max(excess_ref[...]) > safe_excess)
    def _():
        def again(segment, carry):
            own = assign_ref[segment]
            query = unpack_low(recv_ref[own, rows:, :])

            def climb_up(state):
                current, peak, total, mixed = state
                current = parents_ref[current]
                slot = assign_ref[current]
                block = dot_rows(kv_ref[slot], query)
                crest = jnp.maximum(peak, jnp.max(block, axis=0, keepdims=True))
                fade = jnp.exp(peak - crest)
                weight = jnp.exp(block - crest)
                total = total * fade + jnp.sum(weight, axis=0, keepdims=True)
                mixed = mixed * fade + dot_wide(vt_ref[slot], weight.astype(narrow))
                return current, crest, total, mixed

            block = own_scores(own, query)
            peak = jnp.max(block, axis=0, keepdims=True)
            weight = jnp.exp(block - peak)
            total = jnp.sum(weight, axis=0, keepdims=True)
            mixed = dot_wide(vt_ref[own], weight.astype(narrow))
            _, peak, total, mixed = lax.while_loop(
                lambda state: parents_ref[state[0]] >= 0, climb_up, (segment, peak, total, mixed)
            )
            store(own, peak, total, mixed)
            return carry

        lax.fori_loop(0, count, again, 0)


def attend(parents, assignment, part, recv, other):
    count, rows = other.shape[0], other.shape[1] * 2 // 3
    return pl.pallas_call(
        attend_kernel,
        in_specs=[scalar_spec()] * 3 + [whole_spec()] * 2,
        out_specs=[whole_spec()] * 3,
        out_shape=[
            jax.ShapeDtypeStruct((count, rows // 2, LANES), narrow),
            jax.ShapeDtypeStruct((count, HEAD_DIM, rows), wide),
            jax.ShapeDtypeStruct((count, 8, rows), wide),
        ],
        scratch_shapes=[
            pltpu.VMEM((count, SEG, LANES), narrow),
            pltpu.VMEM((count, HEAD_DIM, SEG), narrow),
            pltpu.VMEM((8, rows), wide),
        ],
        compiler_params=pltpu.CompilerParams(vmem_limit_bytes=vmem_bytes),
        cost_estimate=busy(22),
        name="attend",
    )(parents, assignment, part, recv, other)


def attend_back_kernel(
    parents_ref,
    assign_ref,
    part_ref,
    recv_ref,
    other_ref,
    grad_ref,
    ot_ref,
    log_ref,
    dq_ref,
    mine_ref,
    theirs_ref,
    kv_ref,
    kt_ref,
    sum_ref,
):
    part = part_ref[0]
    rows = other_ref.shape[1] * 2 // 3
    count = recv_ref.shape[0]
    gather_parts(part, recv_ref, other_ref, kv_ref, kt_ref, slice(0, HEAD_DIM))

    def clear(slot, carry):
        sum_ref[slot] = jnp.zeros((SEG, LANES), wide)
        return carry

    lax.fori_loop(0, count, clear, 0)

    def run(segment, depth):
        slots = path_of(parents_ref, assign_ref, segment, depth)
        own = slots[0]
        query = unpack_low(recv_ref[own, rows:, :])
        packed = grad_ref[own]
        grad = unpack_high(packed)
        flipped = jnp.transpose(packed.astype(wide))
        grad_t = jnp.concatenate([flipped[:HEAD_DIM], flipped[HEAD_DIM:]], axis=1)
        delta = jnp.sum(grad_t * ot_ref[own], axis=0, keepdims=True)
        log_row = log_ref[own][:1]
        grad_query = jnp.zeros((HEAD_DIM, rows), wide)
        for level, slot in enumerate(slots):
            pair = kv_ref[slot]
            probs = jnp.exp(dot_rows(pair, query) - log_row)
            if level == 0:
                probs = jnp.where(visible(part, SEG, rows), probs, 0.0)
            grad_probs = dot_rows(pair, grad)
            grad_scores = (probs * (grad_probs - delta)).astype(narrow)
            sum_ref[slot] += dot_wide(grad_scores, query) + dot_wide(probs.astype(narrow), grad)
            grad_query = grad_query + dot_wide(kt_ref[slot], grad_scores)
        dq_ref[own] = pack_columns(grad_query * (HEAD_DIM ** (-0.5))).astype(narrow)

    tree_walk(run, count, 2)

    def finish(slot, carry):
        mine_ref[slot] = sum_ref[slot, pl.ds(pl.multiple_of(part * rows, rows), rows), :]
        theirs = sum_ref[slot, pl.ds(pl.multiple_of((1 - part) * rows, rows), rows), :]
        theirs_ref[slot] = theirs.astype(narrow)
        return carry

    lax.fori_loop(0, count, finish, 0)


def attend_back(parents, assignment, part, recv, other, grad, ot, logs):
    count, rows = other.shape[0], other.shape[1] * 2 // 3
    return pl.pallas_call(
        attend_back_kernel,
        in_specs=[scalar_spec()] * 3 + [whole_spec()] * 5,
        out_specs=[whole_spec()] * 3,
        out_shape=[
            jax.ShapeDtypeStruct((count, rows // 2, LANES), narrow),
            jax.ShapeDtypeStruct((count, rows, LANES), wide),
            jax.ShapeDtypeStruct((count, rows, LANES), narrow),
        ],
        scratch_shapes=[
            pltpu.VMEM((count, SEG, LANES), narrow),
            pltpu.VMEM((count, HEAD_DIM, SEG), narrow),
            pltpu.VMEM((count, SEG, LANES), wide),
        ],
        compiler_params=pltpu.CompilerParams(vmem_limit_bytes=vmem_bytes),
        cost_estimate=busy(37),
        name="attend_back",
    )(parents, assignment, part, recv, other, grad, ot, logs)


def heads_to_rows(recv_ref, groups):
    half = recv_ref.shape[1]
    heads = recv_ref.shape[0] // groups
    strips = []
    for pair in range(heads // 2):
        pieces = []
        for part in range(groups):
            left = recv_ref[2 * pair * groups + part].astype(wide)
            right = recv_ref[(2 * pair + 1) * groups + part].astype(wide)
            pieces += list(swap_pairs(left, right))
        strips.append(jnp.concatenate(pieces, axis=0))
    return jnp.concatenate(strips, axis=1).astype(narrow)


def merge_kernel(
    own_ref, other_ref, w_own_ref, w_other_ref, x_ref, gain_ref, attended_ref, hidden_ref, normed_ref
):
    groups = 2
    mine = heads_to_rows(own_ref, groups)
    attended_ref[...] = mine
    theirs = heads_to_rows(other_ref, groups)
    branch = dot_wide(mine, w_own_ref[...]).astype(narrow).astype(wide)
    branch = branch + dot_wide(theirs, w_other_ref[...]).astype(narrow).astype(wide)
    hidden = x_ref[...].astype(wide) + branch
    hidden_ref[...] = hidden
    normed_ref[...] = (hidden * rms_scale(hidden) * gain_ref[...].astype(wide)[None]).astype(narrow)


def merge(own, other, w_own, w_other, inputs, norm_ffn):
    tokens, width = inputs.shape
    local = w_own.shape[0]
    return pl.pallas_call(
        merge_kernel,
        in_specs=[whole_spec()] * 6,
        out_specs=[whole_spec()] * 3,
        out_shape=[
            jax.ShapeDtypeStruct((tokens, local), narrow),
            jax.ShapeDtypeStruct((tokens, width), wide),
            jax.ShapeDtypeStruct((tokens, width), narrow),
        ],
        compiler_params=pltpu.CompilerParams(vmem_limit_bytes=vmem_bytes),
        cost_estimate=busy(6),
        name="merge",
    )(own, other, w_own, w_other, inputs, norm_ffn)


def branch_back_kernel(
    own_ref,
    early_ref,
    late_ref,
    hidden_ref,
    cot_ref,
    gain_ref,
    w_ref,
    send_ref,
    hidden_grad_ref,
    branch_ref,
    gain_grad_ref,
):
    groups = 2
    other = jnp.concatenate([early_ref[...], late_ref[...]], axis=0)
    grad_normed = own_ref[...].astype(wide) + other.astype(wide)
    hidden = hidden_ref[...]
    back, gain_grad = norm_back(grad_normed, hidden, rms_scale(hidden), gain_ref[...].astype(wide)[None])
    gain_grad_ref[...] = gain_grad[None]
    grad_hidden = cot_ref[...].astype(wide) + back
    hidden_grad_ref[...] = grad_hidden
    grad_branch = grad_hidden.astype(narrow)
    branch_ref[...] = grad_branch
    attended_grad = dot_rows(grad_branch, w_ref[...])
    tokens, local = attended_grad.shape
    half = tokens // groups // 2
    for pair in range(local // LANES):
        for part in range(groups):
            cols = slice(pair * LANES, (pair + 1) * LANES)
            low = attended_grad[2 * part * half : (2 * part + 1) * half, cols]
            high = attended_grad[(2 * part + 1) * half : (2 * part + 2) * half, cols]
            for at, tile in enumerate(swap_pairs(low, high)):
                send_ref[2 * pair + at, part] = tile.astype(narrow)


def branch_back(own, early, late, hidden, cotangent, norm_ffn, w_out):
    tokens, width = hidden.shape
    local = w_out.shape[0]
    groups = 2
    return pl.pallas_call(
        branch_back_kernel,
        in_specs=[whole_spec()] * 7,
        out_specs=[whole_spec()] * 4,
        out_shape=[
            jax.ShapeDtypeStruct((local // HEAD_DIM, groups, tokens // groups // 2, LANES), narrow),
            jax.ShapeDtypeStruct((tokens, width), wide),
            jax.ShapeDtypeStruct((tokens, width), narrow),
            jax.ShapeDtypeStruct((1, width), wide),
        ],
        compiler_params=pltpu.CompilerParams(vmem_limit_bytes=vmem_bytes),
        cost_estimate=busy(6),
        name="branch_back",
    )(own, early, late, hidden, cotangent, norm_ffn, w_out)


def fold_kernel(
    part_ref, depth_ref, mine_ref, arrived_ref, dq_ref, turn_ref, send_ref, rows_ref, packed_ref
):
    count, rows, _ = mine_ref.shape
    half = rows // 2
    low = lane_ids((rows, LANES)) < HEAD_DIM
    for at, table in enumerate(turn_rows(turn_ref, part_ref[0] * rows, rows)):
        rows_ref[at] = table
        packed_ref[at] = jnp.where(low[:half], table[:half], table[half:])

    def step(slot, carry):
        depth = turn_depth(turn_ref, depth_ref[slot])
        cosine, sine = turn((rows_ref[0], rows_ref[1]), depth)
        pair = mine_ref[slot] + arrived_ref[slot].astype(wide)
        key = spin(pair, cosine, -sine)
        send_ref[slot, :rows, :] = jnp.where(low, key, pair).astype(narrow)
        cosine, sine = turn((packed_ref[0], packed_ref[1]), depth)
        send_ref[slot, rows:, :] = spin(dq_ref[slot].astype(wide), cosine, -sine).astype(narrow)
        return carry

    lax.fori_loop(0, count, step, 0, unroll=4)


def fold(part, depth_pos, mine, arrived, grad_q, turns):
    count, rows, _ = mine.shape
    return pl.pallas_call(
        fold_kernel,
        in_specs=[scalar_spec()] * 2 + [whole_spec()] * 4,
        out_specs=whole_spec(),
        out_shape=jax.ShapeDtypeStruct((count, rows + rows // 2, LANES), narrow),
        scratch_shapes=[
            pltpu.VMEM((2, rows, LANES), wide),
            pltpu.VMEM((2, rows // 2, LANES), wide),
        ],
        compiler_params=pltpu.CompilerParams(vmem_limit_bytes=vmem_bytes),
        cost_estimate=busy(6),
        name="fold",
    )(part, depth_pos, mine, arrived, grad_q, turns)


def unproject_kernel(recv_ref, wq_ref, wk_ref, wv_ref, first_ref, part_ref):
    groups = 2
    rows = recv_ref.shape[1] * 2 // 3
    heads = recv_ref.shape[0] // groups
    for part in range(groups):
        span = slice(part * rows, (part + 1) * rows)
        keys, values, queries = [], [], []
        for pair in range(heads // 2):
            cols = slice(pair * LANES, (pair + 1) * LANES)
            left = recv_ref[2 * pair * groups + part].astype(wide)
            right = recv_ref[(2 * pair + 1) * groups + part].astype(wide)
            key, value = swap_pairs(left[:rows], right[:rows])
            query = jnp.concatenate(swap_pairs(left[rows:], right[rows:]), axis=0)
            value = 0.5 * value
            first_ref[span, cols] = value
            keys.append(key.astype(narrow))
            values.append(value.astype(narrow))
            queries.append(query.astype(narrow))
        total = dot_rows(jnp.concatenate(queries, axis=1), wq_ref[...])
        total = total + dot_rows(jnp.concatenate(keys, axis=1), wk_ref[...])
        total = total + dot_rows(jnp.concatenate(values, axis=1), wv_ref[...])
        part_ref[span, :] = total.astype(narrow)


def unproject(recv, w_query, w_key, w_value):
    width, local = w_query.shape
    tokens = recv.shape[1] * 4 // 3
    return pl.pallas_call(
        unproject_kernel,
        in_specs=[whole_spec()] * 4,
        out_specs=[whole_spec()] * 2,
        out_shape=[
            jax.ShapeDtypeStruct((tokens, local), wide),
            jax.ShapeDtypeStruct((tokens, width), narrow),
        ],
        compiler_params=pltpu.CompilerParams(vmem_limit_bytes=vmem_bytes),
        cost_estimate=busy(60),
        name="unproject",
    )(recv, w_query, w_key, w_value)


def finish_kernel(
    place_ref, near_ref, far_ref, near_core_ref, far_core_ref, query_ref, key_ref, value_ref, out_ref
):
    length, size, width = near_ref.shape
    chips = 2 * length
    head_rows = 3 * HEAD_DIM // 2
    out_rows = size - head_rows
    place = place_ref[0]
    core = place % 2
    high = (place // 2) % 2

    def emit(first, second):
        for chip in range(chips):
            for at, refs in ((chip, first), (chips + chip, second)):
                rows = refs[chip % 2][chip // 2, head_rows:, :]
                out_ref[at * out_rows : (at + 1) * out_rows, :] = rows.astype(wide)

        def column(block, carry):
            cols = pl.ds(pl.multiple_of(block * LANES, LANES), LANES)
            for pair in range(chips // 2):
                pieces = [
                    jnp.concatenate(
                        [refs[chip % 2][chip // 2, :head_rows, cols] for refs in (first, second)],
                        axis=0,
                    ).astype(wide)
                    for chip in (2 * pair, 2 * pair + 1)
                ]
                for at, target in enumerate((key_ref, value_ref, query_ref)):
                    span = slice(at * HEAD_DIM, (at + 1) * HEAD_DIM)
                    both = jnp.concatenate([piece[span] for piece in pieces], axis=0)
                    target[cols, pair * LANES : (pair + 1) * LANES] = jnp.transpose(both)
            return carry

        lax.fori_loop(0, width // LANES, column, 0)

    for core_at in range(2):
        for high_at in range(2):

            @pl.when((core == core_at) & (high == high_at))
            def _(core_at=core_at, high_at=high_at):
                own = (near_ref, far_ref) if high_at == 0 else (far_ref, near_ref)
                other = (near_core_ref, far_core_ref) if high_at == 0 else (far_core_ref, near_core_ref)
                emit(own, other) if core_at == 0 else emit(other, own)


def finish(place, near, far, near_core, far_core, local):
    width = near.shape[2]
    return pl.pallas_call(
        finish_kernel,
        in_specs=[scalar_spec()] + [whole_spec()] * 4,
        out_specs=[whole_spec()] * 4,
        out_shape=[jax.ShapeDtypeStruct((width, local), wide)] * 3
        + [jax.ShapeDtypeStruct((local, width), wide)],
        compiler_params=pltpu.CompilerParams(vmem_limit_bytes=vmem_bytes),
        cost_estimate=busy(6),
        name="finish",
    )(place, near, far, near_core, far_core)


def swap_tensor(values):
    return lax.ppermute(values, "tensor", [(0, 1), (1, 0)])


def swap_bit(values, bit, count):
    return lax.ppermute(values, "dp", [(i, i ^ bit) for i in range(count)])


def add_narrow(left, right):
    return (left.astype(wide) + right.astype(wide)).astype(narrow)


def take_part(values, index, parts):
    size = values.shape[0] // parts
    return lax.dynamic_slice_in_dim(values, index * size, size, 0)


def reduce_bit(values, bit, place, count):
    mine = (place // bit) % 2
    arrived = swap_bit(take_part(values, 1 - mine, 2), bit, count)
    return add_narrow(take_part(values, mine, 2), arrived)


def side_groups(count):
    return [[chip * 2 + core for chip in range(count // 2)] for core in range(2)]


def to_chips(values, count):
    return lax.all_to_all(
        values, "dp", split_axis=0, concat_axis=0, tiled=True, axis_index_groups=side_groups(count)
    )


def spread(values, count):
    chips = count // 2
    return to_chips(jnp.broadcast_to(values[None], (chips,) + values.shape), count)


def spread_line(copies, count):
    length = count // 4
    return lax.all_to_all(
        copies,
        "dp",
        split_axis=0,
        concat_axis=0,
        tiled=True,
        axis_index_groups=[[z * 4 + rest for z in range(length)] for rest in range(4)],
    )


def gather_core(values, axis, place, count):
    mine = place % 2
    arrived = swap_bit(values, 1, count)
    row = jnp.concatenate([arrived, values, arrived], axis=axis)
    size = values.shape[axis]
    return lax.dynamic_slice_in_dim(row, (1 - mine) * size, 2 * size, axis)


def sum_over_dp(values, place, count):
    chips = count // 2
    values = reduce_bit(values, 1, place, count)
    shares = to_chips(values.reshape((chips, values.shape[0] // chips) + values.shape[1:]), count)
    total = jnp.sum(shares.astype(wide), axis=0).astype(narrow)
    whole = spread(total, count)
    whole = whole.reshape((-1,) + whole.shape[2:])
    return gather_core(whole, 0, place, count)


def reduce_z(values, place, count):
    at = place // 4
    total = take_part(values, at, 4).astype(wide)
    for step in (1, 2, 3):
        share = take_part(values, at ^ step, 4)
        total = total + swap_bit(share, 4 * step, count).astype(wide)
    return total.astype(narrow)


def gather_z(values, place, count):
    at = place // 4
    shares = [values] + [swap_bit(values, 4 * step, count) for step in (1, 2, 3)]
    row = jnp.concatenate(shares, axis=0)
    return jnp.concatenate([take_part(row, at ^ target, 4) for target in range(4)], axis=0)


def gather_bit(values, bit, place, count):
    mine = (place // bit) % 2
    arrived = swap_bit(values, bit, count)
    row = jnp.concatenate([arrived, values, arrived], axis=0)
    size = values.shape[0]
    return lax.dynamic_slice_in_dim(row, (1 - mine) * size, 2 * size, 0)


def after(value, *others):
    return lax.optimization_barrier((value,) + others)[0]


def sum_small(values, count):
    bit = 1
    while bit < count:
        values = values + swap_bit(values, bit, count)
        bit *= 2
    return values


def body_heads(
    inputs,
    first_values,
    w_query,
    w_key,
    w_value,
    w_out,
    w_gate,
    w_up,
    w_down,
    norm_attn,
    norm_ffn,
    cotangent,
    parents,
    depth_pos,
    assignment,
):
    count = parents.shape[0]
    tokens, width = inputs.shape
    local = w_query.shape[1]
    heads = local // HEAD_DIM
    groups = count // heads
    place = lax.axis_index("dp")
    part = (place % groups).astype(jnp.int32)
    part_array = part.reshape(1)

    rows = tokens // groups
    w_out_other = swap_tensor(w_out)
    turns = jnp.asarray(turn_constants())
    place_array = place.astype(jnp.int32).reshape(1)

    send, normed = project(
        place_array,
        depth_pos,
        inputs,
        norm_attn,
        first_values,
        turns,
        w_query,
        w_key,
        w_value,
        groups,
    )
    send = send.reshape(count, rows + rows // 2, LANES)
    recv = lax.all_to_all(send, "dp", split_axis=0, concat_axis=0, tiled=True)
    normed_theirs = swap_bit(take_part(normed, 1 - part, groups), 1, count)
    normed_mine = take_part(normed, part, groups)
    normed_row = jnp.concatenate([normed_theirs, normed_mine, normed_theirs], axis=0)
    normed_chip = lax.dynamic_slice_in_dim(normed_row, (1 - part) * rows, groups * rows, 0)
    side = lax.axis_index("tensor")
    quarter = rows // 2
    normed_quarter = lax.dynamic_index_in_dim(
        normed_chip.reshape(groups, 2, quarter, width), side, 1, keepdims=False
    ).reshape(groups * quarter, width)
    recv, normed_quarter = lax.optimization_barrier((recv, normed_quarter))
    normed_own = lax.all_gather(
        normed_quarter, "dp", axis=0, tiled=True, axis_index_groups=side_groups(count)
    )

    other = swap_bit(recv, 1, count)
    packed, ot, logs = attend(parents, assignment, part_array, recv, other)
    own_out = lax.all_to_all(packed, "dp", split_axis=0, concat_axis=0, tiled=True)
    other_out = swap_tensor(own_out)
    attended, hidden, normed_ffn = merge(own_out, other_out, w_out, w_out_other, inputs, norm_ffn)

    gate_proj = jnp.dot(normed_ffn, w_gate, preferred_element_type=wide)
    up_proj = jnp.dot(normed_ffn, w_up, preferred_element_type=wide)
    silu_gate = jax.nn.silu(gate_proj)
    activated = (silu_gate * up_proj).astype(narrow)
    grad_activated = jnp.einsum("td,fd->tf", cotangent, w_down, preferred_element_type=wide)
    sigmoid_gate = jax.nn.sigmoid(gate_proj)
    grad_gate = (
        grad_activated * up_proj * sigmoid_gate * (1.0 + gate_proj * (1.0 - sigmoid_gate))
    ).astype(narrow)
    grad_up = (grad_activated * silu_gate).astype(narrow)
    ffn_partial = (
        jnp.einsum("tf,df->td", grad_gate, w_gate, preferred_element_type=wide)
        + jnp.einsum("tf,df->td", grad_up, w_up, preferred_element_type=wide)
    ).astype(narrow)
    ffn_early = swap_tensor(ffn_partial[: tokens // 2])
    ffn_grads = tuple(
        jnp.einsum(form, left, right, preferred_element_type=wide).astype(narrow)
        for form, left, right in (
            ("td,tf->df", normed_ffn, grad_gate),
            ("td,tf->df", normed_ffn, grad_up),
            ("tf,td->fd", activated, cotangent),
        )
    )
    feed_partial = jnp.dot(activated, w_down, preferred_element_type=wide).astype(narrow)

    normed_own, *ffn_grads = lax.optimization_barrier((normed_own,) + ffn_grads)
    ffn_sums = lax.psum(tuple(ffn_grads), "dp")
    ffn_early = after(ffn_early, *ffn_grads)

    def way_back(ffn_early, normed_own):
        ffn_late = swap_tensor(ffn_partial[tokens // 2 :])
        grad_send, grad_hidden, grad_branch, grad_gain_ffn = branch_back(
            ffn_partial, ffn_early, ffn_late, hidden, cotangent, norm_ffn, w_out
        )
        grad_recv = lax.all_to_all(
            grad_send.reshape(count, rows // 2, LANES), "dp", split_axis=0, concat_axis=0, tiled=True
        )
        grad_w_out = jnp.einsum("tc,td->cd", attended, grad_branch, preferred_element_type=wide)
        out_half = reduce_bit(grad_w_out.astype(narrow), 1, place, count)
        grad_recv, out_half = lax.optimization_barrier((grad_recv, out_half))
        chips = count // 2
        out_shares = to_chips(out_half.reshape(chips, local // count, width), count)
        normed_other = swap_tensor(normed_own)
        feed_other = swap_tensor(after(feed_partial, normed_other))

        grad_q, mine, theirs = attend_back(
            parents, assignment, part_array, recv, other, grad_recv, ot, logs
        )
        grad_q, mine, theirs, out_shares = lax.optimization_barrier(
            (grad_q, mine, theirs, out_shares)
        )
        arrived = swap_bit(theirs, 1, count)
        back_send = fold(part_array, depth_pos, mine, arrived, grad_q, turns)
        back_recv = lax.all_to_all(back_send, "dp", split_axis=0, concat_axis=0, tiled=True)
        pairs_terms = query_terms = 0.0
        for at, normed_part in ((side, normed_own), (1 - side, normed_other)):
            pairs = lax.dynamic_slice_in_dim(back_send, at * quarter, quarter, 1)
            both = jnp.concatenate([pairs, back_send[:, rows:]], axis=2)
            terms = jnp.einsum(
                "tc,td->cd",
                both.reshape(count * quarter, 2 * LANES),
                normed_part,
                preferred_element_type=wide,
            )
            pairs_terms = pairs_terms + terms[:LANES]
            query_terms = query_terms + lax.dynamic_slice_in_dim(
                terms, LANES + at * HEAD_DIM, HEAD_DIM, 0
            )
        head_grads = jnp.concatenate(
            [pairs_terms[:HEAD_DIM], 0.5 * pairs_terms[HEAD_DIM:], query_terms], axis=0
        ).astype(narrow)
        head_share = reduce_bit(head_grads, 1, place, count)
        out_share = jnp.sum(out_shares.astype(wide), axis=0).astype(narrow)
        share = jnp.concatenate([head_share, out_share], axis=0)
        copies = jnp.broadcast_to(share[None], (count // 4,) + share.shape)
        back_recv, feed_other, copies = lax.optimization_barrier((back_recv, feed_other, copies))
        grad_first, attn_partial = unproject(back_recv, w_query, w_key, w_value)
        attn_other = swap_tensor(attn_partial)
        along = spread_line(copies, count)
        near = after(along, attn_partial)
        far = swap_bit(near, 2, count)
        near_core = swap_bit(near, 1, count)
        output = (hidden + (feed_partial.astype(wide) + feed_other.astype(wide))).astype(narrow)
        inputs_wide = inputs.astype(wide)
        grad_normed = attn_partial.astype(wide) + attn_other.astype(wide)
        grad_input_norm, grad_gain_attn = norm_back(
            grad_normed, inputs_wide, rms_scale(inputs_wide), norm_attn.astype(wide)
        )
        grad_inputs = grad_hidden + grad_input_norm
        gains = sum_small(jnp.stack([grad_gain_attn, grad_gain_ffn[0]]), count)
        far_core = swap_bit(after(far, gains, grad_inputs, output), 1, count)
        return output, grad_inputs, grad_first, gains, near, far, near_core, far_core

    def no_tree(*operands):
        shapes = jax.eval_shape(way_back, *operands)
        return tuple(jnp.zeros(leaf.shape, leaf.dtype) for leaf in shapes)

    output, grad_inputs, grad_first, gains, near, far, near_core, far_core = lax.cond(
        parents[0] < 0, way_back, no_tree, ffn_early, normed_own
    )
    head_query, head_key, head_value, sum_w_out = finish(
        place_array, near, far, near_core, far_core, local
    )
    sums = [after(term, sum_w_out).astype(wide) for term in ffn_sums]
    return (
        output,
        grad_inputs,
        grad_first,
        head_query,
        head_key,
        head_value,
        sum_w_out,
        sums[0],
        sums[1],
        sums[2],
        gains[0],
        gains[1],
    )


def pick_body(mesh):
    if mesh.shape["dp"] == 16 and mesh.shape["tensor"] == 2:
        return body_heads
    return body_general


def solution(mesh):
    placed = (
        P("dp", None),
        P("dp", "tensor"),
        P(None, "tensor"),
        P(None, "tensor"),
        P(None, "tensor"),
        P("tensor", None),
        P(None, "tensor"),
        P(None, "tensor"),
        P("tensor", None),
        P(),
        P(),
        P("dp", None),
        P(),
        P(),
        P(),
    )
    return jax.shard_map(
        pick_body(mesh),
        mesh=mesh,
        in_specs=placed,
        out_specs=(
            P("dp", None),
            P("dp", None),
            P("dp", "tensor"),
            P(None, "tensor"),
            P(None, "tensor"),
            P(None, "tensor"),
            P("tensor", None),
            P(None, "tensor"),
            P(None, "tensor"),
            P("tensor", None),
            P(),
            P(),
        ),
        check_vma=False,
    )
```

```python
import jax
import jax.numpy as jnp
import numpy as np
from jax import lax
from jax.experimental import pallas as pl
from jax.experimental.pallas import tpu as pltpu
from jax.sharding import PartitionSpec as P

HEAD_DIM = 64
SEG = 512


epsilon = 1e-06
rope_base = 10000.0
climb_steps = 5
masked_score = -1e30


def rms_scale(values):
    return lax.rsqrt(jnp.mean(values * values, axis=-1, keepdims=True) + epsilon)


def rotary_tables(positions, head_dim):
    half_dim = head_dim // 2
    frequency = rope_base ** (-jnp.arange(half_dim, dtype=jnp.float32) * 2.0 / head_dim)
    angles = positions.astype(jnp.float32)[:, None] * frequency[None, :]
    return (jnp.cos(angles)[:, None, :], jnp.sin(angles)[:, None, :])


def rotate(values, cosine, sine_table):
    half_dim = values.shape[-1] // 2
    first_half = values[..., :half_dim]
    second_half = values[..., half_dim:]
    return jnp.concatenate(
        [
            first_half * cosine - second_half * sine_table,
            second_half * cosine + first_half * sine_table,
        ],
        axis=-1,
    )


def rotate_back(gradient, cosine, sine_table):
    half_dim = gradient.shape[-1] // 2
    first_half = gradient[..., :half_dim]
    second_half = gradient[..., half_dim:]
    return jnp.concatenate(
        [
            first_half * cosine + second_half * sine_table,
            second_half * cosine - first_half * sine_table,
        ],
        axis=-1,
    )


def parent_slots(parents, assignment):
    count = parents.shape[0]
    slot_ids = jnp.arange(count, dtype=jnp.int32)
    at_slot = assignment[None, :] == slot_ids[:, None]
    parent_seg = jnp.sum(jnp.where(at_slot, parents[None, :], 0), axis=1)
    parent_match = slot_ids[None, :] == parent_seg[:, None]
    above_slot = jnp.sum(jnp.where(parent_match, assignment[None, :], 0), axis=1)
    return jnp.where(parent_seg >= 0, above_slot, -1)


def climb(parent_slot, start_slots):
    slot_ids = jnp.arange(parent_slot.shape[0], dtype=jnp.int32)
    levels = [start_slots]
    current = start_slots
    for step_index in range(climb_steps):
        matched = current[:, None] == slot_ids[None, :]
        upward = jnp.sum(jnp.where(matched, parent_slot[None, :], 0), axis=1)
        current = jnp.where(current >= 0, upward, -1)
        levels.append(current)
    return jnp.stack(levels, axis=1)


def norm_back(grad_normed, values, row_scale, gain_vector):
    scaled_grad = grad_normed * gain_vector
    grad_gain = jnp.sum(grad_normed * values * row_scale, axis=0)
    grad_values = row_scale * (
        scaled_grad
        - values * row_scale * row_scale * jnp.mean(scaled_grad * values, axis=-1, keepdims=True)
    )
    return (grad_values, grad_gain)


def path_rows(source, path_row):
    parts = []
    for level_index in range(climb_steps + 1):
        row_begin = (jnp.maximum(path_row[level_index], 0) * SEG).astype(jnp.int32)
        parts.append(lax.dynamic_slice_in_dim(source, row_begin, SEG, 0))
    return jnp.concatenate(parts, axis=0)


def path_permit(path_row, causal):
    parts = [causal]
    for level_index in range(1, climb_steps + 1):
        parts.append(jnp.broadcast_to(path_row[level_index] >= 0, (SEG, SEG)))
    return jnp.concatenate(parts, axis=1)


def body_general(
    inputs,
    first_values,
    w_query,
    w_key,
    w_value,
    w_out,
    w_gate,
    w_up,
    w_down,
    norm_attn,
    norm_ffn,
    cotangent,
    parents,
    depth_pos,
    assignment,
):
    row_count = inputs.shape[0]
    local_width = w_query.shape[1]
    head_count = local_width // HEAD_DIM
    score_scale = HEAD_DIM ** (-0.5)
    seg_count = row_count // SEG
    slot_total = parents.shape[0]
    slot_ids = jnp.arange(slot_total, dtype=jnp.int32)
    local_rows = jnp.arange(row_count, dtype=jnp.int32)
    own_slots = lax.axis_index("dp") * seg_count + jnp.arange(seg_count, dtype=jnp.int32)
    own_slot_rows = jnp.repeat(own_slots, SEG)
    depth_rows = jnp.sum(
        jnp.where(own_slot_rows[:, None] == slot_ids[None, :], depth_pos[None, :], 0), axis=1
    )
    positions = depth_rows + local_rows % SEG
    parent_slot = parent_slots(parents, assignment)
    own_paths = climb(parent_slot, own_slots)
    offsets = jnp.arange(SEG, dtype=jnp.int32)
    causal = offsets[None, :] <= offsets[:, None]
    cosine, sine_table = rotary_tables(positions, HEAD_DIM)
    inputs_wide = inputs.astype(jnp.float32)
    attn_scale = rms_scale(inputs_wide)
    gain_attn = norm_attn.astype(jnp.float32)
    normed = (inputs_wide * attn_scale * gain_attn).astype(jnp.bfloat16)
    query_proj = jnp.dot(normed, w_query, preferred_element_type=jnp.float32)
    key_proj = jnp.dot(normed, w_key, preferred_element_type=jnp.float32)
    value_proj = jnp.dot(normed, w_value, preferred_element_type=jnp.float32)
    query_rot = rotate(
        query_proj.reshape(row_count, head_count, HEAD_DIM), cosine, sine_table
    ).astype(jnp.bfloat16)
    key_rot = (
        rotate(key_proj.reshape(row_count, head_count, HEAD_DIM), cosine, sine_table)
        .astype(jnp.bfloat16)
        .reshape(row_count, local_width)
    )
    mixed = (0.5 * value_proj + 0.5 * first_values.astype(jnp.float32)).astype(jnp.bfloat16)
    key_all, value_all = (
        lax.all_gather(key_rot, "dp", axis=0, tiled=True),
        lax.all_gather(mixed, "dp", axis=0, tiled=True),
    )
    query_segs = query_rot.reshape(seg_count, SEG, head_count, HEAD_DIM)

    def segment_forward(operand):
        query_block, path_row = operand
        near_keys = path_rows(key_all, path_row).reshape(-1, head_count, HEAD_DIM)
        near_values = path_rows(value_all, path_row).reshape(-1, head_count, HEAD_DIM)
        permit = path_permit(path_row, causal)
        scores = (
            jnp.einsum("qhd,khd->hqk", query_block, near_keys, preferred_element_type=jnp.float32)
            * score_scale
        )
        scores = jnp.where(permit[None], scores, masked_score)
        row_max = jnp.max(scores, axis=-1)
        weights = jnp.where(permit[None], jnp.exp(scores - row_max[..., None]), 0.0)
        row_total = jnp.sum(weights, axis=-1)
        attn_probs = weights / row_total[..., None]
        block_out = jnp.einsum(
            "hqk,khd->qhd",
            attn_probs.astype(jnp.bfloat16),
            near_values,
            preferred_element_type=jnp.float32,
        )
        return (block_out, row_max + jnp.log(row_total))

    attn_parts, log_parts = lax.map(segment_forward, (query_segs, own_paths))
    attn_exact = attn_parts.reshape(row_count, head_count, HEAD_DIM)
    attended = attn_exact.reshape(row_count, local_width).astype(jnp.bfloat16)
    branch_attn = lax.psum(
        jnp.dot(attended, w_out, preferred_element_type=jnp.float32).astype(jnp.bfloat16), "tensor"
    ).astype(jnp.float32)
    hidden_state = inputs_wide + branch_attn
    ffn_scale = rms_scale(hidden_state)
    gain_ffn = norm_ffn.astype(jnp.float32)
    normed_ffn = (hidden_state * ffn_scale * gain_ffn).astype(jnp.bfloat16)
    gate_proj = jnp.dot(normed_ffn, w_gate, preferred_element_type=jnp.float32)
    up_proj = jnp.dot(normed_ffn, w_up, preferred_element_type=jnp.float32)
    silu_gate = jax.nn.silu(gate_proj)
    activated = (silu_gate * up_proj).astype(jnp.bfloat16)
    feed = lax.psum(
        jnp.dot(activated, w_down, preferred_element_type=jnp.float32).astype(jnp.bfloat16),
        "tensor",
    ).astype(jnp.float32)
    output = (hidden_state + feed).astype(jnp.bfloat16)
    grad_w_down = jnp.einsum("tf,td->fd", activated, cotangent, preferred_element_type=jnp.float32)
    grad_activated = jnp.einsum("td,fd->tf", cotangent, w_down, preferred_element_type=jnp.float32)
    sigmoid_gate = jax.nn.sigmoid(gate_proj)
    grad_gate = (
        grad_activated * up_proj * sigmoid_gate * (1.0 + gate_proj * (1.0 - sigmoid_gate))
    ).astype(jnp.bfloat16)
    grad_up = (grad_activated * silu_gate).astype(jnp.bfloat16)
    grad_w_gate = jnp.einsum("td,tf->df", normed_ffn, grad_gate, preferred_element_type=jnp.float32)
    grad_w_up = jnp.einsum("td,tf->df", normed_ffn, grad_up, preferred_element_type=jnp.float32)
    ffn_partial = jnp.einsum(
        "tf,df->td", grad_gate, w_gate, preferred_element_type=jnp.float32
    ) + jnp.einsum("tf,df->td", grad_up, w_up, preferred_element_type=jnp.float32)
    grad_normed_ffn = lax.psum(ffn_partial.astype(jnp.bfloat16), "tensor").astype(jnp.float32)
    grad_hidden_norm, grad_gain_ffn = norm_back(grad_normed_ffn, hidden_state, ffn_scale, gain_ffn)
    grad_hidden = cotangent.astype(jnp.float32) + grad_hidden_norm
    grad_branch = grad_hidden.astype(jnp.bfloat16)
    grad_w_out = jnp.einsum("tc,td->cd", attended, grad_branch, preferred_element_type=jnp.float32)
    grad_attended = jnp.einsum(
        "td,cd->tc", grad_branch, w_out, preferred_element_type=jnp.float32
    ).astype(jnp.bfloat16)
    grad_heads = grad_attended.reshape(row_count, head_count, HEAD_DIM)
    delta_rows = jnp.sum(grad_heads.astype(jnp.float32) * attn_exact, axis=-1)
    delta_parts = jnp.transpose(delta_rows.reshape(seg_count, SEG, head_count), (0, 2, 1))
    grad_segs = grad_heads.reshape(seg_count, SEG, head_count, HEAD_DIM)
    key_back, value_back = (key_all, value_all)

    def segment_back(query_block, grad_block, path_row, log_block, delta_block):
        near_keys = path_rows(key_back, path_row).reshape(-1, head_count, HEAD_DIM)
        near_values = path_rows(value_back, path_row).reshape(-1, head_count, HEAD_DIM)
        permit = path_permit(path_row, causal)
        scores = (
            jnp.einsum("qhd,khd->hqk", query_block, near_keys, preferred_element_type=jnp.float32)
            * score_scale
        )
        scores = jnp.where(permit[None], scores, masked_score)
        attn_probs = jnp.where(permit[None], jnp.exp(scores - log_block[..., None]), 0.0)
        grad_probs = jnp.einsum(
            "qhd,khd->hqk", grad_block, near_values, preferred_element_type=jnp.float32
        )
        grad_scores = (attn_probs * (grad_probs - delta_block[..., None])).astype(jnp.bfloat16)
        grad_part = (
            jnp.einsum("hqk,khd->qhd", grad_scores, near_keys, preferred_element_type=jnp.float32)
            * score_scale
        )
        return (attn_probs, grad_scores, grad_part)

    zero_rows = jnp.zeros((key_back.shape[0], local_width), jnp.float32)

    def scatter_step(fold_state, operand):
        key_acc, value_acc = fold_state
        query_block, grad_block, path_row, log_block, delta_block = operand
        attn_probs, grad_scores, grad_part = segment_back(
            query_block, grad_block, path_row, log_block, delta_block
        )
        key_term = (
            jnp.einsum("hqk,qhd->khd", grad_scores, query_block, preferred_element_type=jnp.float32)
            * score_scale
        ).reshape(climb_steps + 1, SEG, local_width)
        value_term = jnp.einsum(
            "hqk,qhd->khd",
            attn_probs.astype(jnp.bfloat16),
            grad_block,
            preferred_element_type=jnp.float32,
        ).reshape(climb_steps + 1, SEG, local_width)
        for level_index in range(climb_steps + 1):
            row_begin = (jnp.maximum(path_row[level_index], 0) * SEG).astype(jnp.int32)
            key_acc = lax.dynamic_update_slice_in_dim(
                key_acc,
                lax.dynamic_slice_in_dim(key_acc, row_begin, SEG, 0) + key_term[level_index],
                row_begin,
                0,
            )
            value_acc = lax.dynamic_update_slice_in_dim(
                value_acc,
                lax.dynamic_slice_in_dim(value_acc, row_begin, SEG, 0) + value_term[level_index],
                row_begin,
                0,
            )
        return ((key_acc, value_acc), grad_part)

    (key_terms, value_terms), grad_parts = lax.scan(
        scatter_step,
        (zero_rows, zero_rows),
        (query_segs, grad_segs, own_paths, log_parts, delta_parts),
    )
    grad_query_rot = grad_parts.reshape(row_count, head_count, HEAD_DIM)
    key_sums, value_sums = (
        lax.psum_scatter(
            key_terms.astype(jnp.bfloat16), "dp", scatter_dimension=0, tiled=True
        ).astype(jnp.float32),
        lax.psum_scatter(
            value_terms.astype(jnp.bfloat16), "dp", scatter_dimension=0, tiled=True
        ).astype(jnp.float32),
    )
    grad_key_rot = key_sums.reshape(row_count, head_count, HEAD_DIM)
    grad_first_values = 0.5 * value_sums
    grad_value = (0.5 * value_sums).astype(jnp.bfloat16)
    grad_key = (
        rotate_back(grad_key_rot, cosine, sine_table)
        .reshape(row_count, local_width)
        .astype(jnp.bfloat16)
    )
    grad_query = (
        rotate_back(grad_query_rot, cosine, sine_table)
        .reshape(row_count, local_width)
        .astype(jnp.bfloat16)
    )
    grad_w_query = jnp.einsum("td,tc->dc", normed, grad_query, preferred_element_type=jnp.float32)
    grad_w_key = jnp.einsum("td,tc->dc", normed, grad_key, preferred_element_type=jnp.float32)
    grad_w_value = jnp.einsum("td,tc->dc", normed, grad_value, preferred_element_type=jnp.float32)
    attn_partial = (
        jnp.einsum("tc,dc->td", grad_query, w_query, preferred_element_type=jnp.float32)
        + jnp.einsum("tc,dc->td", grad_key, w_key, preferred_element_type=jnp.float32)
        + jnp.einsum("tc,dc->td", grad_value, w_value, preferred_element_type=jnp.float32)
    )
    grad_normed = lax.psum(attn_partial.astype(jnp.bfloat16), "tensor").astype(jnp.float32)
    grad_input_norm, grad_gain_attn = norm_back(grad_normed, inputs_wide, attn_scale, gain_attn)
    grad_inputs = grad_hidden + grad_input_norm
    summed = (
        lax.psum(grad_w_query.astype(jnp.bfloat16), "dp").astype(jnp.float32),
        lax.psum(grad_w_key.astype(jnp.bfloat16), "dp").astype(jnp.float32),
        lax.psum(grad_w_value.astype(jnp.bfloat16), "dp").astype(jnp.float32),
        lax.psum(grad_w_out.astype(jnp.bfloat16), "dp").astype(jnp.float32),
        lax.psum(grad_w_gate.astype(jnp.bfloat16), "dp").astype(jnp.float32),
        lax.psum(grad_w_up.astype(jnp.bfloat16), "dp").astype(jnp.float32),
        lax.psum(grad_w_down.astype(jnp.bfloat16), "dp").astype(jnp.float32),
        lax.psum(grad_gain_attn.astype(jnp.bfloat16), "dp").astype(jnp.float32),
        lax.psum(grad_gain_ffn.astype(jnp.bfloat16), "dp").astype(jnp.float32),
    )
    return (
        output,
        grad_inputs,
        grad_first_values,
        summed[0],
        summed[1],
        summed[2],
        summed[3],
        summed[4],
        summed[5],
        summed[6],
        summed[7],
        summed[8],
    )


TREE = 16
TREE_DEPTHS = (0, 1, 2, 3, 4, 4, 4, 4, 5, 5, 5, 5, 5, 5, 5, 5)
LANES = 128
wide = jnp.float32
narrow = jnp.bfloat16
vmem_bytes = 60 * 1024 * 1024
safe_excess = 40.0


def busy(microseconds):
    return pl.CostEstimate(
        flops=int(microseconds * 1e9), bytes_accessed=int(microseconds * 2e6), transcendentals=0
    )


def lane_ids(shape):
    return lax.broadcasted_iota(jnp.int32, shape, len(shape) - 1)


def swap_pairs(left, right):
    low = lane_ids(left.shape) < HEAD_DIM
    first = jnp.where(low, left, pltpu.roll(right, HEAD_DIM, 1))
    second = jnp.where(low, pltpu.roll(left, HEAD_DIM, 1), right)
    return first, second


def spin(values, cosine, signed_sine):
    half = HEAD_DIM // 2
    ahead = pltpu.roll(values, LANES - half, 1)
    behind = pltpu.roll(values, half, 1)
    other = jnp.where(lane_ids(values.shape) % HEAD_DIM < half, ahead, behind)
    return values * cosine + other * signed_sine


def turn_constants():
    half = HEAD_DIM // 2
    lanes = np.arange(LANES)
    frequency = rope_base ** (-(lanes % half).astype(np.float64) * 2.0 / HEAD_DIM)
    sign = np.where(lanes % HEAD_DIM < half, -1.0, 1.0)
    levels = -(-(climb_steps + 1) // 8) * 8
    at = np.concatenate([np.arange(16), 16 * np.arange(SEG // 16), SEG * np.arange(levels)])
    angles = at[:, None].astype(np.float64) * frequency[None, :]
    return np.stack([np.cos(angles), np.sin(angles) * sign[None, :]]).astype(np.float32)


def turn(one, other):
    return one[0] * other[0] - one[1] * other[1], one[1] * other[0] + one[0] * other[1]


def turn_rows(turn_ref, first, rows):
    fine = turn_ref[0, :16, :], turn_ref[1, :16, :]
    parts = []
    for block in range(rows // 16):
        at = 16 + first // 16 + block
        coarse = turn_ref[0, pl.ds(at, 1), :], turn_ref[1, pl.ds(at, 1), :]
        parts.append(turn(fine, coarse))
    return tuple(jnp.concatenate(pieces, axis=0) for pieces in zip(*parts, strict=True))


def turn_depth(turn_ref, depth_pos):
    at = 16 + SEG // 16 + depth_pos // SEG
    return turn_ref[0, pl.ds(at, 1), :], turn_ref[1, pl.ds(at, 1), :]


def dot_wide(left, right):
    return jnp.dot(left, right, preferred_element_type=wide)


def dot_rows(left, right):
    return lax.dot_general(left, right, (((1,), (1,)), ((), ())), preferred_element_type=wide)


def whole_spec():
    return pl.BlockSpec(memory_space=pltpu.VMEM)


def scalar_spec():
    return pl.BlockSpec(memory_space=pltpu.SMEM)


def project_kernel(
    place_ref,
    depth_ref,
    x_ref,
    gain_ref,
    first_ref,
    turn_ref,
    wq_ref,
    wk_ref,
    wv_ref,
    send_ref,
    normed_ref,
):
    rows = x_ref.shape[0]
    pairs = first_ref.shape[1] // LANES
    x = x_ref[...].astype(wide)
    normed = (x * rms_scale(x) * gain_ref[...].astype(wide)[None]).astype(narrow)
    normed_ref[...] = normed
    query = dot_wide(normed, wq_ref[...]) * (HEAD_DIM ** (-0.5))
    key = dot_wide(normed, wk_ref[...])
    value = dot_wide(normed, wv_ref[...])
    mixed = 0.5 * value + 0.5 * first_ref[...].astype(wide)
    local = turn_rows(turn_ref, pl.program_id(0) * rows, rows)
    cosine, sine = turn(local, turn_depth(turn_ref, depth_ref[place_ref[0]]))
    for pair in range(pairs):
        cols = slice(pair * LANES, (pair + 1) * LANES)
        q = spin(query[:, cols], cosine, sine)
        k = spin(key[:, cols], cosine, sine)
        for at, tile in enumerate(swap_pairs(k, mixed[:, cols])):
            send_ref[2 * pair + at, 0, :rows, :] = tile.astype(narrow)
        for at, tile in enumerate(swap_pairs(q[: rows // 2], q[rows // 2 :])):
            send_ref[2 * pair + at, 0, rows:, :] = tile.astype(narrow)


def project(place, depth_pos, inputs, norm_attn, first_values, turns, w_query, w_key, w_value, groups):
    rows, width = inputs.shape
    local = w_query.shape[1]
    part = rows // groups
    heads = local // HEAD_DIM
    fixed = lambda step: (0, 0)
    moving = lambda step: (step, 0)
    return pl.pallas_call(
        project_kernel,
        grid=(groups,),
        in_specs=[
            scalar_spec(),
            scalar_spec(),
            pl.BlockSpec((part, width), moving),
            pl.BlockSpec((width,), lambda step: (0,)),
            pl.BlockSpec((part, local), moving),
            pl.BlockSpec(turns.shape, lambda step: (0, 0, 0)),
            pl.BlockSpec((width, local), fixed),
            pl.BlockSpec((width, local), fixed),
            pl.BlockSpec((width, local), fixed),
        ],
        out_specs=[
            pl.BlockSpec((heads, 1, part + part // 2, LANES), lambda step: (0, step, 0, 0)),
            pl.BlockSpec((part, width), moving),
        ],
        out_shape=[
            jax.ShapeDtypeStruct((heads, groups, part + part // 2, LANES), narrow),
            jax.ShapeDtypeStruct((rows, width), narrow),
        ],
        compiler_params=pltpu.CompilerParams(vmem_limit_bytes=vmem_bytes),
        cost_estimate=busy(6),
        name="project",
    )(place, depth_pos, inputs, norm_attn, first_values, turns, w_query, w_key, w_value)


def tree_walk(run, count, unroll):
    for base in range(0, count, TREE):
        at = 0
        while at < TREE:
            same = 1
            while at + same < TREE and TREE_DEPTHS[at + same] == TREE_DEPTHS[at]:
                same += 1
            depth = TREE_DEPTHS[at]
            if same == 1:
                run(base + at, depth)
            else:
                def step(i, carry, start=base + at, depth=depth):
                    run(start + i, depth)
                    return carry

                lax.fori_loop(0, same, step, 0, unroll=unroll)
            at += same


def path_of(parents_ref, assign_ref, segment, depth):
    slots = [assign_ref[segment]]
    current = segment
    for _ in range(depth):
        current = parents_ref[current]
        slots.append(assign_ref[current])
    return slots


def unpack_low(packed):
    values = packed.astype(wide)
    low = lane_ids(values.shape) < HEAD_DIM
    top = jnp.where(low, values, 0.0)
    bottom = jnp.where(low, pltpu.roll(values, HEAD_DIM, 1), 0.0)
    return jnp.concatenate([top, bottom], axis=0).astype(narrow)


def unpack_high(packed):
    values = packed.astype(wide)
    high = lane_ids(values.shape) >= HEAD_DIM
    top = jnp.where(high, pltpu.roll(values, HEAD_DIM, 1), 0.0)
    bottom = jnp.where(high, values, 0.0)
    return jnp.concatenate([top, bottom], axis=0).astype(narrow)


def pack_columns(transposed):
    half = transposed.shape[1] // 2
    stacked = jnp.concatenate([transposed[:, :half], transposed[:, half:]], axis=0)
    return jnp.transpose(stacked)


def gather_parts(part, recv_ref, other_ref, kv_ref, kvt_ref, lanes):
    rows = other_ref.shape[1] * 2 // 3

    def fill(slot, carry):
        kv_ref[slot, pl.ds(pl.multiple_of(part * rows, rows), rows), :] = recv_ref[slot, :rows, :]
        kv_ref[slot, pl.ds(pl.multiple_of((1 - part) * rows, rows), rows), :] = other_ref[slot, :rows, :]
        flipped = jnp.transpose(kv_ref[slot].astype(wide))
        kvt_ref[slot] = flipped[lanes].astype(narrow)
        return carry

    lax.fori_loop(0, recv_ref.shape[0], fill, 0)


def visible(part, keys, rows):
    key_row = lax.broadcasted_iota(jnp.int32, (keys, rows), 0)
    query_row = lax.broadcasted_iota(jnp.int32, (keys, rows), 1) + part * rows
    return key_row <= query_row


def fold_rows(values, combine):
    blocks = values.reshape(values.shape[0] // 8, 8, values.shape[1])
    return combine(blocks, axis=0)


def attend_kernel(
    parents_ref,
    assign_ref,
    part_ref,
    recv_ref,
    other_ref,
    send_ref,
    ot_ref,
    log_ref,
    kv_ref,
    vt_ref,
    excess_ref,
):
    part = part_ref[0]
    rows = other_ref.shape[1] * 2 // 3
    count = recv_ref.shape[0]
    gather_parts(part, recv_ref, other_ref, kv_ref, vt_ref, slice(HEAD_DIM, LANES))
    excess_ref[...] = jnp.zeros_like(excess_ref)

    def own_scores(own, query):
        block = dot_rows(kv_ref[own], query)
        return jnp.where(visible(part, SEG, rows), block, masked_score)

    def store(own, peak, total, mixed):
        mixed = mixed / total
        ot_ref[own] = mixed
        log_ref[own] = jnp.broadcast_to(peak + jnp.log(total), (8, rows))
        send_ref[own] = pack_columns(mixed).astype(narrow)

    def run(segment, depth):
        slots = path_of(parents_ref, assign_ref, segment, depth)
        own = slots[0]
        query = unpack_low(recv_ref[own, rows:, :])
        block = own_scores(own, query)
        peak = jnp.max(block, axis=0, keepdims=True)
        weight = jnp.exp(block - peak)
        total = fold_rows(weight, jnp.sum)
        mixed = dot_wide(vt_ref[own], weight.astype(narrow))
        crest = jnp.broadcast_to(peak, (8, rows))
        for slot in slots[1:]:
            block = dot_rows(kv_ref[slot], query)
            crest = jnp.maximum(crest, fold_rows(block, jnp.max))
            weight = jnp.exp(block - peak)
            total = total + fold_rows(weight, jnp.sum)
            mixed = mixed + dot_wide(vt_ref[slot], weight.astype(narrow))
        excess_ref[...] = jnp.maximum(excess_ref[...], crest - peak)
        store(own, peak, jnp.sum(total, axis=0, keepdims=True), mixed)

    tree_walk(run, count, 2)

    @pl.when(jnp.max(excess_ref[...]) > safe_excess)
    def _():
        def again(segment, carry):
            own = assign_ref[segment]
            query = unpack_low(recv_ref[own, rows:, :])

            def climb_up(state):
                current, peak, total, mixed = state
                current = parents_ref[current]
                slot = assign_ref[current]
                block = dot_rows(kv_ref[slot], query)
                crest = jnp.maximum(peak, jnp.max(block, axis=0, keepdims=True))
                fade = jnp.exp(peak - crest)
                weight = jnp.exp(block - crest)
                total = total * fade + jnp.sum(weight, axis=0, keepdims=True)
                mixed = mixed * fade + dot_wide(vt_ref[slot], weight.astype(narrow))
                return current, crest, total, mixed

            block = own_scores(own, query)
            peak = jnp.max(block, axis=0, keepdims=True)
            weight = jnp.exp(block - peak)
            total = jnp.sum(weight, axis=0, keepdims=True)
            mixed = dot_wide(vt_ref[own], weight.astype(narrow))
            _, peak, total, mixed = lax.while_loop(
                lambda state: parents_ref[state[0]] >= 0, climb_up, (segment, peak, total, mixed)
            )
            store(own, peak, total, mixed)
            return carry

        lax.fori_loop(0, count, again, 0)


def attend(parents, assignment, part, recv, other):
    count, rows = other.shape[0], other.shape[1] * 2 // 3
    return pl.pallas_call(
        attend_kernel,
        in_specs=[scalar_spec()] * 3 + [whole_spec()] * 2,
        out_specs=[whole_spec()] * 3,
        out_shape=[
            jax.ShapeDtypeStruct((count, rows // 2, LANES), narrow),
            jax.ShapeDtypeStruct((count, HEAD_DIM, rows), wide),
            jax.ShapeDtypeStruct((count, 8, rows), wide),
        ],
        scratch_shapes=[
            pltpu.VMEM((count, SEG, LANES), narrow),
            pltpu.VMEM((count, HEAD_DIM, SEG), narrow),
            pltpu.VMEM((8, rows), wide),
        ],
        compiler_params=pltpu.CompilerParams(vmem_limit_bytes=vmem_bytes),
        cost_estimate=busy(22),
        name="attend",
    )(parents, assignment, part, recv, other)


def attend_back_kernel(
    parents_ref,
    assign_ref,
    part_ref,
    recv_ref,
    other_ref,
    grad_ref,
    ot_ref,
    log_ref,
    dq_ref,
    mine_ref,
    theirs_ref,
    kv_ref,
    kt_ref,
    sum_ref,
):
    part = part_ref[0]
    rows = other_ref.shape[1] * 2 // 3
    count = recv_ref.shape[0]
    gather_parts(part, recv_ref, other_ref, kv_ref, kt_ref, slice(0, HEAD_DIM))

    def clear(slot, carry):
        sum_ref[slot] = jnp.zeros((SEG, LANES), wide)
        return carry

    lax.fori_loop(0, count, clear, 0)

    def run(segment, depth):
        slots = path_of(parents_ref, assign_ref, segment, depth)
        own = slots[0]
        query = unpack_low(recv_ref[own, rows:, :])
        packed = grad_ref[own]
        grad = unpack_high(packed)
        flipped = jnp.transpose(packed.astype(wide))
        grad_t = jnp.concatenate([flipped[:HEAD_DIM], flipped[HEAD_DIM:]], axis=1)
        delta = jnp.sum(grad_t * ot_ref[own], axis=0, keepdims=True)
        log_row = log_ref[own][:1]
        grad_query = jnp.zeros((HEAD_DIM, rows), wide)
        for level, slot in enumerate(slots):
            pair = kv_ref[slot]
            probs = jnp.exp(dot_rows(pair, query) - log_row)
            if level == 0:
                probs = jnp.where(visible(part, SEG, rows), probs, 0.0)
            grad_probs = dot_rows(pair, grad)
            grad_scores = (probs * (grad_probs - delta)).astype(narrow)
            sum_ref[slot] += dot_wide(grad_scores, query) + dot_wide(probs.astype(narrow), grad)
            grad_query = grad_query + dot_wide(kt_ref[slot], grad_scores)
        dq_ref[own] = pack_columns(grad_query * (HEAD_DIM ** (-0.5))).astype(narrow)

    tree_walk(run, count, 2)

    def finish(slot, carry):
        mine_ref[slot] = sum_ref[slot, pl.ds(pl.multiple_of(part * rows, rows), rows), :]
        theirs = sum_ref[slot, pl.ds(pl.multiple_of((1 - part) * rows, rows), rows), :]
        theirs_ref[slot] = theirs.astype(narrow)
        return carry

    lax.fori_loop(0, count, finish, 0)


def attend_back(parents, assignment, part, recv, other, grad, ot, logs):
    count, rows = other.shape[0], other.shape[1] * 2 // 3
    return pl.pallas_call(
        attend_back_kernel,
        in_specs=[scalar_spec()] * 3 + [whole_spec()] * 5,
        out_specs=[whole_spec()] * 3,
        out_shape=[
            jax.ShapeDtypeStruct((count, rows // 2, LANES), narrow),
            jax.ShapeDtypeStruct((count, rows, LANES), wide),
            jax.ShapeDtypeStruct((count, rows, LANES), narrow),
        ],
        scratch_shapes=[
            pltpu.VMEM((count, SEG, LANES), narrow),
            pltpu.VMEM((count, HEAD_DIM, SEG), narrow),
            pltpu.VMEM((count, SEG, LANES), wide),
        ],
        compiler_params=pltpu.CompilerParams(vmem_limit_bytes=vmem_bytes),
        cost_estimate=busy(37),
        name="attend_back",
    )(parents, assignment, part, recv, other, grad, ot, logs)


def heads_to_rows(recv_ref, groups):
    half = recv_ref.shape[1]
    heads = recv_ref.shape[0] // groups
    strips = []
    for pair in range(heads // 2):
        pieces = []
        for part in range(groups):
            left = recv_ref[2 * pair * groups + part].astype(wide)
            right = recv_ref[(2 * pair + 1) * groups + part].astype(wide)
            pieces += list(swap_pairs(left, right))
        strips.append(jnp.concatenate(pieces, axis=0))
    return jnp.concatenate(strips, axis=1).astype(narrow)


def merge_kernel(
    own_ref, other_ref, w_own_ref, w_other_ref, x_ref, gain_ref, attended_ref, hidden_ref, normed_ref, theirs_ref
):
    groups = 2
    attended_ref[...] = heads_to_rows(own_ref, groups)
    theirs_ref[...] = heads_to_rows(other_ref, groups)
    size = own_ref.shape[1]

    def step(block, carry):
        span = pl.ds(pl.multiple_of(block * size, size), size)
        branch = dot_wide(attended_ref[span, :], w_own_ref[...]).astype(narrow).astype(wide)
        branch = branch + dot_wide(theirs_ref[span, :], w_other_ref[...]).astype(narrow).astype(wide)
        hidden = x_ref[span, :].astype(wide) + branch
        hidden_ref[span, :] = hidden
        normed = hidden * rms_scale(hidden) * gain_ref[...].astype(wide)[None]
        normed_ref[span, :] = normed.astype(narrow)
        return carry

    lax.fori_loop(0, 2 * groups, step, 0)


def merge(own, other, w_own, w_other, inputs, norm_ffn):
    tokens, width = inputs.shape
    local = w_own.shape[0]
    return pl.pallas_call(
        merge_kernel,
        in_specs=[whole_spec()] * 6,
        out_specs=[whole_spec()] * 3,
        out_shape=[
            jax.ShapeDtypeStruct((tokens, local), narrow),
            jax.ShapeDtypeStruct((tokens, width), wide),
            jax.ShapeDtypeStruct((tokens, width), narrow),
        ],
        scratch_shapes=[pltpu.VMEM((tokens, local), narrow)],
        compiler_params=pltpu.CompilerParams(vmem_limit_bytes=vmem_bytes),
        cost_estimate=busy(6),
        name="merge",
    )(own, other, w_own, w_other, inputs, norm_ffn)


def branch_back_kernel(
    own_ref,
    early_ref,
    late_ref,
    hidden_ref,
    cot_ref,
    gain_ref,
    w_ref,
    send_ref,
    hidden_grad_ref,
    branch_ref,
    gain_grad_ref,
):
    groups = 2
    other = jnp.concatenate([early_ref[...], late_ref[...]], axis=0)
    grad_normed = own_ref[...].astype(wide) + other.astype(wide)
    hidden = hidden_ref[...]
    back, gain_grad = norm_back(grad_normed, hidden, rms_scale(hidden), gain_ref[...].astype(wide)[None])
    gain_grad_ref[...] = gain_grad[None]
    grad_hidden = cot_ref[...].astype(wide) + back
    hidden_grad_ref[...] = grad_hidden
    grad_branch = grad_hidden.astype(narrow)
    branch_ref[...] = grad_branch
    tokens = grad_branch.shape[0]
    local = w_ref.shape[0]
    rows = tokens // groups
    half = rows // 2

    def step(part, carry):
        span = pl.ds(pl.multiple_of(part * rows, rows), rows)
        attended_grad = dot_rows(branch_ref[span, :], w_ref[...])
        for pair in range(local // LANES):
            cols = slice(pair * LANES, (pair + 1) * LANES)
            tiles = swap_pairs(attended_grad[:half, cols], attended_grad[half:, cols])
            for at, tile in enumerate(tiles):
                send_ref[2 * pair + at, part] = tile.astype(narrow)
        return carry

    lax.fori_loop(0, groups, step, 0)


def branch_back(own, early, late, hidden, cotangent, norm_ffn, w_out):
    tokens, width = hidden.shape
    local = w_out.shape[0]
    groups = 2
    return pl.pallas_call(
        branch_back_kernel,
        in_specs=[whole_spec()] * 7,
        out_specs=[whole_spec()] * 4,
        out_shape=[
            jax.ShapeDtypeStruct((local // HEAD_DIM, groups, tokens // groups // 2, LANES), narrow),
            jax.ShapeDtypeStruct((tokens, width), wide),
            jax.ShapeDtypeStruct((tokens, width), narrow),
            jax.ShapeDtypeStruct((1, width), wide),
        ],
        compiler_params=pltpu.CompilerParams(vmem_limit_bytes=vmem_bytes),
        cost_estimate=busy(6),
        name="branch_back",
    )(own, early, late, hidden, cotangent, norm_ffn, w_out)


def fold_kernel(
    part_ref, depth_ref, mine_ref, arrived_ref, dq_ref, turn_ref, send_ref, rows_ref, packed_ref
):
    count, rows, _ = mine_ref.shape
    half = rows // 2
    low = lane_ids((rows, LANES)) < HEAD_DIM
    for at, table in enumerate(turn_rows(turn_ref, part_ref[0] * rows, rows)):
        rows_ref[at] = table
        packed_ref[at] = jnp.where(low[:half], table[:half], table[half:])

    def step(slot, carry):
        depth = turn_depth(turn_ref, depth_ref[slot])
        cosine, sine = turn((rows_ref[0], rows_ref[1]), depth)
        pair = mine_ref[slot] + arrived_ref[slot].astype(wide)
        key = spin(pair, cosine, -sine)
        send_ref[slot, :rows, :] = jnp.where(low, key, pair).astype(narrow)
        cosine, sine = turn((packed_ref[0], packed_ref[1]), depth)
        send_ref[slot, rows:, :] = spin(dq_ref[slot].astype(wide), cosine, -sine).astype(narrow)
        return carry

    lax.fori_loop(0, count, step, 0, unroll=4)


def fold(part, depth_pos, mine, arrived, grad_q, turns):
    count, rows, _ = mine.shape
    return pl.pallas_call(
        fold_kernel,
        in_specs=[scalar_spec()] * 2 + [whole_spec()] * 4,
        out_specs=whole_spec(),
        out_shape=jax.ShapeDtypeStruct((count, rows + rows // 2, LANES), narrow),
        scratch_shapes=[
            pltpu.VMEM((2, rows, LANES), wide),
            pltpu.VMEM((2, rows // 2, LANES), wide),
        ],
        compiler_params=pltpu.CompilerParams(vmem_limit_bytes=vmem_bytes),
        cost_estimate=busy(6),
        name="fold",
    )(part, depth_pos, mine, arrived, grad_q, turns)


def unproject_kernel(recv_ref, wq_ref, wk_ref, wv_ref, first_ref, part_ref):
    groups = 2
    rows = recv_ref.shape[1] * 2 // 3
    heads = recv_ref.shape[0] // groups
    for part in range(groups):
        span = slice(part * rows, (part + 1) * rows)
        keys, values, queries = [], [], []
        for pair in range(heads // 2):
            cols = slice(pair * LANES, (pair + 1) * LANES)
            left = recv_ref[2 * pair * groups + part].astype(wide)
            right = recv_ref[(2 * pair + 1) * groups + part].astype(wide)
            key, value = swap_pairs(left[:rows], right[:rows])
            query = jnp.concatenate(swap_pairs(left[rows:], right[rows:]), axis=0)
            value = 0.5 * value
            first_ref[span, cols] = value
            keys.append(key.astype(narrow))
            values.append(value.astype(narrow))
            queries.append(query.astype(narrow))
        total = dot_rows(jnp.concatenate(queries, axis=1), wq_ref[...])
        total = total + dot_rows(jnp.concatenate(keys, axis=1), wk_ref[...])
        total = total + dot_rows(jnp.concatenate(values, axis=1), wv_ref[...])
        part_ref[span, :] = total.astype(narrow)


def unproject(recv, w_query, w_key, w_value):
    width, local = w_query.shape
    tokens = recv.shape[1] * 4 // 3
    return pl.pallas_call(
        unproject_kernel,
        in_specs=[whole_spec()] * 4,
        out_specs=[whole_spec()] * 2,
        out_shape=[
            jax.ShapeDtypeStruct((tokens, local), wide),
            jax.ShapeDtypeStruct((tokens, width), narrow),
        ],
        compiler_params=pltpu.CompilerParams(vmem_limit_bytes=vmem_bytes),
        cost_estimate=busy(60),
        name="unproject",
    )(recv, w_query, w_key, w_value)


def finish_kernel(
    place_ref, near_ref, far_ref, near_core_ref, far_core_ref, query_ref, key_ref, value_ref, out_ref
):
    length, size, width = near_ref.shape
    chips = 2 * length
    head_rows = 3 * HEAD_DIM // 2
    out_rows = size - head_rows
    place = place_ref[0]
    core = place % 2
    high = (place // 2) % 2

    def emit(first, second):
        for chip in range(chips):
            for at, refs in ((chip, first), (chips + chip, second)):
                rows = refs[chip % 2][chip // 2, head_rows:, :]
                out_ref[at * out_rows : (at + 1) * out_rows, :] = rows.astype(wide)

        def column(block, carry):
            cols = pl.ds(pl.multiple_of(block * LANES, LANES), LANES)
            for pair in range(chips // 2):
                pieces = [
                    jnp.concatenate(
                        [refs[chip % 2][chip // 2, :head_rows, cols] for refs in (first, second)],
                        axis=0,
                    ).astype(wide)
                    for chip in (2 * pair, 2 * pair + 1)
                ]
                for at, target in enumerate((key_ref, value_ref, query_ref)):
                    span = slice(at * HEAD_DIM, (at + 1) * HEAD_DIM)
                    both = jnp.concatenate([piece[span] for piece in pieces], axis=0)
                    target[cols, pair * LANES : (pair + 1) * LANES] = jnp.transpose(both)
            return carry

        lax.fori_loop(0, width // LANES, column, 0)

    for core_at in range(2):
        for high_at in range(2):

            @pl.when((core == core_at) & (high == high_at))
            def _(core_at=core_at, high_at=high_at):
                own = (near_ref, far_ref) if high_at == 0 else (far_ref, near_ref)
                other = (near_core_ref, far_core_ref) if high_at == 0 else (far_core_ref, near_core_ref)
                emit(own, other) if core_at == 0 else emit(other, own)


def finish(place, near, far, near_core, far_core, local):
    width = near.shape[2]
    return pl.pallas_call(
        finish_kernel,
        in_specs=[scalar_spec()] + [whole_spec()] * 4,
        out_specs=[whole_spec()] * 4,
        out_shape=[jax.ShapeDtypeStruct((width, local), wide)] * 3
        + [jax.ShapeDtypeStruct((local, width), wide)],
        compiler_params=pltpu.CompilerParams(vmem_limit_bytes=vmem_bytes),
        cost_estimate=busy(6),
        name="finish",
    )(place, near, far, near_core, far_core)


def swap_tensor(values):
    return lax.ppermute(values, "tensor", [(0, 1), (1, 0)])


def swap_bit(values, bit, count):
    return lax.ppermute(values, "dp", [(i, i ^ bit) for i in range(count)])


def add_narrow(left, right):
    return (left.astype(wide) + right.astype(wide)).astype(narrow)


def take_part(values, index, parts):
    size = values.shape[0] // parts
    return lax.dynamic_slice_in_dim(values, index * size, size, 0)


def reduce_bit(values, bit, place, count):
    mine = (place // bit) % 2
    arrived = swap_bit(take_part(values, 1 - mine, 2), bit, count)
    return add_narrow(take_part(values, mine, 2), arrived)


def side_groups(count):
    return [[chip * 2 + core for chip in range(count // 2)] for core in range(2)]


def to_chips(values, count):
    return lax.all_to_all(
        values, "dp", split_axis=0, concat_axis=0, tiled=True, axis_index_groups=side_groups(count)
    )


def spread(values, count):
    chips = count // 2
    return to_chips(jnp.broadcast_to(values[None], (chips,) + values.shape), count)


def spread_line(copies, count):
    length = count // 4
    return lax.all_to_all(
        copies,
        "dp",
        split_axis=0,
        concat_axis=0,
        tiled=True,
        axis_index_groups=[[z * 4 + rest for z in range(length)] for rest in range(4)],
    )


def gather_core(values, axis, place, count):
    mine = place % 2
    arrived = swap_bit(values, 1, count)
    row = jnp.concatenate([arrived, values, arrived], axis=axis)
    size = values.shape[axis]
    return lax.dynamic_slice_in_dim(row, (1 - mine) * size, 2 * size, axis)


def sum_over_dp(values, place, count):
    chips = count // 2
    values = reduce_bit(values, 1, place, count)
    shares = to_chips(values.reshape((chips, values.shape[0] // chips) + values.shape[1:]), count)
    total = jnp.sum(shares.astype(wide), axis=0).astype(narrow)
    whole = spread(total, count)
    whole = whole.reshape((-1,) + whole.shape[2:])
    return gather_core(whole, 0, place, count)


def reduce_z(values, place, count):
    at = place // 4
    total = take_part(values, at, 4).astype(wide)
    for step in (1, 2, 3):
        share = take_part(values, at ^ step, 4)
        total = total + swap_bit(share, 4 * step, count).astype(wide)
    return total.astype(narrow)


def gather_z(values, place, count):
    at = place // 4
    shares = [values] + [swap_bit(values, 4 * step, count) for step in (1, 2, 3)]
    row = jnp.concatenate(shares, axis=0)
    return jnp.concatenate([take_part(row, at ^ target, 4) for target in range(4)], axis=0)


def gather_bit(values, bit, place, count):
    mine = (place // bit) % 2
    arrived = swap_bit(values, bit, count)
    row = jnp.concatenate([arrived, values, arrived], axis=0)
    size = values.shape[0]
    return lax.dynamic_slice_in_dim(row, (1 - mine) * size, 2 * size, 0)


def after(value, *others):
    return lax.optimization_barrier((value,) + others)[0]


def sum_small(values, count):
    bit = 1
    while bit < count:
        values = values + swap_bit(values, bit, count)
        bit *= 2
    return values


def body_heads(
    inputs,
    first_values,
    w_query,
    w_key,
    w_value,
    w_out,
    w_gate,
    w_up,
    w_down,
    norm_attn,
    norm_ffn,
    cotangent,
    parents,
    depth_pos,
    assignment,
):
    count = parents.shape[0]
    tokens, width = inputs.shape
    local = w_query.shape[1]
    heads = local // HEAD_DIM
    groups = count // heads
    place = lax.axis_index("dp")
    part = (place % groups).astype(jnp.int32)
    part_array = part.reshape(1)

    rows = tokens // groups
    w_out_other = swap_tensor(w_out)
    turns = jnp.asarray(turn_constants())
    place_array = place.astype(jnp.int32).reshape(1)

    send, normed = project(
        place_array,
        depth_pos,
        inputs,
        norm_attn,
        first_values,
        turns,
        w_query,
        w_key,
        w_value,
        groups,
    )
    send = send.reshape(count, rows + rows // 2, LANES)
    recv = lax.all_to_all(send, "dp", split_axis=0, concat_axis=0, tiled=True)
    normed_theirs = swap_bit(take_part(normed, 1 - part, groups), 1, count)
    normed_mine = take_part(normed, part, groups)
    normed_row = jnp.concatenate([normed_theirs, normed_mine, normed_theirs], axis=0)
    normed_chip = lax.dynamic_slice_in_dim(normed_row, (1 - part) * rows, groups * rows, 0)
    side = lax.axis_index("tensor")
    quarter = rows // 2
    normed_quarter = lax.dynamic_index_in_dim(
        normed_chip.reshape(groups, 2, quarter, width), side, 1, keepdims=False
    ).reshape(groups * quarter, width)
    recv, normed_quarter = lax.optimization_barrier((recv, normed_quarter))
    normed_own = lax.all_gather(
        normed_quarter, "dp", axis=0, tiled=True, axis_index_groups=side_groups(count)
    )

    other = swap_bit(recv, 1, count)
    packed, ot, logs = attend(parents, assignment, part_array, recv, other)
    own_out = lax.all_to_all(packed, "dp", split_axis=0, concat_axis=0, tiled=True)
    other_out = swap_tensor(own_out)
    attended, hidden, normed_ffn = merge(own_out, other_out, w_out, w_out_other, inputs, norm_ffn)

    gate_proj = jnp.dot(normed_ffn, w_gate, preferred_element_type=wide)
    up_proj = jnp.dot(normed_ffn, w_up, preferred_element_type=wide)
    silu_gate = jax.nn.silu(gate_proj)
    activated = (silu_gate * up_proj).astype(narrow)
    grad_activated = jnp.einsum("td,fd->tf", cotangent, w_down, preferred_element_type=wide)
    sigmoid_gate = jax.nn.sigmoid(gate_proj)
    grad_gate = (
        grad_activated * up_proj * sigmoid_gate * (1.0 + gate_proj * (1.0 - sigmoid_gate))
    ).astype(narrow)
    grad_up = (grad_activated * silu_gate).astype(narrow)
    ffn_partial = (
        jnp.einsum("tf,df->td", grad_gate, w_gate, preferred_element_type=wide)
        + jnp.einsum("tf,df->td", grad_up, w_up, preferred_element_type=wide)
    ).astype(narrow)
    ffn_early = swap_tensor(ffn_partial[: tokens // 2])
    ffn_grads = tuple(
        jnp.einsum(form, left, right, preferred_element_type=wide).astype(narrow)
        for form, left, right in (
            ("td,tf->df", normed_ffn, grad_gate),
            ("td,tf->df", normed_ffn, grad_up),
            ("tf,td->fd", activated, cotangent),
        )
    )
    feed_partial = jnp.dot(activated, w_down, preferred_element_type=wide).astype(narrow)

    normed_own, *ffn_grads = lax.optimization_barrier((normed_own,) + ffn_grads)
    ffn_sums = lax.psum(tuple(ffn_grads), "dp")
    ffn_early = after(ffn_early, *ffn_grads)

    def way_back(ffn_early, normed_own):
        ffn_late = swap_tensor(ffn_partial[tokens // 2 :])
        grad_send, grad_hidden, grad_branch, grad_gain_ffn = branch_back(
            ffn_partial, ffn_early, ffn_late, hidden, cotangent, norm_ffn, w_out
        )
        grad_recv = lax.all_to_all(
            grad_send.reshape(count, rows // 2, LANES), "dp", split_axis=0, concat_axis=0, tiled=True
        )
        grad_w_out = jnp.einsum("tc,td->cd", attended, grad_branch, preferred_element_type=wide)
        out_half = reduce_bit(grad_w_out.astype(narrow), 1, place, count)
        grad_recv, out_half = lax.optimization_barrier((grad_recv, out_half))
        chips = count // 2
        out_shares = to_chips(out_half.reshape(chips, local // count, width), count)
        normed_other = swap_tensor(normed_own)
        feed_other = swap_tensor(after(feed_partial, normed_other))

        grad_q, mine, theirs = attend_back(
            parents, assignment, part_array, recv, other, grad_recv, ot, logs
        )
        grad_q, mine, theirs, out_shares = lax.optimization_barrier(
            (grad_q, mine, theirs, out_shares)
        )
        arrived = swap_bit(theirs, 1, count)
        back_send = fold(part_array, depth_pos, mine, arrived, grad_q, turns)
        back_recv = lax.all_to_all(back_send, "dp", split_axis=0, concat_axis=0, tiled=True)
        pairs_terms = query_terms = 0.0
        for at, normed_part in ((side, normed_own), (1 - side, normed_other)):
            pairs = lax.dynamic_slice_in_dim(back_send, at * quarter, quarter, 1)
            both = jnp.concatenate([pairs, back_send[:, rows:]], axis=2)
            terms = jnp.einsum(
                "tc,td->cd",
                both.reshape(count * quarter, 2 * LANES),
                normed_part,
                preferred_element_type=wide,
            )
            pairs_terms = pairs_terms + terms[:LANES]
            query_terms = query_terms + lax.dynamic_slice_in_dim(
                terms, LANES + at * HEAD_DIM, HEAD_DIM, 0
            )
        head_grads = jnp.concatenate(
            [pairs_terms[:HEAD_DIM], 0.5 * pairs_terms[HEAD_DIM:], query_terms], axis=0
        ).astype(narrow)
        head_share = reduce_bit(head_grads, 1, place, count)
        out_share = jnp.sum(out_shares.astype(wide), axis=0).astype(narrow)
        share = jnp.concatenate([head_share, out_share], axis=0)
        copies = jnp.broadcast_to(share[None], (count // 4,) + share.shape)
        back_recv, feed_other, copies = lax.optimization_barrier((back_recv, feed_other, copies))
        grad_first, attn_partial = unproject(back_recv, w_query, w_key, w_value)
        attn_other = swap_tensor(attn_partial)
        along = spread_line(copies, count)
        near = after(along, attn_partial)
        far = swap_bit(near, 2, count)
        near_core = swap_bit(near, 1, count)
        output = (hidden + (feed_partial.astype(wide) + feed_other.astype(wide))).astype(narrow)
        inputs_wide = inputs.astype(wide)
        grad_normed = attn_partial.astype(wide) + attn_other.astype(wide)
        grad_input_norm, grad_gain_attn = norm_back(
            grad_normed, inputs_wide, rms_scale(inputs_wide), norm_attn.astype(wide)
        )
        grad_inputs = grad_hidden + grad_input_norm
        gains = sum_small(jnp.stack([grad_gain_attn, grad_gain_ffn[0]]), count)
        far_core = swap_bit(after(far, gains, grad_inputs, output), 1, count)
        return output, grad_inputs, grad_first, gains, near, far, near_core, far_core

    def no_tree(*operands):
        shapes = jax.eval_shape(way_back, *operands)
        return tuple(jnp.zeros(leaf.shape, leaf.dtype) for leaf in shapes)

    output, grad_inputs, grad_first, gains, near, far, near_core, far_core = lax.cond(
        parents[0] < 0, way_back, no_tree, ffn_early, normed_own
    )
    head_query, head_key, head_value, sum_w_out = finish(
        place_array, near, far, near_core, far_core, local
    )
    sums = [after(term, sum_w_out).astype(wide) for term in ffn_sums]
    return (
        output,
        grad_inputs,
        grad_first,
        head_query,
        head_key,
        head_value,
        sum_w_out,
        sums[0],
        sums[1],
        sums[2],
        gains[0],
        gains[1],
    )


def pick_body(mesh):
    if mesh.shape["dp"] == 16 and mesh.shape["tensor"] == 2:
        return body_heads
    return body_general


def solution(mesh):
    placed = (
        P("dp", None),
        P("dp", "tensor"),
        P(None, "tensor"),
        P(None, "tensor"),
        P(None, "tensor"),
        P("tensor", None),
        P(None, "tensor"),
        P(None, "tensor"),
        P("tensor", None),
        P(),
        P(),
        P("dp", None),
        P(),
        P(),
        P(),
    )
    return jax.shard_map(
        pick_body(mesh),
        mesh=mesh,
        in_specs=placed,
        out_specs=(
            P("dp", None),
            P("dp", None),
            P("dp", "tensor"),
            P(None, "tensor"),
            P(None, "tensor"),
            P(None, "tensor"),
            P("tensor", None),
            P(None, "tensor"),
            P(None, "tensor"),
            P("tensor", None),
            P(),
            P(),
        ),
        check_vma=False,
    )
```
